256 devices in a mesh: row: 32 (over z, y), col: 8 (over x, core).
Axes of the slice: x: 4, y: 4, z: 8, core: 2. Of those that a mesh axis runs over, the one named last changes fastest.
Arguments:
- positions: float32 [16, 3, 131072], P(None, None, 'row'), may hold values from -4 to 4
- vectors: float32 [8, 131072], P(None, 'row'), may hold values from -6 to 6
- pairs: int32 [32, 8, 10, 2], P('row', 'col'), may hold values from 0 to 31, as said below
- valid: int32 [32, 8, 10], P('row', 'col'), may hold values from 0 to 1, as said below
Outputs:
- leading: float32 [8, 131072], P(None, 'row')
The draws below stay inside these ranges and needn't reach their ends.
Inputs may be any that keep to these rules, and one draw needn't show every extreme that they name: Live slots of a cell come first and name distinct tile pairs with I <= J; no unordered pair of tiles is listed twice in the whole list; padding slots hold 0 0. a < 8, b < 32. `valid`: at most 10 live slots a cell, and some cell has all 10 live.
All inputs are finite; a program needn't handle non-finite values.
Results may differ from the reference program's by a relative error of at most 0.0003.
Values sent between devices are 32-bit elements; how exact they have to be, the bound alone decides.
No kernel may reach another device: no remote copies, remote signals or barrier semaphores. Data moves between devices by JAX's collectives and lax.ppermute only.
A program may use at most 128 MiB of HBM per device.

```python
import jax
import jax.numpy as jnp
from jax import lax

SNAP = 16
TILE = 512
VEC = 8
MAXP = 10
GRID_ROWS = 32
GRID_COLS = 8
TRAJ = 131072
ROW_TILES = 8
SUB_TILES = 1
COL_TILES = 32


def draw_positions(key, part):
    base = jax.random.fold_in(key, 31)
    values = jax.random.uniform(base, (SNAP, 3, TRAJ), jnp.float32, -4.0, 4.0)
    return values.astype(jnp.float32)


def near_pairs(key):
    base = jax.random.fold_in(key, 77)
    key_score, key_count, key_full = jax.random.split(base, 3)
    cells = GRID_ROWS * GRID_COLS
    candidates = ROW_TILES * COL_TILES
    cell_ids = jnp.arange(cells, dtype=jnp.int32)
    grid_row = cell_ids // GRID_COLS
    grid_col = cell_ids % GRID_COLS
    codes = jnp.arange(candidates, dtype=jnp.int32)
    local_row = codes // COL_TILES
    local_col = codes % COL_TILES
    row_tile = grid_row[:, None] * ROW_TILES + local_row[None, :]
    col_tile = (local_col // SUB_TILES)[None, :] * ROW_TILES + grid_col[:, None] * SUB_TILES + (local_col % SUB_TILES)[None, :]
    allowed = row_tile <= col_tile
    full_cell = jax.random.randint(key_full, (), 0, max(cells // 2, 1))
    spread = max((1 << 29) // candidates, 2)
    score = jax.random.randint(key_score, (cells, candidates), 0, spread) * candidates + codes[None, :]
    score = score + jnp.where(allowed, 0, 1 << 30)
    forced = (cell_ids == full_cell)[:, None] & (codes == COL_TILES - 1)[None, :]
    score = jnp.where(forced, -1, score)
    order = jnp.argsort(score, axis=1, stable=True)[:, :MAXP].astype(jnp.int32)
    available = jnp.sum(allowed.astype(jnp.int32), axis=1)
    count = jax.random.randint(key_count, (cells,), max(3 * MAXP // 4, 1), MAXP + 1)
    count = jnp.where(cell_ids == full_cell, MAXP, count)
    count = jnp.minimum(count, available)
    live = jnp.arange(MAXP, dtype=jnp.int32)[None, :] < count[:, None]
    first_part = jnp.where(live, order // COL_TILES, 0)
    second_part = jnp.where(live, order % COL_TILES, 0)
    listed = jnp.stack([first_part, second_part], axis=-1).reshape(GRID_ROWS, GRID_COLS, MAXP, 2)
    return (listed.astype(jnp.int32), live.astype(jnp.int32).reshape(GRID_ROWS, GRID_COLS, MAXP))


def draw_pairs(key, part):
    return near_pairs(key)[0]


def draw_valid(key, part):
    return near_pairs(key)[1]


def levels(stream_key, extent, shards, least, top_value):
    gain, own = 1.0, jax.random.fold_in(stream_key, 6)
    for axis_at, shards_of in shards:
        steps = jnp.exp(jax.random.uniform(jax.random.fold_in(own, axis_at), (shards_of,), jnp.float32, least / len(shards), top_value / len(shards)))
        gain = gain * jnp.repeat(steps, extent[axis_at] // shards_of).reshape([-1 if axis == axis_at else 1 for axis in range(len(extent))])
    return gain


def normal_values(own_key, dims, scale, reach, cuts=(), kind=jnp.bfloat16):
    values = scale * jax.random.normal(own_key, dims, jnp.float32)
    if cuts:
        values = values * levels(own_key, dims, cuts, -0.22, 0.18)
    return jnp.clip(values, -reach, reach).astype(kind)


def setup_inputs(seed: int = 0) -> dict:
    key_list = jax.random.split(jax.random.key(seed), 5)
    return {
        "positions": draw_positions(jax.random.fold_in(key_list[4], 71), 0),
        "vectors": normal_values(key_list[1], (VEC, TRAJ), 1.0, 6.0, ((1, 32),), jnp.float32),
        "pairs": draw_pairs(jax.random.fold_in(key_list[4], 71), 0),
        "valid": draw_valid(jax.random.fold_in(key_list[4], 71), 0),
    }


def form_tile(row_part, col_part):
    total = jnp.zeros((row_part.shape[2], col_part.shape[2]), jnp.float32)
    for snapshot in range(row_part.shape[0]):
        distance = jnp.zeros_like(total)
        for component in range(3):
            spacing = row_part[snapshot, component][:, None] - col_part[snapshot, component][None, :]
            distance = distance + spacing * spacing
        total = total + jnp.exp(-0.5 * distance)
    return total

def reference(positions, vectors, pairs, valid):
    count = GRID_ROWS * GRID_COLS * MAXP
    slot_ids = jnp.arange(count, dtype=jnp.int32)
    grid_row = (slot_ids // (GRID_COLS * MAXP)).astype(jnp.int32)
    grid_col = (slot_ids // MAXP % GRID_COLS).astype(jnp.int32)
    flat_pairs = pairs.reshape(count, 2).astype(jnp.int32)
    weights = valid.reshape(count).astype(jnp.float32)

    def apply_all(field):

        def visit(total, slot):
            local_row, local_col, weight, rr, cc = slot
            row_tile = (rr * ROW_TILES + local_row).astype(jnp.int32)
            col_tile = (local_col // SUB_TILES * ROW_TILES + cc * SUB_TILES + local_col % SUB_TILES).astype(jnp.int32)
            row_start = (row_tile * TILE).astype(jnp.int32)
            col_start = (col_tile * TILE).astype(jnp.int32)
            kernel = form_tile(lax.dynamic_slice_in_dim(positions, row_start, TILE, 2), lax.dynamic_slice_in_dim(positions, col_start, TILE, 2)) * weight
            row_vec = lax.dynamic_slice_in_dim(field, row_start, TILE, 1)
            col_vec = lax.dynamic_slice_in_dim(field, col_start, TILE, 1)
            to_rows = jnp.einsum('kj,ij->ki', col_vec, kernel, precision=lax.Precision.HIGHEST)
            cross = jnp.where(row_tile != col_tile, 1.0, 0.0).astype(jnp.float32)
            to_cols = jnp.einsum('ki,ij->kj', row_vec, kernel, precision=lax.Precision.HIGHEST) * cross
            total = lax.dynamic_update_slice_in_dim(total, lax.dynamic_slice_in_dim(total, row_start, TILE, 1) + to_rows, row_start, 1)
            total = lax.dynamic_update_slice_in_dim(total, lax.dynamic_slice_in_dim(total, col_start, TILE, 1) + to_cols, col_start, 1)
            return (total, None)
        start = jnp.zeros((VEC, TRAJ), jnp.float32)
        result, _ = lax.scan(visit, start, (flat_pairs[:, 0], flat_pairs[:, 1], weights, grid_row, grid_col))
        return result
    first = apply_all(vectors)
    second = apply_all(first)
    total = lax.optimization_barrier(jnp.mean(second * second, axis=1))
    return second / jnp.sqrt(total + 1e-06)[:, None]
```

```python
import functools
import math

import jax
import jax.numpy as jnp
from jax import lax
from jax.experimental import pallas as pl
from jax.experimental.pallas import tpu as pltpu
from jax.sharding import Mesh
from jax.sharding import PartitionSpec as P

TILE = 512
ROW = ("z", "y")
COL = ("x", "core")
LOG2E = math.log2(math.e)
GROUPS = 6
DEPTH = 8 * GROUPS
CHUNK = 128
HALF = 256


def split3(value):
    high = value.astype(jnp.bfloat16).astype(jnp.float32)
    rest = value - high
    mid = rest.astype(jnp.bfloat16).astype(jnp.float32)
    return high, mid, rest - mid


def rows_of(ref, snapshot, scale, norm_at, one_at):
    width = ref.shape[-1]
    place = lax.broadcasted_iota(jnp.int32, (8, width), 0)
    parts = [
        jnp.broadcast_to(ref[3 * snapshot + q : 3 * snapshot + q + 1, :], (8, width))
        for q in range(3)
    ]
    norm = (-0.5 * LOG2E) * (parts[0] * parts[0] + parts[1] * parts[1] + parts[2] * parts[2])
    out = jnp.where(place == norm_at, norm, jnp.where(place == one_at, 1.0, 0.0))
    for q in range(3):
        out = jnp.where(place == q, parts[q] * scale if scale != 1.0 else parts[q], out)
    return out


def prepare_kernel(pos_ref, out_ref):
    for snapshot in range(16):
        high, mid, low = split3(rows_of(pos_ref, snapshot, LOG2E, 4, 3))
        stacked = jnp.concatenate([high, high, mid, mid, high, low], axis=0)
        out_ref[0, snapshot] = stacked.T.astype(jnp.bfloat16)


def prepare_rows(pos):
    tiles = pos.shape[1] // TILE
    return pl.pallas_call(
        prepare_kernel,
        grid=(tiles,),
        in_specs=[pl.BlockSpec((48, TILE), lambda i: (0, i))],
        out_specs=pl.BlockSpec((1, 16, TILE, DEPTH), lambda i: (i, 0, 0, 0)),
        out_shape=jax.ShapeDtypeStruct((tiles, 16, TILE, DEPTH), jnp.bfloat16),
        compiler_params=pltpu.CompilerParams(vmem_limit_bytes=32 << 20),
        cost_estimate=pl.CostEstimate(flops=10**8, bytes_accessed=20 << 20, transcendentals=0),
        name="prepare_rows",
    )(pos)


def multiply(field, high, low, dims):
    terms = jnp.concatenate(split3(field), axis=0).astype(jnp.bfloat16)
    dot = functools.partial(
        lax.dot_general, dimension_numbers=dims, preferred_element_type=jnp.float32
    )
    by_high = dot(terms, high)
    by_low = dot(terms[:16], low)
    return (by_high[0:8] + by_low[0:8]) + (by_high[8:16] + by_low[8:16]) + by_high[16:24]


def add_products(high, low, row_field, col_field, row_at, col_at, crossing, row_acc, col_acc):
    row_acc[row_at] += multiply(col_field, high, low, (((1,), (1,)), ((), ())))

    @pl.when(crossing)
    def _():
        col_acc[col_at] += multiply(row_field, high, low, (((1,), (0,)), ((), ())))


def clear(row_acc, col_acc):
    @pl.when(pl.program_id(0) == 0)
    def _():
        row_acc[...] = jnp.zeros_like(row_acc)
        col_acc[...] = jnp.zeros_like(col_acc)


def form_kernel(
    table, prepared_ref, col_ref, row_vec, high_ref, low_ref, row_acc, col_acc, cols
):
    clear(row_acc, col_acc)
    slot = pl.program_id(0)

    @pl.when(table[2, slot] != 0)
    def _():
        pos = col_ref.at[0]
        for snapshot in range(16):
            high, mid, low = split3(rows_of(pos, snapshot, 1.0, 3, 4))
            stacked = jnp.concatenate([high, mid, high, mid, low, high], axis=0)
            cols[snapshot] = stacked.astype(jnp.bfloat16)

        def step(at, carry):
            start = pl.multiple_of(at * CHUNK, CHUNK)
            for half in range(TILE // HALF):
                total = None
                for snapshot in range(16):
                    exponent = jnp.dot(
                        prepared_ref[0, snapshot, pl.ds(start, CHUNK), :],
                        cols[snapshot, :, half * HALF : (half + 1) * HALF],
                        preferred_element_type=jnp.float32,
                    )
                    term = jnp.exp2(exponent)
                    total = term if total is None else total + term
                high = total.astype(jnp.bfloat16)
                low = (total - high.astype(jnp.float32)).astype(jnp.bfloat16)
                place = (0, pl.ds(start, CHUNK), pl.ds(half * HALF, HALF))
                high_ref[place] = high
                low_ref[place] = low
            return carry

        lax.fori_loop(0, TILE // CHUNK, step, 0)
        row_at = table[0, slot]
        add_products(
            high_ref[0],
            low_ref[0],
            row_vec[row_at],
            col_ref[0, 48:56, :],
            row_at,
            table[1, slot],
            table[3, slot] != 0,
            row_acc,
            col_acc,
        )


def form_and_apply(table, prepared, gathered, row_vec):
    slots = table.shape[1]
    blocks = gathered.shape[0]
    tiles = row_vec.shape[0]
    whole = pl.BlockSpec((tiles, 8, TILE), lambda s, t: (0, 0, 0))
    grid_spec = pltpu.PrefetchScalarGridSpec(
        num_scalar_prefetch=1,
        grid=(slots,),
        in_specs=[
            pl.BlockSpec((1, 16, TILE, DEPTH), lambda s, t: (t[0, s], 0, 0, 0)),
            pl.BlockSpec((1, 56, TILE), lambda s, t: (t[1, s], 0, 0)),
            whole,
        ],
        out_specs=[
            pl.BlockSpec((1, TILE, TILE), lambda s, t: (s, 0, 0)),
            pl.BlockSpec((1, TILE, TILE), lambda s, t: (s, 0, 0)),
            whole,
            pl.BlockSpec((blocks, 8, TILE), lambda s, t: (0, 0, 0)),
        ],
        scratch_shapes=[pltpu.VMEM((16, DEPTH, TILE), jnp.bfloat16)],
    )
    return pl.pallas_call(
        form_kernel,
        grid_spec=grid_spec,
        out_shape=[
            jax.ShapeDtypeStruct((slots, TILE, TILE), jnp.bfloat16),
            jax.ShapeDtypeStruct((slots, TILE, TILE), jnp.bfloat16),
            jax.ShapeDtypeStruct((tiles, 8, TILE), jnp.float32),
            jax.ShapeDtypeStruct((blocks, 8, TILE), jnp.float32),
        ],
        compiler_params=pltpu.CompilerParams(vmem_limit_bytes=40 << 20),
        name="form_and_apply",
    )(table, prepared, gathered, row_vec)


def apply_kernel(table, high_ref, low_ref, row_vec, col_vec, row_acc, col_acc):
    clear(row_acc, col_acc)
    slot = pl.program_id(0)

    @pl.when(table[2, slot] != 0)
    def _():
        row_at = table[0, slot]
        col_at = table[1, slot]
        add_products(
            high_ref[0],
            low_ref[0],
            row_vec[row_at],
            col_vec[col_at],
            row_at,
            col_at,
            table[3, slot] != 0,
            row_acc,
            col_acc,
        )


def apply_again(table, high, low, row_vec, col_vec):
    slots = table.shape[1]
    blocks = col_vec.shape[0]
    tiles = row_vec.shape[0]
    rows = pl.BlockSpec((tiles, 8, TILE), lambda s, t: (0, 0, 0))
    cols = pl.BlockSpec((blocks, 8, TILE), lambda s, t: (0, 0, 0))
    matrix = pl.BlockSpec((1, TILE, TILE), lambda s, t: (s, 0, 0))
    grid_spec = pltpu.PrefetchScalarGridSpec(
        num_scalar_prefetch=1,
        grid=(slots,),
        in_specs=[matrix, matrix, rows, cols],
        out_specs=[rows, cols],
    )
    return pl.pallas_call(
        apply_kernel,
        grid_spec=grid_spec,
        out_shape=[
            jax.ShapeDtypeStruct((tiles, 8, TILE), jnp.float32),
            jax.ShapeDtypeStruct((blocks, 8, TILE), jnp.float32),
        ],
        compiler_params=pltpu.CompilerParams(vmem_limit_bytes=40 << 20),
        name="apply_again",
    )(table, high, low, row_vec, col_vec)


def spread(piece, axes):
    copies = jnp.broadcast_to(piece, (lax.axis_size(axes),) + piece.shape)
    return lax.all_to_all(copies, axes, 0, 0, tiled=True)


def gather_sets(piece):
    return lax.all_gather(lax.all_gather(piece, "y"), "z")


def combine(row_acc, col_acc):
    by_row = lax.all_to_all(row_acc, COL, 0, 0, tiled=True)
    by_col = lax.all_to_all(col_acc, ROW, 0, 0, tiled=True)
    return jnp.sum(by_row, axis=0) + jnp.sum(by_col, axis=0)


def per_device(positions, vectors, pairs, valid):
    grid_row = lax.axis_index(ROW)
    grid_col = lax.axis_index(COL)
    block = positions.shape[2]
    tiles = block // TILE
    blocks = lax.axis_size(ROW)
    local_rows = pairs[0, 0, :, 0]
    local_cols = pairs[0, 0, :, 1]
    crossing = (grid_row * tiles + local_rows) != (local_cols * tiles + grid_col)
    table = jnp.stack(
        [local_rows, local_cols, valid[0, 0], crossing.astype(jnp.int32)], axis=0
    ).astype(jnp.int32)

    flat = positions.reshape(48, block)
    own = lax.dynamic_slice_in_dim(
        jnp.concatenate([flat, vectors], axis=0), grid_col * TILE, TILE, 1
    )
    gathered = gather_sets(own).reshape(blocks, 56, TILE)
    prepared = prepare_rows(flat)
    row_vec = vectors.reshape(8, tiles, TILE).transpose(1, 0, 2)

    high, low, row_acc, col_acc = form_and_apply(table, prepared, gathered, row_vec)
    first = combine(row_acc, col_acc)
    second = combine(*apply_again(table, high, low, spread(first, COL), spread(first, ROW)))

    rows = spread(second, COL)
    squares = jnp.sum(rows * rows, axis=(0, 2))
    squares = spread(jnp.broadcast_to(squares[:, None], (8, 128)), ROW)
    total = jnp.sum(squares[:, :, 0], axis=0) / (block * blocks)
    scaled = rows / jnp.sqrt(total + 1e-06)[None, :, None]
    return scaled.transpose(1, 0, 2).reshape(8, block)


def solution(mesh):
    physical = Mesh(mesh.devices.reshape(8, 4, 4, 2), ("z", "y", "x", "core"))
    placed = (
        P(None, None, ROW),
        P(None, ROW),
        P(ROW, COL, None, None),
        P(ROW, COL, None),
    )
    return jax.shard_map(
        per_device, mesh=physical, in_specs=placed, out_specs=P(None, ROW), check_vma=False
    )
```

```python
import functools
import math

import jax
import jax.numpy as jnp
from jax import lax
from jax.experimental import pallas as pl
from jax.experimental.pallas import tpu as pltpu
from jax.sharding import Mesh
from jax.sharding import PartitionSpec as P

TILE = 512
ROW = ("z", "y")
COL = ("x", "core")
ALL = ROW + COL
ROW_AT, ROW_NEAR, COL_AT, COL_NEAR, LIVE, CROSSING = range(6)
BY_ROWS = (((1,), (0,)), ((), ()))
BY_COLS = (((1,), (1,)), ((), ()))
LOG2E = math.log2(math.e)
GROUPS = 6
DEPTH = 8 * GROUPS
CHUNK = 128
HALF = 256


def in_hbm(value):
    return pltpu.with_memory_space_constraint(value, pltpu.HBM)


def split3(value):
    high = value.astype(jnp.bfloat16).astype(jnp.float32)
    rest = value - high
    mid = rest.astype(jnp.bfloat16).astype(jnp.float32)
    return high, mid, rest - mid


def rows_of(ref, snapshot, scale, norm_at, one_at):
    width = ref.shape[-1]
    place = lax.broadcasted_iota(jnp.int32, (8, width), 0)
    parts = [
        jnp.broadcast_to(ref[16 * q + snapshot : 16 * q + snapshot + 1, :], (8, width))
        for q in range(3)
    ]
    norm = (-0.5 * LOG2E) * (parts[0] * parts[0] + parts[1] * parts[1] + parts[2] * parts[2])
    out = jnp.where(place == norm_at, norm, jnp.where(place == one_at, 1.0, 0.0))
    for q in range(3):
        out = jnp.where(place == q, parts[q] * scale if scale != 1.0 else parts[q], out)
    return out


def prepare_kernel(pos_ref, out_ref):
    for snapshot in range(16):
        high, mid, low = split3(rows_of(pos_ref, snapshot, LOG2E, 4, 3))
        stacked = jnp.concatenate([high, high, mid, mid, high, low], axis=0)
        out_ref[0, snapshot] = stacked.T.astype(jnp.bfloat16)


def prepare_rows(pos):
    tiles = pos.shape[1] // TILE
    return pl.pallas_call(
        prepare_kernel,
        grid=(tiles,),
        in_specs=[pl.BlockSpec((48, TILE), lambda i: (0, i))],
        out_specs=pl.BlockSpec((1, 16, TILE, DEPTH), lambda i: (i, 0, 0, 0)),
        out_shape=pltpu.HBM((tiles, 16, TILE, DEPTH), jnp.bfloat16),
        compiler_params=pltpu.CompilerParams(vmem_limit_bytes=32 << 20),
        cost_estimate=pl.CostEstimate(flops=10**8, bytes_accessed=20 << 20, transcendentals=0),
        name="prepare_rows",
    )(pos)


def multiply(field, high, low, dims):
    terms = jnp.concatenate(split3(field), axis=0).astype(jnp.bfloat16)
    dot = functools.partial(
        lax.dot_general, dimension_numbers=dims, preferred_element_type=jnp.float32
    )
    by_high = dot(terms, high)
    by_low = dot(terms[:16], low)
    return (by_high[0:8] + by_low[0:8]) + (by_high[8:16] + by_low[8:16]) + by_high[16:24]


def clear(acc):
    @pl.when(pl.program_id(0) == 0)
    def _():
        acc[...] = jnp.zeros_like(acc)


def form_kernel(table, prepared_ref, col_ref, row_vec, high_ref, low_ref, col_acc, cols):
    clear(col_acc)
    slot = pl.program_id(0)

    @pl.when(table[LIVE, slot] != 0)
    def _():
        pos = col_ref.at[0]
        for snapshot in range(16):
            high, mid, low = split3(rows_of(pos, snapshot, 1.0, 3, 4))
            stacked = jnp.concatenate([high, mid, high, mid, low, high], axis=0)
            cols[snapshot] = stacked.astype(jnp.bfloat16)

        def step(at, carry):
            start = pl.multiple_of(at * CHUNK, CHUNK)
            for half in range(TILE // HALF):
                total = None
                for snapshot in range(16):
                    exponent = jnp.dot(
                        prepared_ref[0, snapshot, pl.ds(start, CHUNK), :],
                        cols[snapshot, :, half * HALF : (half + 1) * HALF],
                        preferred_element_type=jnp.float32,
                    )
                    term = jnp.exp2(exponent)
                    total = term if total is None else total + term
                high = total.astype(jnp.bfloat16)
                low = (total - high.astype(jnp.float32)).astype(jnp.bfloat16)
                place = (0, pl.ds(start, CHUNK), pl.ds(half * HALF, HALF))
                high_ref[place] = high
                low_ref[place] = low
            return carry

        lax.fori_loop(0, TILE // CHUNK, step, 0)

        @pl.when(table[CROSSING, slot] != 0)
        def _():
            col_acc[table[COL_AT, slot]] += multiply(
                row_vec[table[ROW_AT, slot]], high_ref[0], low_ref[0], BY_ROWS
            )


def form_and_apply(table, prepared, gathered, row_vec):
    slots = table.shape[1]
    blocks = gathered.shape[0]
    tiles = row_vec.shape[0]
    grid_spec = pltpu.PrefetchScalarGridSpec(
        num_scalar_prefetch=1,
        grid=(slots,),
        in_specs=[
            pl.BlockSpec((1, 16, TILE, DEPTH), lambda s, t: (t[ROW_AT, s], 0, 0, 0)),
            pl.BlockSpec((1, 48, TILE), lambda s, t: (t[COL_NEAR, s], 0, 0)),
            pl.BlockSpec((tiles, 8, TILE), lambda s, t: (0, 0, 0)),
        ],
        out_specs=[
            pl.BlockSpec((1, TILE, TILE), lambda s, t: (s, 0, 0)),
            pl.BlockSpec((1, TILE, TILE), lambda s, t: (s, 0, 0)),
            pl.BlockSpec((blocks, 8, TILE), lambda s, t: (0, 0, 0)),
        ],
        scratch_shapes=[pltpu.VMEM((16, DEPTH, TILE), jnp.bfloat16)],
    )
    return pl.pallas_call(
        form_kernel,
        grid_spec=grid_spec,
        out_shape=[
            pltpu.HBM((slots, TILE, TILE), jnp.bfloat16),
            pltpu.HBM((slots, TILE, TILE), jnp.bfloat16),
            jax.ShapeDtypeStruct((blocks, 8, TILE), jnp.float32),
        ],
        compiler_params=pltpu.CompilerParams(vmem_limit_bytes=16 << 20),
        cost_estimate=pl.CostEstimate(
            flops=3 * 10**10, bytes_accessed=30 << 20, transcendentals=4 * 10**7
        ),
        name="form_and_apply",
    )(table, in_hbm(prepared), in_hbm(gathered), row_vec)


def rows_kernel(table, high_ref, low_ref, col_vec, row_acc):
    clear(row_acc)
    slot = pl.program_id(0)

    @pl.when(table[LIVE, slot] != 0)
    def _():
        row_acc[table[ROW_NEAR, slot]] += multiply(
            col_vec[table[COL_AT, slot]], high_ref[0], low_ref[0], BY_COLS
        )


def cols_kernel(table, high_ref, low_ref, row_vec, col_acc):
    clear(col_acc)
    slot = pl.program_id(0)

    @pl.when(table[CROSSING, slot] != 0)
    def _():
        col_acc[table[COL_AT, slot]] += multiply(
            row_vec[table[ROW_NEAR, slot]], high_ref[0], low_ref[0], BY_ROWS
        )


def apply_tiles(kernel, name, table, high, low, field, count):
    slots = table.shape[1]
    matrix = pl.BlockSpec((1, TILE, TILE), lambda s, t: (s, 0, 0))
    grid_spec = pltpu.PrefetchScalarGridSpec(
        num_scalar_prefetch=1,
        grid=(slots,),
        in_specs=[matrix, matrix, pl.BlockSpec(field.shape, lambda s, t: (0, 0, 0))],
        out_specs=pl.BlockSpec((count, 8, TILE), lambda s, t: (0, 0, 0)),
    )
    return pl.pallas_call(
        kernel,
        grid_spec=grid_spec,
        out_shape=jax.ShapeDtypeStruct((count, 8, TILE), jnp.float32),
        compiler_params=pltpu.CompilerParams(vmem_limit_bytes=8 << 20),
        cost_estimate=pl.CostEstimate(
            flops=3 * 10**9, bytes_accessed=12 << 20, transcendentals=0
        ),
        name=name,
    )(table, in_hbm(high), in_hbm(low), field)


def finish_kernel(near, rows_ref, total_ref, out_ref):
    scale = total_ref[...]
    for tile in range(near.shape[0]):
        out_ref[:, tile * TILE : (tile + 1) * TILE] = rows_ref[near[tile]] / scale


def finish(near, rows, root):
    tiles = rows.shape[0]
    return pl.pallas_call(
        finish_kernel,
        in_specs=[
            pl.BlockSpec(memory_space=pltpu.SMEM),
            pl.BlockSpec(memory_space=pltpu.VMEM),
            pl.BlockSpec(memory_space=pltpu.VMEM),
        ],
        out_specs=pl.BlockSpec(memory_space=pltpu.VMEM),
        out_shape=jax.ShapeDtypeStruct((8, tiles * TILE), jnp.float32),
        name="finish",
    )(near, rows, root)


def shift(value, axis, distance):
    size = lax.axis_size(axis)
    return lax.ppermute(value, axis, [(i, (i + distance) % size) for i in range(size)])


def spread(piece, axes):
    copies = jnp.broadcast_to(piece, (lax.axis_size(axes),) + piece.shape)
    return lax.all_to_all(copies, axes, 0, 0, tiled=True)


def spread_near(piece):
    mine = jnp.stack([piece] + [shift(piece, "x", d) for d in range(1, lax.axis_size("x"))])
    return jnp.concatenate([mine, shift(mine, "core", 1)], axis=0)


def reduce_near(row_acc):
    size = lax.axis_size("x")
    mine = row_acc[:size] + shift(row_acc[size:], "core", 1)
    total = mine[0]
    for d in range(1, size):
        total = total + shift(mine[d], "x", size - d)
    return total


def gather_sets(piece):
    near = jnp.stack([piece] + [shift(piece, "y", d) for d in range(1, lax.axis_size("y"))])
    return lax.all_gather(near, "z")


def combine(row_acc, col_acc):
    by_col = lax.all_to_all(col_acc, ROW, 0, 0, tiled=True)
    return reduce_near(row_acc) + jnp.sum(by_col, axis=0)


def near_tile(tile, x, core, size):
    return jnp.where(tile % 2 == core, 0, size) + (x - tile // 2) % size


def per_device(positions, vectors, pairs, valid):
    grid_row = lax.axis_index(ROW)
    grid_col = lax.axis_index(COL)
    x, core, y = lax.axis_index("x"), lax.axis_index("core"), lax.axis_index("y")
    size_x, size_y = lax.axis_size("x"), lax.axis_size("y")
    block = positions.shape[2]
    tiles = block // TILE
    blocks = lax.axis_size(ROW)
    local_rows = pairs[0, 0, :, 0]
    local_cols = pairs[0, 0, :, 1]
    live = valid[0, 0] != 0
    crossing = (grid_row * tiles + local_rows) != (local_cols * tiles + grid_col)
    near_cols = local_cols // size_y * size_y + (y - local_cols % size_y) % size_y
    table = jnp.stack(
        [
            local_rows,
            near_tile(local_rows, x, core, size_x),
            local_cols,
            near_cols,
            live.astype(jnp.int32),
            (live & crossing).astype(jnp.int32),
        ],
        axis=0,
    ).astype(jnp.int32)

    flat = positions.transpose(1, 0, 2).reshape(48, block)
    gathered = gather_sets(lax.dynamic_slice_in_dim(flat, grid_col * TILE, TILE, 1))
    gathered = gathered.reshape(blocks, 48, TILE)
    prepared = prepare_rows(flat)
    row_vec = vectors.reshape(8, tiles, TILE).transpose(1, 0, 2)
    own_vec = lax.dynamic_index_in_dim(row_vec, grid_col, 0, keepdims=False)
    gathered, own_vec = lax.optimization_barrier((gathered, own_vec))
    col_vec = spread(own_vec, ROW)

    high, low, col_acc = form_and_apply(table, prepared, gathered, row_vec)
    row_acc = apply_tiles(rows_kernel, "apply_rows", table, high, low, col_vec, tiles)
    first = combine(row_acc, col_acc)

    col_vec = spread(first, ROW)
    col_acc = apply_tiles(cols_kernel, "apply_cols", table, high, low, spread_near(first), blocks)
    row_acc = apply_tiles(rows_kernel, "apply_rows", table, high, low, col_vec, tiles)
    second = combine(row_acc, col_acc)

    squares = jnp.sum(second * second, axis=1)
    width = 128
    squares = spread(jnp.pad(squares[None, :], ((0, 0), (0, width - 8))), ALL)
    rows = spread_near(second)
    total = jnp.sum(squares[:, 0, :8], axis=0) / (block * blocks)
    root = jnp.sqrt(total + 1e-06)[:, None]
    near = near_tile(jnp.arange(tiles, dtype=jnp.int32), x, core, size_x)
    return finish(near.astype(jnp.int32), rows, jnp.broadcast_to(root, (8, TILE)))


def solution(mesh):
    physical = Mesh(mesh.devices.reshape(8, 4, 4, 2), ("z", "y", "x", "core"))
    placed = (
        P(None, None, ROW),
        P(None, ROW),
        P(ROW, COL, None, None),
        P(ROW, COL, None),
    )
    return jax.shard_map(
        per_device, mesh=physical, in_specs=placed, out_specs=P(None, ROW), check_vma=False
    )
```

```python
import functools
import math

import jax
import jax.numpy as jnp
from jax import lax
from jax.experimental import pallas as pl
from jax.experimental.pallas import tpu as pltpu
from jax.sharding import Mesh
from jax.sharding import PartitionSpec as P

TILE = 512
ROW = ("z", "y")
COL = ("x", "core")
ROW_AT, ROW_NEAR, COL_AT, SOURCE, PLACE, STAGE, LIVE, CROSSING = range(8)
PER_STAGE = 3
LAST_STAGE = 4
BY_ROWS = (((1,), (0,)), ((), ()))
BY_COLS = (((1,), (1,)), ((), ()))
LOG2E = math.log2(math.e)
GROUPS = 6
DEPTH = 8 * GROUPS
CHUNK = 256
HALF = 256


def in_hbm(value):
    return pltpu.with_memory_space_constraint(value, pltpu.HBM)


def split3(value):
    high = value.astype(jnp.bfloat16).astype(jnp.float32)
    rest = value - high
    mid = rest.astype(jnp.bfloat16).astype(jnp.float32)
    return high, mid, rest - mid


def rows_of(ref, snapshot, scale, norm_at, one_at):
    width = ref.shape[-1]
    place = lax.broadcasted_iota(jnp.int32, (8, width), 0)
    parts = [
        jnp.broadcast_to(ref[16 * q + snapshot : 16 * q + snapshot + 1, :], (8, width))
        for q in range(3)
    ]
    norm = (-0.5 * LOG2E) * (parts[0] * parts[0] + parts[1] * parts[1] + parts[2] * parts[2])
    out = jnp.where(place == norm_at, norm, jnp.where(place == one_at, 1.0, 0.0))
    for q in range(3):
        out = jnp.where(place == q, parts[q] * scale if scale != 1.0 else parts[q], out)
    return out


def prepare_kernel(pos_ref, out_ref):
    for snapshot in range(16):
        high, mid, low = split3(rows_of(pos_ref, snapshot, LOG2E, 4, 3))
        stacked = jnp.concatenate([high, high, mid, mid, high, low], axis=0)
        out_ref[0, snapshot] = stacked.T.astype(jnp.bfloat16)


def prepare_rows(pos):
    tiles = pos.shape[1] // TILE
    return pl.pallas_call(
        prepare_kernel,
        grid=(tiles,),
        in_specs=[pl.BlockSpec((48, TILE), lambda i: (0, i))],
        out_specs=pl.BlockSpec((1, 16, TILE, DEPTH), lambda i: (i, 0, 0, 0)),
        out_shape=jax.ShapeDtypeStruct((tiles, 16, TILE, DEPTH), jnp.bfloat16),
        compiler_params=pltpu.CompilerParams(vmem_limit_bytes=32 << 20),
        cost_estimate=pl.CostEstimate(flops=10**8, bytes_accessed=20 << 20, transcendentals=0),
        name="prepare_rows",
    )(pos)


def multiply(field, high, low, dims):
    terms = jnp.concatenate(split3(field), axis=0).astype(jnp.bfloat16)
    dot = functools.partial(
        lax.dot_general, dimension_numbers=dims, preferred_element_type=jnp.float32
    )
    by_high = dot(terms, high)
    by_low = dot(terms[:16], low)
    return (by_high[0:8] + by_low[0:8]) + (by_high[8:16] + by_low[8:16]) + by_high[16:24]


def stage_kernel(stage, sources, table, prepared_ref, row_vec, *refs):
    places = refs[:sources]
    high_ref, low_ref, row_acc, col_acc, tile, cols, high_tile, low_tile, sems = refs[-9:]
    if stage == 0:
        row_acc[...] = jnp.zeros_like(row_acc)
        col_acc[...] = jnp.zeros_like(col_acc)
    else:
        row_acc[...] = refs[sources + 2][...]
        col_acc[...] = refs[sources + 3][...]

    def form(slot):
        for source in range(sources):

            @pl.when(table[SOURCE, slot] == source)
            def _():
                tile[...] = places[source][table[PLACE, slot]]

        for snapshot in range(16):
            high, mid, low = split3(rows_of(tile, snapshot, 1.0, 3, 4))
            stacked = jnp.concatenate([high, mid, high, mid, low, high], axis=0)
            cols[snapshot] = stacked.astype(jnp.bfloat16)
        row_at = table[ROW_AT, slot]

        def step(at, carry):
            start = pl.multiple_of(at * CHUNK, CHUNK)
            for half in range(TILE // HALF):
                total = None
                for snapshot in range(16):
                    exponent = jnp.dot(
                        prepared_ref[row_at, snapshot, pl.ds(start, CHUNK), :],
                        cols[snapshot, :, half * HALF : (half + 1) * HALF],
                        preferred_element_type=jnp.float32,
                    )
                    term = jnp.exp2(exponent)
                    total = term if total is None else total + term
                high = total.astype(jnp.bfloat16)
                low = (total - high.astype(jnp.float32)).astype(jnp.bfloat16)
                place = (pl.ds(start, CHUNK), pl.ds(half * HALF, HALF))
                high_tile[place] = high
                low_tile[place] = low
            return carry

        lax.fori_loop(0, TILE // CHUNK, step, 0)
        copies = [
            pltpu.make_async_copy(high_tile, high_ref.at[slot], sems.at[0]),
            pltpu.make_async_copy(low_tile, low_ref.at[slot], sems.at[1]),
        ]
        for copy in copies:
            copy.start()
        row_acc[table[ROW_NEAR, slot]] += multiply(
            tile[48:56, :], high_tile[...], low_tile[...], BY_COLS
        )

        @pl.when(table[CROSSING, slot] != 0)
        def _():
            col_acc[table[COL_AT, slot]] += multiply(
                row_vec[row_at], high_tile[...], low_tile[...], BY_ROWS
            )

        for copy in copies:
            copy.wait()

    def visit(slot, carry):
        @pl.when(table[STAGE, slot] == stage)
        def _():
            form(slot)

        return carry

    lax.fori_loop(0, high_ref.shape[0], visit, 0)


def form_stage(stage, table, prepared, row_vec, places, state, blocks):
    slots = table.shape[1]
    tiles = row_vec.shape[0]
    vmem = pl.BlockSpec(memory_space=pltpu.VMEM)
    hbm = pl.BlockSpec(memory_space=pltpu.HBM)
    shapes = [
        pltpu.HBM((slots, TILE, TILE), jnp.bfloat16),
        pltpu.HBM((slots, TILE, TILE), jnp.bfloat16),
        jax.ShapeDtypeStruct((tiles, 8, TILE), jnp.float32),
        jax.ShapeDtypeStruct((blocks, 8, TILE), jnp.float32),
    ]
    first = 3 + len(places)
    return pl.pallas_call(
        functools.partial(stage_kernel, stage, len(places)),
        in_specs=[pl.BlockSpec(memory_space=pltpu.SMEM)]
        + [vmem] * (2 + len(places))
        + ([hbm, hbm, vmem, vmem] if state else []),
        out_specs=[hbm, hbm, vmem, vmem],
        out_shape=shapes,
        input_output_aliases={first + i: i for i in range(len(state))},
        scratch_shapes=[
            pltpu.VMEM((56, TILE), jnp.float32),
            pltpu.VMEM((16, DEPTH, TILE), jnp.bfloat16),
            pltpu.VMEM((TILE, TILE), jnp.bfloat16),
            pltpu.VMEM((TILE, TILE), jnp.bfloat16),
            pltpu.SemaphoreType.DMA((2,)),
        ],
        compiler_params=pltpu.CompilerParams(vmem_limit_bytes=8 << 20),
        cost_estimate=pl.CostEstimate(
            flops=8 * 10**9, bytes_accessed=8 << 20, transcendentals=10**7
        ),
        name=f"form_{stage}",
    )(table, prepared, row_vec, *places, *state)


def apply_kernel(wanted, table, high_ref, low_ref, field, acc, high, low, sems):
    slots = high_ref.shape[0]

    def copies(slot):
        return [
            pltpu.make_async_copy(high_ref.at[slot], high.at[slot], sems.at[0, slot]),
            pltpu.make_async_copy(low_ref.at[slot], low.at[slot], sems.at[1, slot]),
        ]

    for slot in range(slots):

        @pl.when(table[wanted, slot] != 0)
        def _():
            for copy in copies(slot):
                copy.start()

    acc[...] = jnp.zeros_like(acc)

    def visit(slot, carry):
        @pl.when(table[wanted, slot] != 0)
        def _():
            for copy in copies(slot):
                copy.wait()
            row_at, col_at = table[ROW_NEAR, slot], table[COL_AT, slot]
            if wanted == LIVE:
                acc[row_at] += multiply(field[col_at], high[slot], low[slot], BY_COLS)
            else:
                acc[col_at] += multiply(field[row_at], high[slot], low[slot], BY_ROWS)

        return carry

    lax.fori_loop(0, slots, visit, 0)


def apply_tiles(wanted, name, table, high, low, field, count):
    vmem = pl.BlockSpec(memory_space=pltpu.VMEM)
    hbm = pl.BlockSpec(memory_space=pltpu.HBM)
    return pl.pallas_call(
        functools.partial(apply_kernel, wanted),
        in_specs=[pl.BlockSpec(memory_space=pltpu.SMEM), hbm, hbm, vmem],
        out_specs=vmem,
        out_shape=jax.ShapeDtypeStruct((count, 8, TILE), jnp.float32),
        scratch_shapes=[
            pltpu.VMEM(high.shape, high.dtype),
            pltpu.VMEM(low.shape, low.dtype),
            pltpu.SemaphoreType.DMA((2, high.shape[0])),
        ],
        compiler_params=pltpu.CompilerParams(vmem_limit_bytes=16 << 20),
        cost_estimate=pl.CostEstimate(
            flops=3 * 10**9, bytes_accessed=12 << 20, transcendentals=0
        ),
        name=name,
    )(table, in_hbm(high), in_hbm(low), field)


def shift(value, axis, distance):
    size = lax.axis_size(axis)
    return lax.ppermute(value, axis, [(i, (i + distance) % size) for i in range(size)])


def spread(piece, axes):
    copies = jnp.broadcast_to(piece, (lax.axis_size(axes),) + piece.shape)
    return lax.all_to_all(copies, axes, 0, 0, tiled=True)


def spread_near(piece):
    mine = jnp.stack([piece] + [shift(piece, "x", d) for d in range(1, lax.axis_size("x"))])
    return jnp.concatenate([mine, shift(mine, "core", 1)], axis=0)


def reduce_near(row_acc):
    size = lax.axis_size("x")
    mine = row_acc[:size] + shift(row_acc[size:], "core", 1)
    total = mine[0]
    for d in range(1, size):
        total = total + shift(mine[d], "x", size - d)
    return total


def gather_near(piece):
    near = jnp.stack([piece] + [shift(piece, "y", d) for d in range(1, lax.axis_size("y"))])
    size, half = lax.axis_size("z"), near.shape[0] // 2
    arrived = [[near]]
    behind = ahead = near
    for distance in range(1, size // 2 + 1):
        if distance == size // 2:
            behind, ahead = behind[:half], ahead[half:]
        behind, ahead = shift(behind, "z", 1), shift(ahead, "z", size - 1)
        arrived.append([behind, ahead])
    return arrived


def plan(source, live):
    stage = jnp.where(live, (source + 1) // 2, LAST_STAGE)
    slots = jnp.arange(source.shape[0])
    key = stage * source.shape[0] + slots
    before = key[None, :] <= key[:, None]
    rank = jnp.sum(before.astype(jnp.int32), axis=1)
    turn = jnp.max(
        jnp.where(before, PER_STAGE * stage[None, :] + rank[:, None] - rank[None, :], 0), axis=1
    )
    return jnp.where(live, jnp.minimum(turn // PER_STAGE, LAST_STAGE), -1)


def combine(row_acc, col_acc):
    by_col = lax.all_to_all(col_acc, ROW, 0, 0, tiled=True)
    return reduce_near(row_acc) + jnp.sum(by_col, axis=0)


def near_tile(tile, x, core, size):
    return jnp.where(tile % 2 == core, 0, size) + (x - tile // 2) % size


def per_device(positions, vectors, pairs, valid):
    grid_row = lax.axis_index(ROW)
    grid_col = lax.axis_index(COL)
    x, core = lax.axis_index("x"), lax.axis_index("core")
    y, z = lax.axis_index("y"), lax.axis_index("z")
    size_x, size_y = lax.axis_size("x"), lax.axis_size("y")
    block = positions.shape[2]
    tiles = block // TILE
    blocks = lax.axis_size(ROW)
    local_rows = pairs[0, 0, :, 0]
    local_cols = pairs[0, 0, :, 1]
    live = valid[0, 0] != 0
    crossing = (grid_row * tiles + local_rows) != (local_cols * tiles + grid_col)
    size_z = lax.axis_size("z")
    behind = (z - local_cols // size_y) % size_z
    place = (y - local_cols % size_y) % size_y
    far = behind == size_z // 2
    upper = place >= size_y // 2
    source = jnp.where(behind < size_z // 2, 2 * behind - 1, 2 * (size_z - behind))
    source = jnp.where(behind == 0, 0, jnp.where(far & ~upper, size_z - 1, source))
    place = jnp.where(far & upper, place - size_y // 2, place)
    table = jnp.stack(
        [
            local_rows,
            near_tile(local_rows, x, core, size_x),
            local_cols,
            source,
            place,
            plan(source, live),
            live.astype(jnp.int32),
            (live & crossing).astype(jnp.int32),
        ],
        axis=0,
    ).astype(jnp.int32)

    flat = positions.transpose(1, 0, 2).reshape(48, block)
    own = jnp.concatenate(
        [
            lax.dynamic_slice_in_dim(flat, grid_col * TILE, TILE, 1),
            lax.dynamic_slice_in_dim(vectors, grid_col * TILE, TILE, 1),
        ],
        axis=0,
    )
    row_vec = vectors.reshape(8, tiles, TILE).transpose(1, 0, 2)
    prepared = prepare_rows(flat)
    places, state = [], []
    for stage, arrived in enumerate(gather_near(own)):
        places = places + arrived
        state = form_stage(stage, table, prepared, row_vec, places, state, blocks)
    high, low, row_acc, col_acc = state
    first = combine(row_acc, col_acc)

    col_vec = spread(first, ROW)
    col_acc = apply_tiles(CROSSING, "apply_cols", table, high, low, spread_near(first), blocks)
    row_acc = apply_tiles(LIVE, "apply_rows", table, high, low, col_vec, tiles)
    second = combine(row_acc, col_acc)

    rows = spread(second, COL)
    squares = jnp.sum(rows * rows, axis=(0, 2))
    squares = spread(jnp.broadcast_to(squares[:, None], (8, 128)), ROW)
    total = jnp.sum(squares[:, :, 0], axis=0) / (block * blocks)
    scaled = rows / jnp.sqrt(total + 1e-06)[None, :, None]
    return scaled.transpose(1, 0, 2).reshape(8, block)


def solution(mesh):
    physical = Mesh(mesh.devices.reshape(8, 4, 4, 2), ("z", "y", "x", "core"))
    placed = (
        P(None, None, ROW),
        P(None, ROW),
        P(ROW, COL, None, None),
        P(ROW, COL, None),
    )
    return jax.shard_map(
        per_device, mesh=physical, in_specs=placed, out_specs=P(None, ROW), check_vma=False
    )
```

```python
import functools
import math

import jax
import jax.numpy as jnp
from jax import lax
from jax.experimental import pallas as pl
from jax.experimental.pallas import tpu as pltpu
from jax.sharding import Mesh
from jax.sharding import PartitionSpec as P

TILE = 512
ROW = ("z", "y")
COL = ("x", "core")
ROW_AT, ROW_NEAR, COL_AT, SOURCE, PLACE, STAGE, LIVE, CROSSING = range(8)
LAST_STAGE = 4
BY_ROWS = (((1,), (0,)), ((), ()))
BY_COLS = (((1,), (1,)), ((), ()))
LOG2E = math.log2(math.e)
GROUPS = 6
DEPTH = 8 * GROUPS
CHUNK = 256
HALF = 256


def in_hbm(value):
    return pltpu.with_memory_space_constraint(value, pltpu.HBM)


def split3(value):
    high = value.astype(jnp.bfloat16).astype(jnp.float32)
    rest = value - high
    mid = rest.astype(jnp.bfloat16).astype(jnp.float32)
    return high, mid, rest - mid


def rows_of(ref, snapshot, scale, norm_at, one_at):
    width = ref.shape[-1]
    place = lax.broadcasted_iota(jnp.int32, (8, width), 0)
    parts = [
        jnp.broadcast_to(ref[16 * q + snapshot : 16 * q + snapshot + 1, :], (8, width))
        for q in range(3)
    ]
    norm = (-0.5 * LOG2E) * (parts[0] * parts[0] + parts[1] * parts[1] + parts[2] * parts[2])
    out = jnp.where(place == norm_at, norm, jnp.where(place == one_at, 1.0, 0.0))
    for q in range(3):
        out = jnp.where(place == q, parts[q] * scale if scale != 1.0 else parts[q], out)
    return out


def prepare_kernel(pos_ref, out_ref):
    for snapshot in range(16):
        high, mid, low = split3(rows_of(pos_ref, snapshot, LOG2E, 4, 3))
        stacked = jnp.concatenate([high, high, mid, mid, high, low], axis=0)
        out_ref[0, snapshot] = stacked.T.astype(jnp.bfloat16)


def prepare_rows(pos):
    tiles = pos.shape[1] // TILE
    return pl.pallas_call(
        prepare_kernel,
        grid=(tiles,),
        in_specs=[pl.BlockSpec((48, TILE), lambda i: (0, i))],
        out_specs=pl.BlockSpec((1, 16, TILE, DEPTH), lambda i: (i, 0, 0, 0)),
        out_shape=jax.ShapeDtypeStruct((tiles, 16, TILE, DEPTH), jnp.bfloat16),
        compiler_params=pltpu.CompilerParams(vmem_limit_bytes=32 << 20),
        cost_estimate=pl.CostEstimate(flops=10**8, bytes_accessed=20 << 20, transcendentals=0),
        name="prepare_rows",
    )(pos)


def multiply(field, high, low, dims):
    terms = jnp.concatenate(split3(field), axis=0).astype(jnp.bfloat16)
    dot = functools.partial(
        lax.dot_general, dimension_numbers=dims, preferred_element_type=jnp.float32
    )
    by_high = dot(terms, high)
    by_low = dot(terms[:16], low)
    return (by_high[0:8] + by_low[0:8]) + (by_high[8:16] + by_low[8:16]) + by_high[16:24]


def stage_kernel(stage, sources, table, prepared_ref, row_vec, *refs):
    places = refs[:sources]
    high_ref, low_ref, row_acc, col_acc, tile, cols, high_tile, low_tile, sems = refs[-9:]
    if stage == 0:
        row_acc[...] = jnp.zeros_like(row_acc)
        col_acc[...] = jnp.zeros_like(col_acc)
    else:
        row_acc[...] = refs[sources + 2][...]
        col_acc[...] = refs[sources + 3][...]

    def copies(slot):
        return [
            pltpu.make_async_copy(high_tile, high_ref.at[slot], sems.at[0]),
            pltpu.make_async_copy(low_tile, low_ref.at[slot], sems.at[1]),
        ]

    def form(slot, pending):
        for source in range(sources):

            @pl.when(table[SOURCE, slot] == source)
            def _():
                tile[...] = places[source][table[PLACE, slot]]

        for snapshot in range(16):
            high, mid, low = split3(rows_of(tile, snapshot, 1.0, 3, 4))
            stacked = jnp.concatenate([high, mid, high, mid, low, high], axis=0)
            cols[snapshot] = stacked.astype(jnp.bfloat16)
        row_at = table[ROW_AT, slot]

        @pl.when(pending != 0)
        def _():
            for copy in copies(slot):
                copy.wait()

        def step(at, carry):
            start = pl.multiple_of(at * CHUNK, CHUNK)
            for half in range(TILE // HALF):
                total = None
                for snapshot in range(16):
                    exponent = jnp.dot(
                        prepared_ref[row_at, snapshot, pl.ds(start, CHUNK), :],
                        cols[snapshot, :, half * HALF : (half + 1) * HALF],
                        preferred_element_type=jnp.float32,
                    )
                    term = jnp.exp2(exponent)
                    total = term if total is None else total + term
                high = total.astype(jnp.bfloat16)
                low = (total - high.astype(jnp.float32)).astype(jnp.bfloat16)
                place = (pl.ds(start, CHUNK), pl.ds(half * HALF, HALF))
                high_tile[place] = high
                low_tile[place] = low
            return carry

        lax.fori_loop(0, TILE // CHUNK, step, 0)
        for copy in copies(slot):
            copy.start()
        row_acc[table[ROW_NEAR, slot]] += multiply(
            tile[48:56, :], high_tile[...], low_tile[...], BY_COLS
        )

        @pl.when(table[CROSSING, slot] != 0)
        def _():
            col_acc[table[COL_AT, slot]] += multiply(
                row_vec[row_at], high_tile[...], low_tile[...], BY_ROWS
            )

    def visit(slot, pending):
        mine = table[STAGE, slot] == stage

        @pl.when(mine)
        def _():
            form(slot, pending)

        return jnp.where(mine, 1, pending)

    pending = lax.fori_loop(0, high_ref.shape[0], visit, 0)

    @pl.when(pending != 0)
    def _():
        for copy in copies(0):
            copy.wait()


def form_stage(stage, table, prepared, row_vec, places, state, blocks):
    slots = table.shape[1]
    tiles = row_vec.shape[0]
    vmem = pl.BlockSpec(memory_space=pltpu.VMEM)
    hbm = pl.BlockSpec(memory_space=pltpu.HBM)
    shapes = [
        pltpu.HBM((slots, TILE, TILE), jnp.bfloat16),
        pltpu.HBM((slots, TILE, TILE), jnp.bfloat16),
        jax.ShapeDtypeStruct((tiles, 8, TILE), jnp.float32),
        jax.ShapeDtypeStruct((blocks, 8, TILE), jnp.float32),
    ]
    first = 3 + len(places)
    return pl.pallas_call(
        functools.partial(stage_kernel, stage, len(places)),
        in_specs=[pl.BlockSpec(memory_space=pltpu.SMEM)]
        + [vmem] * (2 + len(places))
        + ([hbm, hbm, vmem, vmem] if state else []),
        out_specs=[hbm, hbm, vmem, vmem],
        out_shape=shapes,
        input_output_aliases={
            first + i: i for i in range(2 if stage == LAST_STAGE else len(state))
        },
        scratch_shapes=[
            pltpu.VMEM((56, TILE), jnp.float32),
            pltpu.VMEM((16, DEPTH, TILE), jnp.bfloat16),
            pltpu.VMEM((TILE, TILE), jnp.bfloat16),
            pltpu.VMEM((TILE, TILE), jnp.bfloat16),
            pltpu.SemaphoreType.DMA((2,)),
        ],
        compiler_params=pltpu.CompilerParams(vmem_limit_bytes=8 << 20),
        cost_estimate=pl.CostEstimate(
            flops=8 * 10**9, bytes_accessed=8 << 20, transcendentals=10**7
        ),
        name=f"form_{stage}",
    )(table, prepared, row_vec, *places, *state)


def apply_kernel(wanted, table, high_ref, low_ref, field, acc, high, low, sems):
    slots = high_ref.shape[0]

    def copies(slot):
        return [
            pltpu.make_async_copy(high_ref.at[slot], high.at[slot], sems.at[0, slot]),
            pltpu.make_async_copy(low_ref.at[slot], low.at[slot], sems.at[1, slot]),
        ]

    for slot in range(slots):

        @pl.when(table[wanted, slot] != 0)
        def _():
            for copy in copies(slot):
                copy.start()

    acc[...] = jnp.zeros_like(acc)

    def visit(slot, carry):
        @pl.when(table[wanted, slot] != 0)
        def _():
            for copy in copies(slot):
                copy.wait()
            row_at, col_at = table[ROW_NEAR, slot], table[COL_AT, slot]
            if wanted == LIVE:
                acc[row_at] += multiply(field[col_at], high[slot], low[slot], BY_COLS)
            else:
                acc[col_at] += multiply(field[row_at], high[slot], low[slot], BY_ROWS)

        return carry

    lax.fori_loop(0, slots, visit, 0)


def apply_tiles(wanted, name, table, high, low, field, count):
    vmem = pl.BlockSpec(memory_space=pltpu.VMEM)
    hbm = pl.BlockSpec(memory_space=pltpu.HBM)
    return pl.pallas_call(
        functools.partial(apply_kernel, wanted),
        in_specs=[pl.BlockSpec(memory_space=pltpu.SMEM), hbm, hbm, vmem],
        out_specs=vmem,
        out_shape=jax.ShapeDtypeStruct((count, 8, TILE), jnp.float32),
        scratch_shapes=[
            pltpu.VMEM(high.shape, high.dtype),
            pltpu.VMEM(low.shape, low.dtype),
            pltpu.SemaphoreType.DMA((2, high.shape[0])),
        ],
        compiler_params=pltpu.CompilerParams(vmem_limit_bytes=16 << 20),
        cost_estimate=pl.CostEstimate(
            flops=3 * 10**9, bytes_accessed=12 << 20, transcendentals=0
        ),
        name=name,
    )(table, in_hbm(high), in_hbm(low), field)


def shift(value, axis, distance):
    size = lax.axis_size(axis)
    return lax.ppermute(value, axis, [(i, (i + distance) % size) for i in range(size)])


def spread(piece, axes):
    copies = jnp.broadcast_to(piece, (lax.axis_size(axes),) + piece.shape)
    return lax.all_to_all(copies, axes, 0, 0, tiled=True)


def spread_near(piece):
    mine = jnp.stack([piece] + [shift(piece, "x", d) for d in range(1, lax.axis_size("x"))])
    return jnp.concatenate([mine, shift(mine, "core", 1)], axis=0)


def reduce_near(row_acc):
    size = lax.axis_size("x")
    mine = row_acc[:size] + shift(row_acc[size:], "core", 1)
    total = mine[0]
    for d in range(1, size):
        total = total + shift(mine[d], "x", size - d)
    return total


def gather_y(piece):
    return jnp.stack([piece] + [shift(piece, "y", d) for d in range(1, lax.axis_size("y"))])


def gather_z(near):
    size, half = lax.axis_size("z"), near.shape[0] // 2
    arrived = [[near]]
    behind = ahead = near
    for distance in range(1, size // 2 + 1):
        if distance == size // 2:
            behind, ahead = behind[:half], ahead[half:]
        behind, ahead = shift(behind, "z", 1), shift(ahead, "z", size - 1)
        arrived.append([behind, ahead])
    return arrived


def plan(source, live):
    stage = jnp.where(live, (source + 1) // 2, LAST_STAGE)
    slots = jnp.arange(source.shape[0])
    key = stage * source.shape[0] + slots
    before = key[None, :] <= key[:, None]
    rank = jnp.sum(before.astype(jnp.int32), axis=1)
    start = jnp.maximum(3 * stage - 1, 0)
    turn = jnp.max(jnp.where(before, start[None, :] + rank[:, None] - rank[None, :], 0), axis=1)
    return jnp.where(live, jnp.minimum((turn + 1) // 3, LAST_STAGE), -1)


def combine(row_acc, col_acc):
    by_col = lax.all_to_all(col_acc, ROW, 0, 0, tiled=True)
    return reduce_near(row_acc) + jnp.sum(by_col, axis=0)


def near_tile(tile, x, core, size):
    return jnp.where(tile % 2 == core, 0, size) + (x - tile // 2) % size


def per_device(positions, vectors, pairs, valid):
    grid_row = lax.axis_index(ROW)
    grid_col = lax.axis_index(COL)
    x, core = lax.axis_index("x"), lax.axis_index("core")
    y, z = lax.axis_index("y"), lax.axis_index("z")
    size_x, size_y = lax.axis_size("x"), lax.axis_size("y")
    block = positions.shape[2]
    tiles = block // TILE
    blocks = lax.axis_size(ROW)
    local_rows = pairs[0, 0, :, 0]
    local_cols = pairs[0, 0, :, 1]
    live = valid[0, 0] != 0
    crossing = (grid_row * tiles + local_rows) != (local_cols * tiles + grid_col)
    size_z = lax.axis_size("z")
    behind = (z - local_cols // size_y) % size_z
    place = (y - local_cols % size_y) % size_y
    far = behind == size_z // 2
    upper = place >= size_y // 2
    source = jnp.where(behind < size_z // 2, 2 * behind - 1, 2 * (size_z - behind))
    source = jnp.where(behind == 0, 0, jnp.where(far & ~upper, size_z - 1, source))
    place = jnp.where(far & upper, place - size_y // 2, place)
    table = jnp.stack(
        [
            local_rows,
            near_tile(local_rows, x, core, size_x),
            local_cols,
            source,
            place,
            plan(source, live),
            live.astype(jnp.int32),
            (live & crossing).astype(jnp.int32),
        ],
        axis=0,
    ).astype(jnp.int32)

    flat = positions.transpose(1, 0, 2).reshape(48, block)
    own = jnp.concatenate(
        [
            lax.dynamic_slice_in_dim(flat, grid_col * TILE, TILE, 1),
            lax.dynamic_slice_in_dim(vectors, grid_col * TILE, TILE, 1),
        ],
        axis=0,
    )
    row_vec = vectors.reshape(8, tiles, TILE).transpose(1, 0, 2)
    near = gather_y(own)
    flat, near = lax.optimization_barrier((flat, near))
    prepared = prepare_rows(flat)
    places, state = [], []
    for stage, arrived in enumerate(gather_z(near)):
        places = places + arrived
        state = form_stage(stage, table, prepared, row_vec, places, state, blocks)
    high, low, row_acc, col_acc = state
    first = combine(row_acc, col_acc)

    col_vec = spread(first, ROW)
    col_acc = apply_tiles(CROSSING, "apply_cols", table, high, low, spread_near(first), blocks)
    row_acc = apply_tiles(LIVE, "apply_rows", table, high, low, col_vec, tiles)
    second = combine(row_acc, col_acc)

    rows = spread(second, COL)
    squares = jnp.sum(rows * rows, axis=(0, 2))
    squares = spread(jnp.pad(squares[None, :], ((0, 0), (0, 120))), ROW)
    total = jnp.sum(squares[:, 0, :8], axis=0) / (block * blocks)
    scaled = rows / jnp.sqrt(total + 1e-06)[None, :, None]
    return scaled.transpose(1, 0, 2).reshape(8, block)


def solution(mesh):
    physical = Mesh(mesh.devices.reshape(8, 4, 4, 2), ("z", "y", "x", "core"))
    placed = (
        P(None, None, ROW),
        P(None, ROW),
        P(ROW, COL, None, None),
        P(ROW, COL, None),
    )
    return jax.shard_map(
        per_device, mesh=physical, in_specs=placed, out_specs=P(None, ROW), check_vma=False
    )
```

```python
import functools
import math

import jax
import jax.numpy as jnp
from jax import lax
from jax.experimental import pallas as pl
from jax.experimental.pallas import tpu as pltpu
from jax.sharding import Mesh
from jax.sharding import PartitionSpec as P

TILE = 512
ROW = ("z", "y")
COL = ("x", "core")
ROW_AT, ROW_NEAR, COL_AT, SOURCE, PLACE, STAGE, LIVE, CROSSING = range(8)
LAST_STAGE = 4
BY_ROWS = (((1,), (0,)), ((), ()))
BY_COLS = (((1,), (1,)), ((), ()))
LOG2E = math.log2(math.e)
GROUPS = 6
DEPTH = 8 * GROUPS
HALF = 256


def in_hbm(value):
    return pltpu.with_memory_space_constraint(value, pltpu.HBM)


def split3(value):
    high = value.astype(jnp.bfloat16).astype(jnp.float32)
    rest = value - high
    mid = rest.astype(jnp.bfloat16).astype(jnp.float32)
    return high, mid, rest - mid


def rows_of(ref, snapshot, scale, norm_at, one_at):
    width = ref.shape[-1]
    place = lax.broadcasted_iota(jnp.int32, (8, width), 0)
    parts = [
        jnp.broadcast_to(ref[16 * q + snapshot : 16 * q + snapshot + 1, :], (8, width))
        for q in range(3)
    ]
    norm = (-0.5 * LOG2E) * (parts[0] * parts[0] + parts[1] * parts[1] + parts[2] * parts[2])
    out = jnp.where(place == norm_at, norm, jnp.where(place == one_at, 1.0, 0.0))
    for q in range(3):
        out = jnp.where(place == q, parts[q] * scale if scale != 1.0 else parts[q], out)
    return out


def prepare_kernel(pos_ref, out_ref):
    def visit(tile, carry):
        part = pos_ref.at[:, pl.ds(pl.multiple_of(tile * TILE, TILE), TILE)]
        for snapshot in range(16):
            high, mid, low = split3(rows_of(part, snapshot, LOG2E, 4, 3))
            stacked = jnp.concatenate([high, high, mid, mid, high, low], axis=0)
            out_ref[tile, snapshot] = stacked.T.astype(jnp.bfloat16)
        return carry

    lax.fori_loop(0, out_ref.shape[0], visit, 0)


def prepare_rows(pos):
    tiles = pos.shape[1] // TILE
    vmem = pl.BlockSpec(memory_space=pltpu.VMEM)
    return pl.pallas_call(
        prepare_kernel,
        in_specs=[vmem],
        out_specs=vmem,
        out_shape=jax.ShapeDtypeStruct((tiles, 16, TILE, DEPTH), jnp.bfloat16),
        compiler_params=pltpu.CompilerParams(vmem_limit_bytes=4 << 20),
        cost_estimate=pl.CostEstimate(flops=10**8, bytes_accessed=8 << 20, transcendentals=0),
        name="prepare_rows",
    )(pos)


def multiply(field, high, low, dims):
    terms = jnp.concatenate(split3(field), axis=0).astype(jnp.bfloat16)
    dot = functools.partial(
        lax.dot_general, dimension_numbers=dims, preferred_element_type=jnp.float32
    )
    by_high = dot(terms, high)
    by_low = dot(terms[:16], low)
    return (by_high[0:8] + by_low[0:8]) + (by_high[8:16] + by_low[8:16]) + by_high[16:24]


def stage_kernel(stage, sources, table, prepared_ref, row_vec, *refs):
    places = refs[:sources]
    high_ref, low_ref, slot_vec, col_acc, tile, cols, high_tile, low_tile, sems = refs[-9:]
    if stage == 0:
        col_acc[...] = jnp.zeros_like(col_acc)
    else:
        slot_vec[...] = refs[sources + 2][...]
        col_acc[...] = refs[sources + 3][...]

    def copies(slot):
        return [
            pltpu.make_async_copy(high_tile, high_ref.at[slot], sems.at[0]),
            pltpu.make_async_copy(low_tile, low_ref.at[slot], sems.at[1]),
        ]

    def form(slot, pending):
        for source in range(sources):

            @pl.when(table[SOURCE, slot] == source)
            def _():
                tile[...] = places[source][table[PLACE, slot]]

        for snapshot in range(16):
            high, mid, low = split3(rows_of(tile, snapshot, 1.0, 3, 4))
            stacked = jnp.concatenate([high, mid, high, mid, low, high], axis=0)
            cols[snapshot] = stacked.astype(jnp.bfloat16)
        row_at = table[ROW_AT, slot]

        @pl.when(pending != 0)
        def _():
            for copy in copies(slot):
                copy.wait()

        def step(at, carry):
            part = pl.ds(pl.multiple_of(at * HALF, HALF), HALF)
            total = None
            for snapshot in range(16):
                exponent = jnp.dot(
                    prepared_ref[row_at, snapshot],
                    cols[snapshot, :, part],
                    preferred_element_type=jnp.float32,
                )
                term = jnp.exp2(exponent)
                total = term if total is None else total + term
            high = total.astype(jnp.bfloat16)
            high_tile[:, part] = high
            low_tile[:, part] = (total - high.astype(jnp.float32)).astype(jnp.bfloat16)
            return carry

        lax.fori_loop(0, TILE // HALF, step, 0)
        for copy in copies(slot):
            copy.start()
        slot_vec[slot] = tile[48:56, :]

        @pl.when(table[CROSSING, slot] != 0)
        def _():
            col_acc[table[COL_AT, slot]] += multiply(
                row_vec[row_at], high_tile[...], low_tile[...], BY_ROWS
            )

    def visit(slot, pending):
        mine = table[STAGE, slot] == stage

        @pl.when(mine)
        def _():
            form(slot, pending)

        return jnp.where(mine, 1, pending)

    pending = lax.fori_loop(0, high_ref.shape[0], visit, 0)

    @pl.when(pending != 0)
    def _():
        for copy in copies(0):
            copy.wait()


def form_stage(stage, table, prepared, row_vec, places, state, blocks):
    slots = table.shape[1]
    vmem = pl.BlockSpec(memory_space=pltpu.VMEM)
    hbm = pl.BlockSpec(memory_space=pltpu.HBM)
    shapes = [
        pltpu.HBM((slots, TILE, TILE), jnp.bfloat16),
        pltpu.HBM((slots, TILE, TILE), jnp.bfloat16),
        jax.ShapeDtypeStruct((slots, 8, TILE), jnp.float32),
        jax.ShapeDtypeStruct((blocks, 8, TILE), jnp.float32),
    ]
    first = 3 + len(places)
    return pl.pallas_call(
        functools.partial(stage_kernel, stage, len(places)),
        in_specs=[pl.BlockSpec(memory_space=pltpu.SMEM)]
        + [vmem] * (2 + len(places))
        + ([hbm, hbm, vmem, vmem] if state else []),
        out_specs=[hbm, hbm, vmem, vmem],
        out_shape=shapes,
        input_output_aliases={
            first + i: i for i in range(2 if stage == LAST_STAGE else len(state))
        },
        scratch_shapes=[
            pltpu.VMEM((56, TILE), jnp.float32),
            pltpu.VMEM((16, DEPTH, TILE), jnp.bfloat16),
            pltpu.VMEM((TILE, TILE), jnp.bfloat16),
            pltpu.VMEM((TILE, TILE), jnp.bfloat16),
            pltpu.SemaphoreType.DMA((2,)),
        ],
        compiler_params=pltpu.CompilerParams(vmem_limit_bytes=8 << 20),
        cost_estimate=pl.CostEstimate(
            flops=8 * 10**9, bytes_accessed=8 << 20, transcendentals=10**7
        ),
        name=f"form_{stage}",
    )(table, prepared, row_vec, *places, *state)


def apply_kernel(wanted, col_at, table, high_ref, low_ref, field, acc, high, low, sems):
    slots = high_ref.shape[0]

    def copies(slot):
        return [
            pltpu.make_async_copy(high_ref.at[slot], high.at[slot], sems.at[0, slot]),
            pltpu.make_async_copy(low_ref.at[slot], low.at[slot], sems.at[1, slot]),
        ]

    for slot in range(slots):

        @pl.when(table[wanted, slot] != 0)
        def _():
            for copy in copies(slot):
                copy.start()

    acc[...] = jnp.zeros_like(acc)

    def visit(slot, carry):
        @pl.when(table[wanted, slot] != 0)
        def _():
            for copy in copies(slot):
                copy.wait()
            row = table[ROW_NEAR, slot]
            col = slot if col_at is None else table[col_at, slot]
            if wanted == LIVE:
                acc[row] += multiply(field[col], high[slot], low[slot], BY_COLS)
            else:
                acc[col] += multiply(field[row], high[slot], low[slot], BY_ROWS)

        return carry

    lax.fori_loop(0, slots, visit, 0)


def apply_tiles(wanted, col_at, name, table, high, low, field, count):
    vmem = pl.BlockSpec(memory_space=pltpu.VMEM)
    hbm = pl.BlockSpec(memory_space=pltpu.HBM)
    return pl.pallas_call(
        functools.partial(apply_kernel, wanted, col_at),
        in_specs=[pl.BlockSpec(memory_space=pltpu.SMEM), hbm, hbm, vmem],
        out_specs=vmem,
        out_shape=jax.ShapeDtypeStruct((count, 8, TILE), jnp.float32),
        scratch_shapes=[
            pltpu.VMEM(high.shape, high.dtype),
            pltpu.VMEM(low.shape, low.dtype),
            pltpu.SemaphoreType.DMA((2, high.shape[0])),
        ],
        compiler_params=pltpu.CompilerParams(vmem_limit_bytes=16 << 20),
        cost_estimate=pl.CostEstimate(
            flops=3 * 10**9, bytes_accessed=12 << 20, transcendentals=0
        ),
        name=name,
    )(table, in_hbm(high), in_hbm(low), field)


def shift(value, axis, distance):
    size = lax.axis_size(axis)
    return lax.ppermute(value, axis, [(i, (i + distance) % size) for i in range(size)])


def spread(piece, axes):
    copies = jnp.broadcast_to(piece, (lax.axis_size(axes),) + piece.shape)
    return lax.all_to_all(copies, axes, 0, 0, tiled=True)


def spread_near(piece):
    mine = jnp.stack([piece] + [shift(piece, "x", d) for d in range(1, lax.axis_size("x"))])
    return jnp.concatenate([mine, shift(mine, "core", 1)], axis=0)


def reduce_near(row_acc):
    size = lax.axis_size("x")
    mine = row_acc[:size] + shift(row_acc[size:], "core", 1)
    total = mine[0]
    for d in range(1, size):
        total = total + shift(mine[d], "x", size - d)
    return total


def gather_y(piece):
    return jnp.stack([piece] + [shift(piece, "y", d) for d in range(1, lax.axis_size("y"))])


def gather_z(near):
    size, half = lax.axis_size("z"), near.shape[0] // 2
    arrived = [[near]]
    behind = ahead = near
    for distance in range(1, size // 2 + 1):
        if distance == size // 2:
            behind, ahead = behind[:half], ahead[half:]
        behind, ahead = shift(behind, "z", 1), shift(ahead, "z", size - 1)
        arrived.append([behind, ahead])
    return arrived


def table_kernel(pairs, valid, sizes, out):
    size_z, size_y, size_x, tiles = sizes
    z, y = lax.axis_index("z"), lax.axis_index("y")
    x, core = lax.axis_index("x"), lax.axis_index("core")
    slots = out.shape[1]
    arrival, keys = [], []
    for slot in range(slots):
        row, col, live = pairs[0, slot], pairs[1, slot], valid[0, slot] != 0
        behind = lax.rem(z - col // size_y + size_z, size_z)
        place = lax.rem(y - lax.rem(col, size_y) + size_y, size_y)
        upper = place >= size_y // 2
        far = jnp.where(upper, size_z, size_z - 1)
        source = jnp.where(behind < size_z // 2, 2 * behind - 1, 2 * (size_z - behind))
        source = jnp.where(behind == size_z // 2, far, source)
        source = jnp.where(behind == 0, 0, source)
        place = jnp.where((behind == size_z // 2) & upper, place - size_y // 2, place)
        crossing = ((z * size_y + y) * tiles + row) != (col * tiles + 2 * x + core)
        near = jnp.where(lax.rem(row, 2) == core, 0, size_x)
        near = near + lax.rem(x - row // 2 + size_x, size_x)
        out[ROW_AT, slot] = row
        out[ROW_NEAR, slot] = near
        out[COL_AT, slot] = col
        out[SOURCE, slot] = source
        out[PLACE, slot] = place
        out[LIVE, slot] = jnp.where(live, 1, 0)
        out[CROSSING, slot] = jnp.where(live & crossing, 1, 0)
        stage = jnp.where(live, (source + 1) // 2, LAST_STAGE)
        arrival.append(jnp.maximum(3 * stage - 1, 0))
        keys.append(stage * slots + slot)
    ranks = [
        sum(jnp.where(other <= key, 1, 0) for other in keys) for key in keys
    ]
    for slot in range(slots):
        turn = arrival[slot]
        for other in range(slots):
            if other != slot:
                wait = arrival[other] + ranks[slot] - ranks[other]
                turn = jnp.maximum(turn, jnp.where(keys[other] <= keys[slot], wait, 0))
        stage = jnp.minimum((turn + 1) // 3, LAST_STAGE)
        out[STAGE, slot] = jnp.where(valid[0, slot] != 0, stage, -1)


def slot_table(pairs, valid, sizes):
    smem = pl.BlockSpec(memory_space=pltpu.SMEM)

    def kernel(pairs_ref, valid_ref, out_ref):
        table_kernel(pairs_ref, valid_ref, sizes, out_ref)

    return pl.pallas_call(
        kernel,
        in_specs=[smem, smem],
        out_specs=smem,
        out_shape=jax.ShapeDtypeStruct((8, pairs.shape[1]), jnp.int32),
        name="slot_table",
    )(pairs, valid)


def combine(row_acc, col_acc):
    by_col = lax.all_to_all(col_acc, ROW, 0, 0, tiled=True)
    return reduce_near(row_acc) + jnp.sum(by_col, axis=0)


def per_device(positions, vectors, pairs, valid):
    grid_col = lax.axis_index(COL)
    block = positions.shape[2]
    tiles = block // TILE
    blocks = lax.axis_size(ROW)
    sizes = (lax.axis_size("z"), lax.axis_size("y"), lax.axis_size("x"), tiles)
    table = slot_table(pairs[0, 0].transpose(1, 0), valid[0], sizes)

    flat = positions.transpose(1, 0, 2).reshape(48, block)
    own = jnp.concatenate(
        [
            lax.dynamic_slice_in_dim(flat, grid_col * TILE, TILE, 1),
            lax.dynamic_slice_in_dim(vectors, grid_col * TILE, TILE, 1),
        ],
        axis=0,
    )
    row_vec = vectors.reshape(8, tiles, TILE).transpose(1, 0, 2)
    near = gather_y(own)
    prepared = prepare_rows(flat)
    places, state = [], []
    for stage, arrived in enumerate(gather_z(near)):
        places = places + arrived
        state = form_stage(stage, table, prepared, row_vec, places, state, blocks)
    high, low, slot_vec, col_acc = state
    row_acc = apply_tiles(LIVE, None, "apply_first", table, high, low, slot_vec, tiles)
    first = combine(row_acc, col_acc)

    col_vec = spread(first, ROW)
    col_acc = apply_tiles(CROSSING, COL_AT, "apply_cols", table, high, low, spread_near(first), blocks)
    row_acc = apply_tiles(LIVE, COL_AT, "apply_rows", table, high, low, col_vec, tiles)
    second = combine(row_acc, col_acc)

    rows = spread(second, COL)
    squares = jnp.sum(rows * rows, axis=(0, 2))
    squares = spread(jnp.pad(squares[None, :], ((0, 0), (0, 120))), ROW)
    total = jnp.sum(squares[:, 0, :8], axis=0) / (block * blocks)
    scaled = rows / jnp.sqrt(total + 1e-06)[None, :, None]
    return scaled.transpose(1, 0, 2).reshape(8, block)


def solution(mesh):
    physical = Mesh(mesh.devices.reshape(8, 4, 4, 2), ("z", "y", "x", "core"))
    placed = (
        P(None, None, ROW),
        P(None, ROW),
        P(ROW, COL, None, None),
        P(ROW, COL, None),
    )
    return jax.shard_map(
        per_device, mesh=physical, in_specs=placed, out_specs=P(None, ROW), check_vma=False
    )
```

```python
import functools
import math

import jax
import jax.numpy as jnp
from jax import lax
from jax.experimental import pallas as pl
from jax.experimental.pallas import tpu as pltpu
from jax.sharding import Mesh
from jax.sharding import PartitionSpec as P

TILE = 512
ROW = ("z", "y")
COL = ("x", "core")
ROW_AT, ROW_NEAR, COL_AT, SOURCE, PLACE, STAGE, LIVE, CROSSING, LATE = range(9)
LAST_STAGE = 4
BY_ROWS = (((1,), (0,)), ((), ()))
BY_COLS = (((1,), (1,)), ((), ()))
LOG2E = math.log2(math.e)
GROUPS = 6
DEPTH = 8 * GROUPS
HALF = 256


def in_hbm(value):
    return pltpu.with_memory_space_constraint(value, pltpu.HBM)


def split3(value):
    high = value.astype(jnp.bfloat16).astype(jnp.float32)
    rest = value - high
    mid = rest.astype(jnp.bfloat16).astype(jnp.float32)
    return high, mid, rest - mid


def rows_of(ref, snapshot, scale, norm_at, one_at):
    width = ref.shape[-1]
    place = lax.broadcasted_iota(jnp.int32, (8, width), 0)
    parts = [
        jnp.broadcast_to(ref[16 * q + snapshot : 16 * q + snapshot + 1, :], (8, width))
        for q in range(3)
    ]
    norm = (-0.5 * LOG2E) * (parts[0] * parts[0] + parts[1] * parts[1] + parts[2] * parts[2])
    out = jnp.where(place == norm_at, norm, jnp.where(place == one_at, 1.0, 0.0))
    for q in range(3):
        out = jnp.where(place == q, parts[q] * scale if scale != 1.0 else parts[q], out)
    return out


def prepare_kernel(pos_ref, out_ref):
    def visit(tile, carry):
        part = pos_ref.at[:, pl.ds(pl.multiple_of(tile * TILE, TILE), TILE)]
        for snapshot in range(16):
            high, mid, low = split3(rows_of(part, snapshot, LOG2E, 4, 3))
            stacked = jnp.concatenate([high, high, mid, mid, high, low], axis=0)
            out_ref[tile, snapshot] = stacked.T.astype(jnp.bfloat16)
        return carry

    lax.fori_loop(0, out_ref.shape[0], visit, 0)


def prepare_rows(pos):
    tiles = pos.shape[1] // TILE
    vmem = pl.BlockSpec(memory_space=pltpu.VMEM)
    return pl.pallas_call(
        prepare_kernel,
        in_specs=[vmem],
        out_specs=vmem,
        out_shape=jax.ShapeDtypeStruct((tiles, 16, TILE, DEPTH), jnp.bfloat16),
        compiler_params=pltpu.CompilerParams(vmem_limit_bytes=4 << 20),
        cost_estimate=pl.CostEstimate(flops=10**8, bytes_accessed=8 << 20, transcendentals=0),
        name="prepare_rows",
    )(pos)


def multiply(field, high, low, dims):
    terms = jnp.concatenate(split3(field), axis=0).astype(jnp.bfloat16)
    dot = functools.partial(
        lax.dot_general, dimension_numbers=dims, preferred_element_type=jnp.float32
    )
    by_high = dot(terms, high)
    by_low = dot(terms[:16], low)
    return (by_high[0:8] + by_low[0:8]) + (by_high[8:16] + by_low[8:16]) + by_high[16:24]


def stage_kernel(stage, sources, table, prepared_ref, row_vec, *refs):
    places = refs[:sources]
    last = stage == LAST_STAGE
    high_ref, low_ref, rows_out, col_acc, tile, cols, high_tile, low_tile, sems = refs[-9:]
    if stage == 0:
        rows_out[...] = jnp.zeros_like(rows_out)
        col_acc[...] = jnp.zeros_like(col_acc)
    else:
        if not last:
            rows_out[...] = refs[sources + 2][...]
        col_acc[...] = refs[sources + 3][...]

    def copies(slot, buffer):
        return [
            pltpu.make_async_copy(high_tile.at[buffer], high_ref.at[slot], sems.at[0, buffer]),
            pltpu.make_async_copy(low_tile.at[buffer], low_ref.at[slot], sems.at[1, buffer]),
        ]

    def form(slot, formed):
        buffer = lax.rem(formed, 2)
        for source in range(sources):

            @pl.when(table[SOURCE, slot] == source)
            def _():
                tile[...] = places[source][table[PLACE, slot]]

        for snapshot in range(16):
            high, mid, low = split3(rows_of(tile, snapshot, 1.0, 3, 4))
            stacked = jnp.concatenate([high, mid, high, mid, low, high], axis=0)
            cols[snapshot] = stacked.astype(jnp.bfloat16)
        row_at = table[ROW_AT, slot]

        @pl.when(formed >= 2)
        def _():
            for copy in copies(slot, buffer):
                copy.wait()

        def step(at, carry):
            part = pl.ds(pl.multiple_of(at * HALF, HALF), HALF)
            total = None
            for snapshot in range(16):
                exponent = jnp.dot(
                    prepared_ref[row_at, snapshot],
                    cols[snapshot, :, part],
                    preferred_element_type=jnp.float32,
                )
                term = jnp.exp2(exponent)
                total = term if total is None else total + term
            high = total.astype(jnp.bfloat16)
            high_tile[buffer, :, part] = high
            low_tile[buffer, :, part] = (total - high.astype(jnp.float32)).astype(jnp.bfloat16)
            return carry

        lax.fori_loop(0, TILE // HALF, step, 0)
        for copy in copies(slot, buffer):
            copy.start()
        if last:
            rows_out[slot] = tile[48:56, :]
        else:
            rows_out[table[ROW_NEAR, slot]] += multiply(
                tile[48:56, :], high_tile[buffer], low_tile[buffer], BY_COLS
            )

        @pl.when(table[CROSSING, slot] != 0)
        def _():
            col_acc[table[COL_AT, slot]] += multiply(
                row_vec[row_at], high_tile[buffer], low_tile[buffer], BY_ROWS
            )

    def visit(slot, formed):
        mine = table[STAGE, slot] == stage

        @pl.when(mine)
        def _():
            form(slot, formed)

        return formed + jnp.where(mine, 1, 0)

    formed = lax.fori_loop(0, high_ref.shape[0], visit, 0)
    for back in (1, 2):

        @pl.when(formed >= back)
        def _():
            for copy in copies(0, lax.rem(formed + back, 2)):
                copy.wait()


def form_stage(stage, table, prepared, row_vec, places, state, blocks):
    slots = table.shape[1]
    vmem = pl.BlockSpec(memory_space=pltpu.VMEM)
    hbm = pl.BlockSpec(memory_space=pltpu.HBM)
    shapes = [
        pltpu.HBM((slots, TILE, TILE), jnp.bfloat16),
        pltpu.HBM((slots, TILE, TILE), jnp.bfloat16),
        jax.ShapeDtypeStruct(
            (slots if stage == LAST_STAGE else row_vec.shape[0], 8, TILE), jnp.float32
        ),
        jax.ShapeDtypeStruct((blocks, 8, TILE), jnp.float32),
    ]
    first = 3 + len(places)
    return pl.pallas_call(
        functools.partial(stage_kernel, stage, len(places)),
        in_specs=[pl.BlockSpec(memory_space=pltpu.SMEM)]
        + [vmem] * (2 + len(places))
        + ([hbm, hbm, vmem, vmem] if state else []),
        out_specs=[hbm, hbm, vmem, vmem],
        out_shape=shapes,
        input_output_aliases={
            first + i: i for i in range(2 if stage == LAST_STAGE else len(state))
        },
        scratch_shapes=[
            pltpu.VMEM((56, TILE), jnp.float32),
            pltpu.VMEM((16, DEPTH, TILE), jnp.bfloat16),
            pltpu.VMEM((2, TILE, TILE), jnp.bfloat16),
            pltpu.VMEM((2, TILE, TILE), jnp.bfloat16),
            pltpu.SemaphoreType.DMA((2, 2)),
        ],
        compiler_params=pltpu.CompilerParams(vmem_limit_bytes=8 << 20),
        cost_estimate=pl.CostEstimate(
            flops=8 * 10**9, bytes_accessed=8 << 20, transcendentals=10**7
        ),
        name=f"form_{stage}",
    )(table, prepared, row_vec, *places, *state)


def apply_kernel(wanted, col_at, table, high_ref, low_ref, field, *refs):
    acc, high, low, sems = refs[-4:]
    slots = high_ref.shape[0]

    def copies(slot):
        return [
            pltpu.make_async_copy(high_ref.at[slot], high.at[slot], sems.at[0, slot]),
            pltpu.make_async_copy(low_ref.at[slot], low.at[slot], sems.at[1, slot]),
        ]

    for slot in range(slots):

        @pl.when(table[wanted, slot] != 0)
        def _():
            for copy in copies(slot):
                copy.start()

    acc[...] = jnp.zeros_like(acc) if len(refs) == 4 else refs[0][...]

    def visit(slot, carry):
        @pl.when(table[wanted, slot] != 0)
        def _():
            for copy in copies(slot):
                copy.wait()
            row = table[ROW_NEAR, slot]
            col = slot if col_at is None else table[col_at, slot]
            if wanted != CROSSING:
                acc[row] += multiply(field[col], high[slot], low[slot], BY_COLS)
            else:
                acc[col] += multiply(field[row], high[slot], low[slot], BY_ROWS)

        return carry

    lax.fori_loop(0, slots, visit, 0)


def apply_tiles(wanted, col_at, name, table, high, low, field, count, start=()):
    vmem = pl.BlockSpec(memory_space=pltpu.VMEM)
    hbm = pl.BlockSpec(memory_space=pltpu.HBM)
    return pl.pallas_call(
        functools.partial(apply_kernel, wanted, col_at),
        in_specs=[pl.BlockSpec(memory_space=pltpu.SMEM), hbm, hbm, vmem] + [vmem] * len(start),
        out_specs=vmem,
        out_shape=jax.ShapeDtypeStruct((count, 8, TILE), jnp.float32),
        scratch_shapes=[
            pltpu.VMEM(high.shape, high.dtype),
            pltpu.VMEM(low.shape, low.dtype),
            pltpu.SemaphoreType.DMA((2, high.shape[0])),
        ],
        compiler_params=pltpu.CompilerParams(vmem_limit_bytes=16 << 20),
        cost_estimate=pl.CostEstimate(
            flops=3 * 10**9, bytes_accessed=12 << 20, transcendentals=0
        ),
        name=name,
    )(table, in_hbm(high), in_hbm(low), field, *start)


def shift(value, axis, distance):
    size = lax.axis_size(axis)
    return lax.ppermute(value, axis, [(i, (i + distance) % size) for i in range(size)])


def spread(piece, axes):
    copies = jnp.broadcast_to(piece, (lax.axis_size(axes),) + piece.shape)
    return lax.all_to_all(copies, axes, 0, 0, tiled=True)


def spread_near(piece):
    mine = jnp.stack([piece] + [shift(piece, "x", d) for d in range(1, lax.axis_size("x"))])
    return jnp.concatenate([mine, shift(mine, "core", 1)], axis=0)


def reduce_near(row_acc):
    size = lax.axis_size("x")
    mine = row_acc[:size] + shift(row_acc[size:], "core", 1)
    total = mine[0]
    for d in range(1, size):
        total = total + shift(mine[d], "x", size - d)
    return total


def gather_y(piece):
    return jnp.stack([piece] + [shift(piece, "y", d) for d in range(1, lax.axis_size("y"))])


def gather_z(near):
    size, half = lax.axis_size("z"), near.shape[0] // 2
    arrived = [[near]]
    behind = ahead = near
    for distance in range(1, size // 2 + 1):
        if distance == size // 2:
            behind, ahead = behind[:half], ahead[half:]
        behind, ahead = shift(behind, "z", 1), shift(ahead, "z", size - 1)
        arrived.append([behind, ahead])
    return arrived


def table_kernel(pairs, valid, sizes, out):
    size_z, size_y, size_x, tiles = sizes
    z, y = lax.axis_index("z"), lax.axis_index("y")
    x, core = lax.axis_index("x"), lax.axis_index("core")
    slots = out.shape[1]
    arrival, keys = [], []
    for slot in range(slots):
        row, col, live = pairs[0, slot], pairs[1, slot], valid[0, slot] != 0
        behind = lax.rem(z - col // size_y + size_z, size_z)
        place = lax.rem(y - lax.rem(col, size_y) + size_y, size_y)
        upper = place >= size_y // 2
        far = jnp.where(upper, size_z, size_z - 1)
        source = jnp.where(behind < size_z // 2, 2 * behind - 1, 2 * (size_z - behind))
        source = jnp.where(behind == size_z // 2, far, source)
        source = jnp.where(behind == 0, 0, source)
        place = jnp.where((behind == size_z // 2) & upper, place - size_y // 2, place)
        crossing = ((z * size_y + y) * tiles + row) != (col * tiles + 2 * x + core)
        near = jnp.where(lax.rem(row, 2) == core, 0, size_x)
        near = near + lax.rem(x - row // 2 + size_x, size_x)
        out[ROW_AT, slot] = row
        out[ROW_NEAR, slot] = near
        out[COL_AT, slot] = col
        out[SOURCE, slot] = source
        out[PLACE, slot] = place
        out[LIVE, slot] = jnp.where(live, 1, 0)
        out[CROSSING, slot] = jnp.where(live & crossing, 1, 0)
        stage = jnp.where(live, (source + 1) // 2, LAST_STAGE)
        arrival.append(jnp.maximum(3 * stage - 1, 0))
        keys.append(stage * slots + slot)
    ranks = [
        sum(jnp.where(other <= key, 1, 0) for other in keys) for key in keys
    ]
    for slot in range(slots):
        turn = arrival[slot]
        for other in range(slots):
            if other != slot:
                wait = arrival[other] + ranks[slot] - ranks[other]
                turn = jnp.maximum(turn, jnp.where(keys[other] <= keys[slot], wait, 0))
        stage = jnp.minimum((turn + 1) // 3, LAST_STAGE)
        live = valid[0, slot] != 0
        out[STAGE, slot] = jnp.where(live, stage, -1)
        out[LATE, slot] = jnp.where(live & (stage == LAST_STAGE), 1, 0)


def slot_table(pairs, valid, sizes):
    smem = pl.BlockSpec(memory_space=pltpu.SMEM)

    def kernel(pairs_ref, valid_ref, out_ref):
        table_kernel(pairs_ref, valid_ref, sizes, out_ref)

    return pl.pallas_call(
        kernel,
        in_specs=[smem, smem],
        out_specs=smem,
        out_shape=jax.ShapeDtypeStruct((9, pairs.shape[1]), jnp.int32),
        name="slot_table",
    )(pairs, valid)


def combine(row_acc, col_acc):
    by_col = lax.all_to_all(col_acc, ROW, 0, 0, tiled=True)
    return reduce_near(row_acc) + jnp.sum(by_col, axis=0)


def per_device(positions, vectors, pairs, valid):
    grid_col = lax.axis_index(COL)
    block = positions.shape[2]
    tiles = block // TILE
    blocks = lax.axis_size(ROW)
    sizes = (lax.axis_size("z"), lax.axis_size("y"), lax.axis_size("x"), tiles)
    table = slot_table(pairs[0, 0].transpose(1, 0), valid[0], sizes)

    flat = positions.transpose(1, 0, 2).reshape(48, block)
    own = jnp.concatenate(
        [
            lax.dynamic_slice_in_dim(flat, grid_col * TILE, TILE, 1),
            lax.dynamic_slice_in_dim(vectors, grid_col * TILE, TILE, 1),
        ],
        axis=0,
    )
    row_vec = vectors.reshape(8, tiles, TILE).transpose(1, 0, 2)
    near = gather_y(own)
    prepared = prepare_rows(flat)
    places, state = [], []
    for stage, arrived in enumerate(gather_z(near)):
        places = places + arrived
        early = state
        state = form_stage(stage, table, prepared, row_vec, places, state, blocks)
    high, low, slot_vec, col_acc = state
    row_acc = apply_tiles(
        LATE, None, "apply_late", table, high, low, slot_vec, tiles, (early[2],)
    )
    first = combine(row_acc, col_acc)

    col_vec = spread(first, ROW)
    col_acc = apply_tiles(CROSSING, COL_AT, "apply_cols", table, high, low, spread_near(first), blocks)
    row_acc = apply_tiles(LIVE, COL_AT, "apply_rows", table, high, low, col_vec, tiles)
    second = combine(row_acc, col_acc)

    rows = spread(second, COL)
    squares = jnp.sum(rows * rows, axis=(0, 2))
    squares = spread(jnp.pad(squares[None, :], ((0, 0), (0, 120))), ROW)
    total = jnp.sum(squares[:, 0, :8], axis=0) / (block * blocks)
    scaled = rows / jnp.sqrt(total + 1e-06)[None, :, None]
    return scaled.transpose(1, 0, 2).reshape(8, block)


def solution(mesh):
    physical = Mesh(mesh.devices.reshape(8, 4, 4, 2), ("z", "y", "x", "core"))
    placed = (
        P(None, None, ROW),
        P(None, ROW),
        P(ROW, COL, None, None),
        P(ROW, COL, None),
    )
    return jax.shard_map(
        per_device, mesh=physical, in_specs=placed, out_specs=P(None, ROW), check_vma=False
    )
```

```python
import functools
import math

import jax
import jax.numpy as jnp
from jax import lax
from jax.experimental import pallas as pl
from jax.experimental.pallas import tpu as pltpu
from jax.sharding import Mesh
from jax.sharding import PartitionSpec as P

TILE = 512
ROW = ("z", "y")
COL = ("x", "core")
ROW_AT, ROW_NEAR, COL_AT, SOURCE, PLACE, STAGE, LIVE, CROSSING, LATE = range(9)
LAST_STAGE = 4
PER_STAGE = 2
BY_ROWS = (((1,), (0,)), ((), ()))
BY_COLS = (((1,), (1,)), ((), ()))
LOG2E = math.log2(math.e)
GROUPS = 6
DEPTH = 8 * GROUPS
HALF = 256


def in_hbm(value):
    return pltpu.with_memory_space_constraint(value, pltpu.HBM)


def split3(value):
    high = value.astype(jnp.bfloat16).astype(jnp.float32)
    rest = value - high
    mid = rest.astype(jnp.bfloat16).astype(jnp.float32)
    return high, mid, rest - mid


def rows_of(ref, snapshot, scale, norm_at, one_at):
    width = ref.shape[-1]
    place = lax.broadcasted_iota(jnp.int32, (8, width), 0)
    parts = [
        jnp.broadcast_to(ref[16 * q + snapshot : 16 * q + snapshot + 1, :], (8, width))
        for q in range(3)
    ]
    norm = (-0.5 * LOG2E) * (parts[0] * parts[0] + parts[1] * parts[1] + parts[2] * parts[2])
    out = jnp.where(place == norm_at, norm, jnp.where(place == one_at, 1.0, 0.0))
    for q in range(3):
        out = jnp.where(place == q, parts[q] * scale if scale != 1.0 else parts[q], out)
    return out


def prepare_kernel(pos_ref, out_ref):
    def visit(tile, carry):
        part = pos_ref.at[:, pl.ds(pl.multiple_of(tile * TILE, TILE), TILE)]
        for snapshot in range(16):
            high, mid, low = split3(rows_of(part, snapshot, LOG2E, 4, 3))
            stacked = jnp.concatenate([high, high, mid, mid, high, low], axis=0)
            out_ref[tile, snapshot] = stacked.T.astype(jnp.bfloat16)
        return carry

    lax.fori_loop(0, out_ref.shape[0], visit, 0)


def prepare_rows(pos):
    tiles = pos.shape[1] // TILE
    vmem = pl.BlockSpec(memory_space=pltpu.VMEM)
    return pl.pallas_call(
        prepare_kernel,
        in_specs=[vmem],
        out_specs=vmem,
        out_shape=jax.ShapeDtypeStruct((tiles, 16, TILE, DEPTH), jnp.bfloat16),
        compiler_params=pltpu.CompilerParams(vmem_limit_bytes=4 << 20),
        cost_estimate=pl.CostEstimate(flops=10**8, bytes_accessed=8 << 20, transcendentals=0),
        name="prepare_rows",
    )(pos)


def multiply(field, high, low, dims):
    terms = jnp.concatenate(split3(field), axis=0).astype(jnp.bfloat16)
    dot = functools.partial(
        lax.dot_general, dimension_numbers=dims, preferred_element_type=jnp.float32
    )
    by_high = dot(terms, high)
    by_low = dot(terms[:16], low)
    return (by_high[0:8] + by_low[0:8]) + (by_high[8:16] + by_low[8:16]) + by_high[16:24]


def stage_kernel(stage, sources, table, prepared_ref, row_vec, *refs):
    places = refs[:sources]
    last = stage == LAST_STAGE
    high_ref, low_ref, rows_out, col_acc, tile, cols, high_tile, low_tile, sems = refs[-9:]
    if stage == 0:
        rows_out[...] = jnp.zeros_like(rows_out)
        col_acc[...] = jnp.zeros_like(col_acc)
    else:
        if not last:
            rows_out[...] = refs[sources + 2][...]
        col_acc[...] = refs[sources + 3][...]

    def copies(slot, buffer):
        return [
            pltpu.make_async_copy(high_tile.at[buffer], high_ref.at[slot], sems.at[0, buffer]),
            pltpu.make_async_copy(low_tile.at[buffer], low_ref.at[slot], sems.at[1, buffer]),
        ]

    def form(slot, formed):
        buffer = lax.rem(formed, 2)
        for source in range(sources):

            @pl.when(table[SOURCE, slot] == source)
            def _():
                tile[...] = places[source][table[PLACE, slot]]

        for snapshot in range(16):
            high, mid, low = split3(rows_of(tile, snapshot, 1.0, 3, 4))
            stacked = jnp.concatenate([high, mid, high, mid, low, high], axis=0)
            cols[snapshot] = stacked.astype(jnp.bfloat16)
        row_at = table[ROW_AT, slot]

        @pl.when(formed >= 2)
        def _():
            for copy in copies(slot, buffer):
                copy.wait()

        def step(at, carry):
            part = pl.ds(pl.multiple_of(at * HALF, HALF), HALF)
            total = None
            for snapshot in range(16):
                exponent = jnp.dot(
                    prepared_ref[row_at, snapshot],
                    cols[snapshot, :, part],
                    preferred_element_type=jnp.float32,
                )
                term = jnp.exp2(exponent)
                total = term if total is None else total + term
            high = total.astype(jnp.bfloat16)
            high_tile[buffer, :, part] = high
            low_tile[buffer, :, part] = (total - high.astype(jnp.float32)).astype(jnp.bfloat16)
            return carry

        lax.fori_loop(0, TILE // HALF, step, 0)
        for copy in copies(slot, buffer):
            copy.start()
        if last:
            rows_out[slot] = tile[48:56, :]
        else:
            rows_out[table[ROW_NEAR, slot]] += multiply(
                tile[48:56, :], high_tile[buffer], low_tile[buffer], BY_COLS
            )

        @pl.when(table[CROSSING, slot] != 0)
        def _():
            col_acc[table[COL_AT, slot]] += multiply(
                row_vec[row_at], high_tile[buffer], low_tile[buffer], BY_ROWS
            )

    def visit(slot, formed):
        mine = table[STAGE, slot] == stage

        @pl.when(mine)
        def _():
            form(slot, formed)

        return formed + jnp.where(mine, 1, 0)

    formed = lax.fori_loop(0, high_ref.shape[0], visit, 0)
    for back in (1, 2):

        @pl.when(formed >= back)
        def _():
            for copy in copies(0, lax.rem(formed + back, 2)):
                copy.wait()


def form_stage(stage, table, prepared, row_vec, places, state, blocks):
    slots = table.shape[1]
    vmem = pl.BlockSpec(memory_space=pltpu.VMEM)
    hbm = pl.BlockSpec(memory_space=pltpu.HBM)
    shapes = [
        pltpu.HBM((slots, TILE, TILE), jnp.bfloat16),
        pltpu.HBM((slots, TILE, TILE), jnp.bfloat16),
        jax.ShapeDtypeStruct(
            (slots if stage == LAST_STAGE else row_vec.shape[0], 8, TILE), jnp.float32
        ),
        jax.ShapeDtypeStruct((blocks, 8, TILE), jnp.float32),
    ]
    first = 3 + len(places)
    return pl.pallas_call(
        functools.partial(stage_kernel, stage, len(places)),
        in_specs=[pl.BlockSpec(memory_space=pltpu.SMEM)]
        + [vmem] * (2 + len(places))
        + ([hbm, hbm, vmem, vmem] if state else []),
        out_specs=[hbm, hbm, vmem, vmem],
        out_shape=shapes,
        input_output_aliases={
            first + i: i for i in range(2 if stage == LAST_STAGE else len(state))
        },
        scratch_shapes=[
            pltpu.VMEM((56, TILE), jnp.float32),
            pltpu.VMEM((16, DEPTH, TILE), jnp.bfloat16),
            pltpu.VMEM((2, TILE, TILE), jnp.bfloat16),
            pltpu.VMEM((2, TILE, TILE), jnp.bfloat16),
            pltpu.SemaphoreType.DMA((2, 2)),
        ],
        compiler_params=pltpu.CompilerParams(vmem_limit_bytes=8 << 20),
        cost_estimate=pl.CostEstimate(
            flops=8 * 10**9, bytes_accessed=8 << 20, transcendentals=10**7
        ),
        name=f"form_{stage}",
    )(table, prepared, row_vec, *places, *state)


def apply_kernel(wanted, col_at, table, high_ref, low_ref, field, *refs):
    acc, high, low, sems = refs[-4:]
    slots = high_ref.shape[0]

    def copies(slot):
        return [
            pltpu.make_async_copy(high_ref.at[slot], high.at[slot], sems.at[0, slot]),
            pltpu.make_async_copy(low_ref.at[slot], low.at[slot], sems.at[1, slot]),
        ]

    for slot in range(slots):

        @pl.when(table[wanted, slot] != 0)
        def _():
            for copy in copies(slot):
                copy.start()

    acc[...] = jnp.zeros_like(acc) if len(refs) == 4 else refs[0][...]

    def visit(slot, carry):
        @pl.when(table[wanted, slot] != 0)
        def _():
            for copy in copies(slot):
                copy.wait()
            row = table[ROW_NEAR, slot]
            col = slot if col_at is None else table[col_at, slot]
            if wanted != CROSSING:
                acc[row] += multiply(field[col], high[slot], low[slot], BY_COLS)
            else:
                acc[col] += multiply(field[row], high[slot], low[slot], BY_ROWS)

        return carry

    lax.fori_loop(0, slots, visit, 0)


def apply_tiles(wanted, col_at, name, table, high, low, field, count, start=()):
    vmem = pl.BlockSpec(memory_space=pltpu.VMEM)
    hbm = pl.BlockSpec(memory_space=pltpu.HBM)
    return pl.pallas_call(
        functools.partial(apply_kernel, wanted, col_at),
        in_specs=[pl.BlockSpec(memory_space=pltpu.SMEM), hbm, hbm, vmem] + [vmem] * len(start),
        out_specs=vmem,
        out_shape=jax.ShapeDtypeStruct((count, 8, TILE), jnp.float32),
        scratch_shapes=[
            pltpu.VMEM(high.shape, high.dtype),
            pltpu.VMEM(low.shape, low.dtype),
            pltpu.SemaphoreType.DMA((2, high.shape[0])),
        ],
        compiler_params=pltpu.CompilerParams(vmem_limit_bytes=16 << 20),
        cost_estimate=pl.CostEstimate(
            flops=3 * 10**9, bytes_accessed=12 << 20, transcendentals=0
        ),
        name=name,
    )(table, in_hbm(high), in_hbm(low), field, *start)


def shift(value, axis, distance):
    size = lax.axis_size(axis)
    return lax.ppermute(value, axis, [(i, (i + distance) % size) for i in range(size)])


def spread(piece, axes):
    copies = jnp.broadcast_to(piece, (lax.axis_size(axes),) + piece.shape)
    return lax.all_to_all(copies, axes, 0, 0, tiled=True)


def spread_near(piece):
    mine = jnp.stack([piece] + [shift(piece, "x", d) for d in range(1, lax.axis_size("x"))])
    return jnp.concatenate([mine, shift(mine, "core", 1)], axis=0)


def reduce_near(row_acc):
    size = lax.axis_size("x")
    mine = row_acc[:size] + shift(row_acc[size:], "core", 1)
    total = mine[0]
    for d in range(1, size):
        total = total + shift(mine[d], "x", size - d)
    return total


def gather_y(piece):
    return jnp.stack([piece] + [shift(piece, "y", d) for d in range(1, lax.axis_size("y"))])


def gather_z(near):
    size, half = lax.axis_size("z"), near.shape[0] // 2
    arrived = [[near]]
    behind = ahead = near
    for distance in range(1, size // 2 + 1):
        if distance == size // 2:
            behind, ahead = behind[:half], ahead[half:]
        behind, ahead = shift(behind, "z", 1), shift(ahead, "z", size - 1)
        arrived.append([behind, ahead])
    return arrived


def table_kernel(pairs, valid, sizes, out):
    size_z, size_y, size_x, tiles = sizes
    z, y = lax.axis_index("z"), lax.axis_index("y")
    x, core = lax.axis_index("x"), lax.axis_index("core")
    slots = out.shape[1]
    arrival, keys = [], []
    for slot in range(slots):
        row, col, live = pairs[0, slot], pairs[1, slot], valid[0, slot] != 0
        behind = lax.rem(z - col // size_y + size_z, size_z)
        place = lax.rem(y - lax.rem(col, size_y) + size_y, size_y)
        upper = place >= size_y // 2
        far = jnp.where(upper, size_z, size_z - 1)
        source = jnp.where(behind < size_z // 2, 2 * behind - 1, 2 * (size_z - behind))
        source = jnp.where(behind == size_z // 2, far, source)
        source = jnp.where(behind == 0, 0, source)
        place = jnp.where((behind == size_z // 2) & upper, place - size_y // 2, place)
        crossing = ((z * size_y + y) * tiles + row) != (col * tiles + 2 * x + core)
        near = jnp.where(lax.rem(row, 2) == core, 0, size_x)
        near = near + lax.rem(x - row // 2 + size_x, size_x)
        out[ROW_AT, slot] = row
        out[ROW_NEAR, slot] = near
        out[COL_AT, slot] = col
        out[SOURCE, slot] = source
        out[PLACE, slot] = place
        out[LIVE, slot] = jnp.where(live, 1, 0)
        out[CROSSING, slot] = jnp.where(live & crossing, 1, 0)
        stage = jnp.where(live, (source + 1) // 2, LAST_STAGE)
        arrival.append(PER_STAGE * stage)
        keys.append(stage * slots + slot)
    ranks = [
        sum(jnp.where(other <= key, 1, 0) for other in keys) for key in keys
    ]
    for slot in range(slots):
        turn = arrival[slot]
        for other in range(slots):
            if other != slot:
                wait = arrival[other] + ranks[slot] - ranks[other]
                turn = jnp.maximum(turn, jnp.where(keys[other] <= keys[slot], wait, 0))
        stage = jnp.minimum(turn // PER_STAGE, LAST_STAGE)
        live = valid[0, slot] != 0
        out[STAGE, slot] = jnp.where(live, stage, -1)
        out[LATE, slot] = jnp.where(live & (stage == LAST_STAGE), 1, 0)


def slot_table(pairs, valid, sizes):
    smem = pl.BlockSpec(memory_space=pltpu.SMEM)

    def kernel(pairs_ref, valid_ref, out_ref):
        table_kernel(pairs_ref, valid_ref, sizes, out_ref)

    return pl.pallas_call(
        kernel,
        in_specs=[smem, smem],
        out_specs=smem,
        out_shape=jax.ShapeDtypeStruct((9, pairs.shape[1]), jnp.int32),
        name="slot_table",
    )(pairs, valid)


def combine(row_acc, col_acc):
    by_col = lax.all_to_all(col_acc, ROW, 0, 0, tiled=True)
    return reduce_near(row_acc) + jnp.sum(by_col, axis=0)


def per_device(positions, vectors, pairs, valid):
    grid_col = lax.axis_index(COL)
    block = positions.shape[2]
    tiles = block // TILE
    blocks = lax.axis_size(ROW)
    sizes = (lax.axis_size("z"), lax.axis_size("y"), lax.axis_size("x"), tiles)
    table = slot_table(pairs[0, 0].transpose(1, 0), valid[0], sizes)

    flat = positions.transpose(1, 0, 2).reshape(48, block)
    own = jnp.concatenate(
        [
            lax.dynamic_slice_in_dim(flat, grid_col * TILE, TILE, 1),
            lax.dynamic_slice_in_dim(vectors, grid_col * TILE, TILE, 1),
        ],
        axis=0,
    )
    row_vec = vectors.reshape(8, tiles, TILE).transpose(1, 0, 2)
    near = gather_y(own)
    prepared = prepare_rows(flat)
    places, state = [], []
    for stage, arrived in enumerate(gather_z(near)):
        places = places + arrived
        early = state
        state = form_stage(stage, table, prepared, row_vec, places, state, blocks)
    high, low, slot_vec, col_acc = state
    row_acc = apply_tiles(
        LATE, None, "apply_late", table, high, low, slot_vec, tiles, (early[2],)
    )
    first = combine(row_acc, col_acc)

    col_vec = spread(first, ROW)
    col_acc = apply_tiles(CROSSING, COL_AT, "apply_cols", table, high, low, spread_near(first), blocks)
    row_acc = apply_tiles(LIVE, COL_AT, "apply_rows", table, high, low, col_vec, tiles)
    second = combine(row_acc, col_acc)

    rows = spread(second, COL)
    squares = jnp.sum(rows * rows, axis=(0, 2))
    squares = spread(jnp.pad(squares[None, :], ((0, 0), (0, 120))), ROW)
    total = jnp.sum(squares[:, 0, :8], axis=0) / (block * blocks)
    scaled = rows / jnp.sqrt(total + 1e-06)[None, :, None]
    return scaled.transpose(1, 0, 2).reshape(8, block)


def solution(mesh):
    physical = Mesh(mesh.devices.reshape(8, 4, 4, 2), ("z", "y", "x", "core"))
    placed = (
        P(None, None, ROW),
        P(None, ROW),
        P(ROW, COL, None, None),
        P(ROW, COL, None),
    )
    return jax.shard_map(
        per_device, mesh=physical, in_specs=placed, out_specs=P(None, ROW), check_vma=False
    )
```

```python
import functools
import math

import jax
import jax.numpy as jnp
from jax import lax
from jax.experimental import pallas as pl
from jax.experimental.pallas import tpu as pltpu
from jax.sharding import Mesh
from jax.sharding import PartitionSpec as P

TILE = 512
ROW = ("z", "y")
COL = ("x", "core")
ROW_AT, ROW_NEAR, COL_AT, SOURCE, PLACE, STAGE, LIVE, CROSSING, LATE = range(9)
LAST_STAGE = 4
PER_STAGE = 2
BY_ROWS = (((1,), (0,)), ((), ()))
BY_COLS = (((1,), (1,)), ((), ()))
LOG2E = math.log2(math.e)
GROUPS = 6
DEPTH = 8 * GROUPS
HALF = 256


def in_hbm(value):
    return pltpu.with_memory_space_constraint(value, pltpu.HBM)


def split3(value):
    high = value.astype(jnp.bfloat16).astype(jnp.float32)
    rest = value - high
    mid = rest.astype(jnp.bfloat16).astype(jnp.float32)
    return high, mid, rest - mid


def rows_of(ref, snapshot, scale, norm_at, one_at):
    width = ref.shape[-1]
    place = lax.broadcasted_iota(jnp.int32, (8, width), 0)
    parts = [
        jnp.broadcast_to(ref[16 * q + snapshot : 16 * q + snapshot + 1, :], (8, width))
        for q in range(3)
    ]
    norm = (-0.5 * LOG2E) * (parts[0] * parts[0] + parts[1] * parts[1] + parts[2] * parts[2])
    out = jnp.where(place == norm_at, norm, jnp.where(place == one_at, 1.0, 0.0))
    for q in range(3):
        out = jnp.where(place == q, parts[q] * scale if scale != 1.0 else parts[q], out)
    return out


def prepare_kernel(pos_ref, out_ref):
    def visit(tile, carry):
        part = pos_ref.at[:, pl.ds(pl.multiple_of(tile * TILE, TILE), TILE)]
        for snapshot in range(16):
            high, mid, low = split3(rows_of(part, snapshot, LOG2E, 4, 3))
            stacked = jnp.concatenate([high, high, mid, mid, high, low], axis=0)
            out_ref[tile, snapshot] = stacked.T.astype(jnp.bfloat16)
        return carry

    lax.fori_loop(0, out_ref.shape[0], visit, 0)


def prepare_rows(pos):
    tiles = pos.shape[1] // TILE
    vmem = pl.BlockSpec(memory_space=pltpu.VMEM)
    return pl.pallas_call(
        prepare_kernel,
        in_specs=[vmem],
        out_specs=vmem,
        out_shape=jax.ShapeDtypeStruct((tiles, 16, TILE, DEPTH), jnp.bfloat16),
        compiler_params=pltpu.CompilerParams(vmem_limit_bytes=4 << 20),
        cost_estimate=pl.CostEstimate(flops=10**8, bytes_accessed=8 << 20, transcendentals=0),
        name="prepare_rows",
    )(pos)


def multiply(field, high, low, dims):
    terms = jnp.concatenate(split3(field), axis=0).astype(jnp.bfloat16)
    dot = functools.partial(
        lax.dot_general, dimension_numbers=dims, preferred_element_type=jnp.float32
    )
    by_high = dot(terms, high)
    by_low = dot(terms[:16], low)
    return (by_high[0:8] + by_low[0:8]) + (by_high[8:16] + by_low[8:16]) + by_high[16:24]


def stage_kernel(stage, sources, table, prepared_ref, row_vec, *refs):
    places = refs[:sources]
    last = stage == LAST_STAGE
    high_ref, low_ref, rows_out, col_acc, tile, cols, high_tile, low_tile, sems = refs[-9:]
    if stage == 0:
        rows_out[...] = jnp.zeros_like(rows_out)
        col_acc[...] = jnp.zeros_like(col_acc)
    else:
        if not last:
            rows_out[...] = refs[sources + 2][...]
        col_acc[...] = refs[sources + 3][...]

    def copies(slot, buffer):
        return [
            pltpu.make_async_copy(high_tile.at[buffer], high_ref.at[slot], sems.at[0, buffer]),
            pltpu.make_async_copy(low_tile.at[buffer], low_ref.at[slot], sems.at[1, buffer]),
        ]

    def form(slot, formed):
        buffer = lax.rem(formed, 2)
        for source in range(sources):

            @pl.when(table[SOURCE, slot] == source)
            def _():
                tile[...] = places[source][table[PLACE, slot]]

        for snapshot in range(16):
            high, mid, low = split3(rows_of(tile, snapshot, 1.0, 3, 4))
            stacked = jnp.concatenate([high, mid, high, mid, low, high], axis=0)
            cols[snapshot] = stacked.astype(jnp.bfloat16)
        row_at = table[ROW_AT, slot]

        @pl.when(formed >= 2)
        def _():
            for copy in copies(slot, buffer):
                copy.wait()

        def step(at, carry):
            part = pl.ds(pl.multiple_of(at * HALF, HALF), HALF)
            total = None
            for snapshot in range(16):
                exponent = jnp.dot(
                    prepared_ref[row_at, snapshot],
                    cols[snapshot, :, part],
                    preferred_element_type=jnp.float32,
                )
                term = jnp.exp2(exponent)
                total = term if total is None else total + term
            high = total.astype(jnp.bfloat16)
            high_tile[buffer, :, part] = high
            low_tile[buffer, :, part] = (total - high.astype(jnp.float32)).astype(jnp.bfloat16)
            return carry

        lax.fori_loop(0, TILE // HALF, step, 0)
        for copy in copies(slot, buffer):
            copy.start()
        if last:
            rows_out[slot] = tile[48:56, :]
        else:
            rows_out[table[ROW_NEAR, slot]] += multiply(
                tile[48:56, :], high_tile[buffer], low_tile[buffer], BY_COLS
            )

        @pl.when(table[CROSSING, slot] != 0)
        def _():
            col_acc[table[COL_AT, slot]] += multiply(
                row_vec[row_at], high_tile[buffer], low_tile[buffer], BY_ROWS
            )

    def visit(slot, formed):
        mine = table[STAGE, slot] == stage

        @pl.when(mine)
        def _():
            form(slot, formed)

        return formed + jnp.where(mine, 1, 0)

    formed = lax.fori_loop(0, high_ref.shape[0], visit, 0)
    for back in (1, 2):

        @pl.when(formed >= back)
        def _():
            for copy in copies(0, lax.rem(formed + back, 2)):
                copy.wait()


def form_stage(stage, table, prepared, row_vec, places, state, blocks):
    slots = table.shape[1]
    vmem = pl.BlockSpec(memory_space=pltpu.VMEM)
    hbm = pl.BlockSpec(memory_space=pltpu.HBM)
    shapes = [
        pltpu.HBM((slots, TILE, TILE), jnp.bfloat16),
        pltpu.HBM((slots, TILE, TILE), jnp.bfloat16),
        jax.ShapeDtypeStruct(
            (slots if stage == LAST_STAGE else row_vec.shape[0], 8, TILE), jnp.float32
        ),
        jax.ShapeDtypeStruct((blocks, 8, TILE), jnp.float32),
    ]
    first = 3 + len(places)
    return pl.pallas_call(
        functools.partial(stage_kernel, stage, len(places)),
        in_specs=[pl.BlockSpec(memory_space=pltpu.SMEM)]
        + [vmem] * (2 + len(places))
        + ([hbm, hbm, vmem, vmem] if state else []),
        out_specs=[hbm, hbm, vmem, vmem],
        out_shape=shapes,
        input_output_aliases={
            first + i: i for i in range(2 if stage == LAST_STAGE else len(state))
        },
        scratch_shapes=[
            pltpu.VMEM((56, TILE), jnp.float32),
            pltpu.VMEM((16, DEPTH, TILE), jnp.bfloat16),
            pltpu.VMEM((2, TILE, TILE), jnp.bfloat16),
            pltpu.VMEM((2, TILE, TILE), jnp.bfloat16),
            pltpu.SemaphoreType.DMA((2, 2)),
        ],
        compiler_params=pltpu.CompilerParams(vmem_limit_bytes=8 << 20),
        cost_estimate=pl.CostEstimate(
            flops=8 * 10**9, bytes_accessed=8 << 20, transcendentals=10**7
        ),
        name=f"form_{stage}",
    )(table, prepared, row_vec, *places, *state)


def apply_kernel(wanted, col_at, table, high_ref, low_ref, field, *refs):
    acc, high, low, sems = refs[-4:]
    slots = high_ref.shape[0]

    def copies(slot):
        return [
            pltpu.make_async_copy(high_ref.at[slot], high.at[slot], sems.at[0, slot]),
            pltpu.make_async_copy(low_ref.at[slot], low.at[slot], sems.at[1, slot]),
        ]

    for slot in range(slots):

        @pl.when(table[wanted, slot] != 0)
        def _():
            for copy in copies(slot):
                copy.start()

    acc[...] = jnp.zeros_like(acc) if len(refs) == 4 else refs[0][...]

    def visit(slot, carry):
        @pl.when(table[wanted, slot] != 0)
        def _():
            for copy in copies(slot):
                copy.wait()
            row = table[ROW_NEAR, slot]
            col = slot if col_at is None else table[col_at, slot]
            if wanted != CROSSING:
                acc[row] += multiply(field[col], high[slot], low[slot], BY_COLS)
            else:
                acc[col] += multiply(field[row], high[slot], low[slot], BY_ROWS)

        return carry

    lax.fori_loop(0, slots, visit, 0)


def apply_tiles(wanted, col_at, name, table, high, low, field, count, start=()):
    vmem = pl.BlockSpec(memory_space=pltpu.VMEM)
    hbm = pl.BlockSpec(memory_space=pltpu.HBM)
    return pl.pallas_call(
        functools.partial(apply_kernel, wanted, col_at),
        in_specs=[pl.BlockSpec(memory_space=pltpu.SMEM), hbm, hbm, vmem] + [vmem] * len(start),
        out_specs=vmem,
        out_shape=jax.ShapeDtypeStruct((count, 8, TILE), jnp.float32),
        scratch_shapes=[
            pltpu.VMEM(high.shape, high.dtype),
            pltpu.VMEM(low.shape, low.dtype),
            pltpu.SemaphoreType.DMA((2, high.shape[0])),
        ],
        compiler_params=pltpu.CompilerParams(vmem_limit_bytes=16 << 20),
        cost_estimate=pl.CostEstimate(
            flops=3 * 10**9, bytes_accessed=12 << 20, transcendentals=0
        ),
        name=name,
    )(table, in_hbm(high), in_hbm(low), field, *start)


def shift(value, axis, distance):
    size = lax.axis_size(axis)
    return lax.ppermute(value, axis, [(i, (i + distance) % size) for i in range(size)])


def spread(piece, axes):
    copies = jnp.broadcast_to(piece, (lax.axis_size(axes),) + piece.shape)
    return lax.all_to_all(copies, axes, 0, 0, tiled=True)


def spread_near(piece):
    both = jnp.stack([piece, shift(piece, "core", 1)])
    near = [both] + [shift(both, "x", d) for d in range(1, lax.axis_size("x"))]
    return jnp.stack(near, axis=1).reshape(2 * len(near), *piece.shape)


def reduce_near(row_acc):
    size = lax.axis_size("x")
    mine = row_acc[:size] + shift(row_acc[size:], "core", 1)
    total = mine[0]
    for d in range(1, size):
        total = total + shift(mine[d], "x", size - d)
    return total


def gather_y(piece):
    return jnp.stack([piece] + [shift(piece, "y", d) for d in range(1, lax.axis_size("y"))])


def gather_z(near):
    size, half = lax.axis_size("z"), near.shape[0] // 2
    arrived = [[near]]
    behind = ahead = near
    for distance in range(1, size // 2 + 1):
        if distance == size // 2:
            behind, ahead = behind[:half], ahead[half:]
        behind, ahead = shift(behind, "z", 1), shift(ahead, "z", size - 1)
        arrived.append([behind, ahead])
    return arrived


def table_kernel(pairs, valid, sizes, out):
    size_z, size_y, size_x, tiles = sizes
    z, y = lax.axis_index("z"), lax.axis_index("y")
    x, core = lax.axis_index("x"), lax.axis_index("core")
    slots = out.shape[1]
    arrival, keys = [], []
    for slot in range(slots):
        row, col, live = pairs[0, slot], pairs[1, slot], valid[0, slot] != 0
        behind = lax.rem(z - col // size_y + size_z, size_z)
        place = lax.rem(y - lax.rem(col, size_y) + size_y, size_y)
        upper = place >= size_y // 2
        far = jnp.where(upper, size_z, size_z - 1)
        source = jnp.where(behind < size_z // 2, 2 * behind - 1, 2 * (size_z - behind))
        source = jnp.where(behind == size_z // 2, far, source)
        source = jnp.where(behind == 0, 0, source)
        place = jnp.where((behind == size_z // 2) & upper, place - size_y // 2, place)
        crossing = ((z * size_y + y) * tiles + row) != (col * tiles + 2 * x + core)
        near = jnp.where(lax.rem(row, 2) == core, 0, size_x)
        near = near + lax.rem(x - row // 2 + size_x, size_x)
        out[ROW_AT, slot] = row
        out[ROW_NEAR, slot] = near
        out[COL_AT, slot] = col
        out[SOURCE, slot] = source
        out[PLACE, slot] = place
        out[LIVE, slot] = jnp.where(live, 1, 0)
        out[CROSSING, slot] = jnp.where(live & crossing, 1, 0)
        stage = jnp.where(live, (source + 1) // 2, LAST_STAGE)
        arrival.append(jnp.maximum(PER_STAGE * stage - 1, 0))
        keys.append(stage * slots + slot)
    ranks = [
        sum(jnp.where(other <= key, 1, 0) for other in keys) for key in keys
    ]
    for slot in range(slots):
        turn = arrival[slot]
        for other in range(slots):
            if other != slot:
                wait = arrival[other] + ranks[slot] - ranks[other]
                turn = jnp.maximum(turn, jnp.where(keys[other] <= keys[slot], wait, 0))
        stage = jnp.minimum((turn + 1) // PER_STAGE, LAST_STAGE)
        live = valid[0, slot] != 0
        out[STAGE, slot] = jnp.where(live, stage, -1)
        out[LATE, slot] = jnp.where(live & (stage == LAST_STAGE), 1, 0)


def slot_table(pairs, valid, sizes):
    smem = pl.BlockSpec(memory_space=pltpu.SMEM)

    def kernel(pairs_ref, valid_ref, out_ref):
        table_kernel(pairs_ref, valid_ref, sizes, out_ref)

    return pl.pallas_call(
        kernel,
        in_specs=[smem, smem],
        out_specs=smem,
        out_shape=jax.ShapeDtypeStruct((9, pairs.shape[1]), jnp.int32),
        name="slot_table",
    )(pairs, valid)


def combine(row_acc, col_acc):
    by_col = lax.all_to_all(col_acc, ROW, 0, 0, tiled=True)
    return reduce_near(row_acc) + jnp.sum(by_col, axis=0)


def per_device(positions, vectors, pairs, valid):
    grid_col = lax.axis_index(COL)
    block = positions.shape[2]
    tiles = block // TILE
    blocks = lax.axis_size(ROW)
    sizes = (lax.axis_size("z"), lax.axis_size("y"), lax.axis_size("x"), tiles)
    table = slot_table(pairs[0, 0].transpose(1, 0), valid[0], sizes)

    flat = positions.transpose(1, 0, 2).reshape(48, block)
    own = jnp.concatenate(
        [
            lax.dynamic_slice_in_dim(flat, grid_col * TILE, TILE, 1),
            lax.dynamic_slice_in_dim(vectors, grid_col * TILE, TILE, 1),
        ],
        axis=0,
    )
    row_vec = vectors.reshape(8, tiles, TILE).transpose(1, 0, 2)
    near = gather_y(own)
    flat, near = lax.optimization_barrier((flat, near))
    prepared = prepare_rows(flat)
    places, state = [], []
    for stage, arrived in enumerate(gather_z(near)):
        places = places + arrived
        early = state
        state = form_stage(stage, table, prepared, row_vec, places, state, blocks)
    high, low, slot_vec, col_acc = state
    row_acc = apply_tiles(
        LATE, None, "apply_late", table, high, low, slot_vec, tiles, (early[2],)
    )
    first = combine(row_acc, col_acc)

    col_vec = spread(first, ROW)
    col_acc = apply_tiles(CROSSING, COL_AT, "apply_cols", table, high, low, spread_near(first), blocks)
    row_acc = apply_tiles(LIVE, COL_AT, "apply_rows", table, high, low, col_vec, tiles)
    second = combine(row_acc, col_acc)

    rows = spread(second, COL)
    squares = jnp.sum(rows * rows, axis=(0, 2))
    squares = spread(jnp.pad(squares[None, :], ((0, 0), (0, 120))), ROW)
    total = jnp.sum(squares[:, 0, :8], axis=0) / (block * blocks)
    scaled = rows / jnp.sqrt(total + 1e-06)[None, :, None]
    return scaled.transpose(1, 0, 2).reshape(8, block)


def solution(mesh):
    physical = Mesh(mesh.devices.reshape(8, 4, 4, 2), ("z", "y", "x", "core"))
    placed = (
        P(None, None, ROW),
        P(None, ROW),
        P(ROW, COL, None, None),
        P(ROW, COL, None),
    )
    return jax.shard_map(
        per_device, mesh=physical, in_specs=placed, out_specs=P(None, ROW), check_vma=False
    )
```

```python
import functools
import math

import jax
import jax.numpy as jnp
from jax import lax
from jax.experimental import pallas as pl
from jax.experimental.pallas import tpu as pltpu
from jax.sharding import Mesh
from jax.sharding import PartitionSpec as P

TILE = 512
ROW = ("z", "y")
COL = ("x", "core")
ROW_AT, ROW_NEAR, COL_AT, SOURCE, PLACE, STAGE, LIVE, CROSSING, LATE = range(9)
LAST_STAGE = 4
LAST_TURN = 6
BY_ROWS = (((1,), (0,)), ((), ()))
BY_COLS = (((1,), (1,)), ((), ()))
LOG2E = math.log2(math.e)
GROUPS = 6
DEPTH = 8 * GROUPS
HALF = 256


def in_hbm(value):
    return pltpu.with_memory_space_constraint(value, pltpu.HBM)


def split3(value):
    high = value.astype(jnp.bfloat16).astype(jnp.float32)
    rest = value - high
    mid = rest.astype(jnp.bfloat16).astype(jnp.float32)
    return high, mid, rest - mid


def rows_of(ref, snapshot, scale, norm_at, one_at):
    width = ref.shape[-1]
    place = lax.broadcasted_iota(jnp.int32, (8, width), 0)
    parts = [
        jnp.broadcast_to(ref[pl.ds(16 * q + snapshot, 1), :], (8, width))
        for q in range(3)
    ]
    norm = (-0.5 * LOG2E) * (parts[0] * parts[0] + parts[1] * parts[1] + parts[2] * parts[2])
    out = jnp.where(place == norm_at, norm, jnp.where(place == one_at, 1.0, 0.0))
    for q in range(3):
        out = jnp.where(place == q, parts[q] * scale if scale != 1.0 else parts[q], out)
    return out


def prepare_kernel(pos_ref, out_ref):
    def visit(tile, carry):
        part = pos_ref.at[:, pl.ds(pl.multiple_of(tile * TILE, TILE), TILE)]
        for snapshot in range(16):
            high, mid, low = split3(rows_of(part, snapshot, LOG2E, 4, 3))
            stacked = jnp.concatenate([high, high, mid, mid, high, low], axis=0)
            out_ref[tile, snapshot] = stacked.T.astype(jnp.bfloat16)
        return carry

    lax.fori_loop(0, out_ref.shape[0], visit, 0)


def prepare_rows(pos):
    tiles = pos.shape[1] // TILE
    vmem = pl.BlockSpec(memory_space=pltpu.VMEM)
    return pl.pallas_call(
        prepare_kernel,
        in_specs=[vmem],
        out_specs=vmem,
        out_shape=jax.ShapeDtypeStruct((tiles, 16, TILE, DEPTH), jnp.bfloat16),
        compiler_params=pltpu.CompilerParams(vmem_limit_bytes=4 << 20),
        cost_estimate=pl.CostEstimate(flops=10**8, bytes_accessed=8 << 20, transcendentals=0),
        name="prepare_rows",
    )(pos)


def multiply(field, high, low, dims):
    terms = jnp.concatenate(split3(field), axis=0).astype(jnp.bfloat16)
    dot = functools.partial(
        lax.dot_general, dimension_numbers=dims, preferred_element_type=jnp.float32
    )
    by_high = dot(terms, high)
    by_low = dot(terms[:16], low)
    return (by_high[0:8] + by_low[0:8]) + (by_high[8:16] + by_low[8:16]) + by_high[16:24]


def stage_kernel(stage, sources, table, prepared_ref, row_vec, *refs):
    places = refs[:sources]
    last = stage == LAST_STAGE
    high_ref, low_ref, rows_out, col_acc, tile, cols, high_tile, low_tile, sems = refs[-9:]
    if stage == 0:
        rows_out[...] = jnp.zeros_like(rows_out)
        col_acc[...] = jnp.zeros_like(col_acc)
    else:
        if not last:
            rows_out[...] = refs[sources + 2][...]
        col_acc[...] = refs[sources + 3][...]

    def copies(slot, buffer):
        return [
            pltpu.make_async_copy(high_tile.at[buffer], high_ref.at[slot], sems.at[0, buffer]),
            pltpu.make_async_copy(low_tile.at[buffer], low_ref.at[slot], sems.at[1, buffer]),
        ]

    def form(slot, formed):
        buffer = lax.rem(formed, 2)
        for source in range(sources):

            @pl.when(table[SOURCE, slot] == source)
            def _():
                tile[...] = places[source][table[PLACE, slot]]

        def stack(at, carry):
            for snapshot in (at * 4, at * 4 + 1, at * 4 + 2, at * 4 + 3):
                high, mid, low = split3(rows_of(tile, snapshot, 1.0, 3, 4))
                stacked = jnp.concatenate([high, mid, high, mid, low, high], axis=0)
                cols[snapshot] = stacked.astype(jnp.bfloat16)
            return carry

        lax.fori_loop(0, 4, stack, 0)
        row_at = table[ROW_AT, slot]

        @pl.when(formed >= 2)
        def _():
            for copy in copies(slot, buffer):
                copy.wait()

        def step(at, carry):
            part = pl.ds(pl.multiple_of(at * HALF, HALF), HALF)
            total = None
            for snapshot in range(16):
                exponent = jnp.dot(
                    prepared_ref[row_at, snapshot],
                    cols[snapshot, :, part],
                    preferred_element_type=jnp.float32,
                )
                term = jnp.exp2(exponent)
                total = term if total is None else total + term
            high = total.astype(jnp.bfloat16)
            high_tile[buffer, :, part] = high
            low_tile[buffer, :, part] = (total - high.astype(jnp.float32)).astype(jnp.bfloat16)
            return carry

        lax.fori_loop(0, TILE // HALF, step, 0)
        for copy in copies(slot, buffer):
            copy.start()
        if last:
            rows_out[slot] = tile[48:56, :]
        else:
            rows_out[table[ROW_NEAR, slot]] += multiply(
                tile[48:56, :], high_tile[buffer], low_tile[buffer], BY_COLS
            )

        @pl.when(table[CROSSING, slot] != 0)
        def _():
            col_acc[table[COL_AT, slot]] += multiply(
                row_vec[row_at], high_tile[buffer], low_tile[buffer], BY_ROWS
            )

    def visit(slot, formed):
        mine = table[STAGE, slot] == stage

        @pl.when(mine)
        def _():
            form(slot, formed)

        return formed + jnp.where(mine, 1, 0)

    formed = lax.fori_loop(0, high_ref.shape[0], visit, 0)
    for back in (1, 2):

        @pl.when(formed >= back)
        def _():
            for copy in copies(0, lax.rem(formed + back, 2)):
                copy.wait()


def form_stage(stage, table, prepared, row_vec, places, state, blocks):
    slots = table.shape[1]
    vmem = pl.BlockSpec(memory_space=pltpu.VMEM)
    hbm = pl.BlockSpec(memory_space=pltpu.HBM)
    shapes = [
        pltpu.HBM((slots, TILE, TILE), jnp.bfloat16),
        pltpu.HBM((slots, TILE, TILE), jnp.bfloat16),
        jax.ShapeDtypeStruct(
            (slots if stage == LAST_STAGE else row_vec.shape[0], 8, TILE), jnp.float32
        ),
        jax.ShapeDtypeStruct((blocks, 8, TILE), jnp.float32),
    ]
    first = 3 + len(places)
    return pl.pallas_call(
        functools.partial(stage_kernel, stage, len(places)),
        in_specs=[pl.BlockSpec(memory_space=pltpu.SMEM)]
        + [vmem] * (2 + len(places))
        + ([hbm, hbm, vmem, vmem] if state else []),
        out_specs=[hbm, hbm, vmem, vmem],
        out_shape=shapes,
        input_output_aliases={
            first + i: i for i in range(2 if stage == LAST_STAGE else len(state))
        },
        scratch_shapes=[
            pltpu.VMEM((56, TILE), jnp.float32),
            pltpu.VMEM((16, DEPTH, TILE), jnp.bfloat16),
            pltpu.VMEM((2, TILE, TILE), jnp.bfloat16),
            pltpu.VMEM((2, TILE, TILE), jnp.bfloat16),
            pltpu.SemaphoreType.DMA((2, 2)),
        ],
        compiler_params=pltpu.CompilerParams(vmem_limit_bytes=8 << 20),
        cost_estimate=pl.CostEstimate(
            flops=8 * 10**9, bytes_accessed=8 << 20, transcendentals=10**7
        ),
        name=f"form_{stage}",
    )(table, prepared, row_vec, *places, *state)


def apply_kernel(wanted, col_at, table, high_ref, low_ref, field, *refs):
    acc, high, low, sems = refs[-4:]
    slots = high_ref.shape[0]

    def copies(slot):
        return [
            pltpu.make_async_copy(high_ref.at[slot], high.at[slot], sems.at[0, slot]),
            pltpu.make_async_copy(low_ref.at[slot], low.at[slot], sems.at[1, slot]),
        ]

    for slot in range(slots):

        @pl.when(table[wanted, slot] != 0)
        def _():
            for copy in copies(slot):
                copy.start()

    acc[...] = jnp.zeros_like(acc) if len(refs) == 4 else refs[0][...]

    def visit(slot, carry):
        @pl.when(table[wanted, slot] != 0)
        def _():
            for copy in copies(slot):
                copy.wait()
            row = table[ROW_NEAR, slot]
            col = slot if col_at is None else table[col_at, slot]
            if wanted != CROSSING:
                acc[row] += multiply(field[col], high[slot], low[slot], BY_COLS)
            else:
                acc[col] += multiply(field[row], high[slot], low[slot], BY_ROWS)

        return carry

    lax.fori_loop(0, slots, visit, 0)


def apply_tiles(wanted, col_at, name, table, high, low, field, count, start=()):
    vmem = pl.BlockSpec(memory_space=pltpu.VMEM)
    hbm = pl.BlockSpec(memory_space=pltpu.HBM)
    return pl.pallas_call(
        functools.partial(apply_kernel, wanted, col_at),
        in_specs=[pl.BlockSpec(memory_space=pltpu.SMEM), hbm, hbm, vmem] + [vmem] * len(start),
        out_specs=vmem,
        out_shape=jax.ShapeDtypeStruct((count, 8, TILE), jnp.float32),
        scratch_shapes=[
            pltpu.VMEM(high.shape, high.dtype),
            pltpu.VMEM(low.shape, low.dtype),
            pltpu.SemaphoreType.DMA((2, high.shape[0])),
        ],
        compiler_params=pltpu.CompilerParams(vmem_limit_bytes=16 << 20),
        cost_estimate=pl.CostEstimate(
            flops=3 * 10**9, bytes_accessed=12 << 20, transcendentals=0
        ),
        name=name,
    )(table, in_hbm(high), in_hbm(low), field, *start)


def shift(value, axis, distance):
    size = lax.axis_size(axis)
    return lax.ppermute(value, axis, [(i, (i + distance) % size) for i in range(size)])


def spread(piece, axes):
    copies = jnp.broadcast_to(piece, (lax.axis_size(axes),) + piece.shape)
    return lax.all_to_all(copies, axes, 0, 0, tiled=True)


def spread_near(piece):
    both = jnp.stack([piece, shift(piece, "core", 1)])
    near = [both] + [shift(both, "x", d) for d in range(1, lax.axis_size("x"))]
    return jnp.stack(near, axis=1).reshape(2 * len(near), *piece.shape)


def reduce_near(row_acc):
    size = lax.axis_size("x")
    mine = row_acc[:size] + shift(row_acc[size:], "core", 1)
    total = mine[0]
    for d in range(1, size):
        total = total + shift(mine[d], "x", size - d)
    return total


def gather_y(piece):
    size = lax.axis_size("y")
    near = [piece] + [shift(piece, "y", d) for d in range(1, size)]
    return [jnp.stack(near[: size // 2]), jnp.stack(near[size // 2 :])]


def gather_z(near):
    size = lax.axis_size("z")
    arrived = [near]
    behind, ahead = near, near
    for distance in range(1, size // 2):
        behind = [shift(half, "z", 1) for half in behind]
        ahead = [shift(half, "z", size - 1) for half in ahead]
        arrived.append(behind + ahead)
    arrived.append([shift(behind[0], "z", 1), shift(ahead[1], "z", size - 1)])
    return arrived


def table_kernel(pairs, valid, sizes, out):
    size_z, size_y, size_x, tiles = sizes
    z, y = lax.axis_index("z"), lax.axis_index("y")
    x, core = lax.axis_index("x"), lax.axis_index("core")
    slots = out.shape[1]
    arrival, keys = [], []
    for slot in range(slots):
        row, col, live = pairs[0, slot], pairs[1, slot], valid[0, slot] != 0
        behind = lax.rem(z - col // size_y + size_z, size_z)
        place = lax.rem(y - lax.rem(col, size_y) + size_y, size_y)
        half = place // (size_y // 2)
        place = place - half * (size_y // 2)
        distance = jnp.minimum(behind, size_z - behind)
        source = 4 * distance - 2 + half + jnp.where(behind > size_z // 2, 2, 0)
        source = jnp.where(distance == 0, half, source)
        crossing = ((z * size_y + y) * tiles + row) != (col * tiles + 2 * x + core)
        near = jnp.where(lax.rem(row, 2) == core, 0, size_x)
        near = near + lax.rem(x - row // 2 + size_x, size_x)
        out[ROW_AT, slot] = row
        out[ROW_NEAR, slot] = near
        out[COL_AT, slot] = col
        out[SOURCE, slot] = source
        out[PLACE, slot] = place
        out[LIVE, slot] = jnp.where(live, 1, 0)
        out[CROSSING, slot] = jnp.where(live & crossing, 1, 0)
        stage = jnp.where(live, distance, LAST_STAGE)
        arrival.append(jnp.where(stage == LAST_STAGE, LAST_TURN, stage))
        keys.append(stage * slots + slot)
    ranks = [
        sum(jnp.where(other <= key, 1, 0) for other in keys) for key in keys
    ]
    for slot in range(slots):
        turn = arrival[slot]
        for other in range(slots):
            if other != slot:
                wait = arrival[other] + ranks[slot] - ranks[other]
                turn = jnp.maximum(turn, jnp.where(keys[other] <= keys[slot], wait, 0))
        stage = jnp.where(turn < LAST_TURN, jnp.minimum(turn, LAST_STAGE - 1), LAST_STAGE)
        live = valid[0, slot] != 0
        out[STAGE, slot] = jnp.where(live, stage, -1)
        out[LATE, slot] = jnp.where(live & (stage == LAST_STAGE), 1, 0)


def slot_table(pairs, valid, sizes):
    smem = pl.BlockSpec(memory_space=pltpu.SMEM)

    def kernel(pairs_ref, valid_ref, out_ref):
        table_kernel(pairs_ref, valid_ref, sizes, out_ref)

    return pl.pallas_call(
        kernel,
        in_specs=[smem, smem],
        out_specs=smem,
        out_shape=jax.ShapeDtypeStruct((9, pairs.shape[1]), jnp.int32),
        name="slot_table",
    )(pairs, valid)


def combine(row_acc, col_acc):
    by_col = lax.all_to_all(col_acc, ROW, 0, 0, tiled=True)
    return reduce_near(row_acc) + jnp.sum(by_col, axis=0)


def per_device(positions, vectors, pairs, valid):
    grid_col = lax.axis_index(COL)
    block = positions.shape[2]
    tiles = block // TILE
    blocks = lax.axis_size(ROW)
    sizes = (lax.axis_size("z"), lax.axis_size("y"), lax.axis_size("x"), tiles)
    table = slot_table(pairs[0, 0].transpose(1, 0), valid[0], sizes)

    flat = positions.transpose(1, 0, 2).reshape(48, block)
    own = jnp.concatenate(
        [
            lax.dynamic_slice_in_dim(flat, grid_col * TILE, TILE, 1),
            lax.dynamic_slice_in_dim(vectors, grid_col * TILE, TILE, 1),
        ],
        axis=0,
    )
    row_vec = vectors.reshape(8, tiles, TILE).transpose(1, 0, 2)
    near = gather_y(own)
    flat, near = lax.optimization_barrier((flat, near))
    prepared = prepare_rows(flat)
    places, state = [], []
    for stage, arrived in enumerate(gather_z(near)):
        places = places + arrived
        early = state
        state = form_stage(stage, table, prepared, row_vec, places, state, blocks)
    high, low, slot_vec, col_acc = state
    row_acc = apply_tiles(
        LATE, None, "apply_late", table, high, low, slot_vec, tiles, (early[2],)
    )
    first = combine(row_acc, col_acc)

    col_vec = spread(first, ROW)
    col_acc = apply_tiles(CROSSING, COL_AT, "apply_cols", table, high, low, spread_near(first), blocks)
    row_acc = apply_tiles(LIVE, COL_AT, "apply_rows", table, high, low, col_vec, tiles)
    second = combine(row_acc, col_acc)

    rows = spread(second, COL)
    squares = jnp.sum(rows * rows, axis=(0, 2))
    squares = spread(jnp.pad(squares[None, :], ((0, 0), (0, 120))), ROW)
    total = jnp.sum(squares[:, 0, :8], axis=0) / (block * blocks)
    scaled = rows / jnp.sqrt(total + 1e-06)[None, :, None]
    return scaled.transpose(1, 0, 2).reshape(8, block)


def solution(mesh):
    physical = Mesh(mesh.devices.reshape(8, 4, 4, 2), ("z", "y", "x", "core"))
    placed = (
        P(None, None, ROW),
        P(None, ROW),
        P(ROW, COL, None, None),
        P(ROW, COL, None),
    )
    return jax.shard_map(
        per_device, mesh=physical, in_specs=placed, out_specs=P(None, ROW), check_vma=False
    )
```

```python
import functools
import math

import jax
import jax.numpy as jnp
from jax import lax
from jax.experimental import pallas as pl
from jax.experimental.pallas import tpu as pltpu
from jax.sharding import Mesh
from jax.sharding import PartitionSpec as P

TILE = 512
ROW = ("z", "y")
COL = ("x", "core")
ROW_AT, ROW_NEAR, COL_AT, SOURCE, PLACE, STAGE, LIVE, CROSSING, LATE = range(9)
LAST_STAGE = 4
PER_STAGE = 2
BY_ROWS = (((1,), (0,)), ((), ()))
BY_COLS = (((1,), (1,)), ((), ()))
LOG2E = math.log2(math.e)
GROUPS = 6
DEPTH = 8 * GROUPS
HALF = 256


def in_hbm(value):
    return pltpu.with_memory_space_constraint(value, pltpu.HBM)


def split3(value):
    high = value.astype(jnp.bfloat16).astype(jnp.float32)
    rest = value - high
    mid = rest.astype(jnp.bfloat16).astype(jnp.float32)
    return high, mid, rest - mid


def rows_of(ref, snapshot, scale, norm_at, one_at):
    width = ref.shape[-1]
    place = lax.broadcasted_iota(jnp.int32, (8, width), 0)
    parts = [
        jnp.broadcast_to(ref[16 * q + snapshot : 16 * q + snapshot + 1, :], (8, width))
        for q in range(3)
    ]
    norm = (-0.5 * LOG2E) * (parts[0] * parts[0] + parts[1] * parts[1] + parts[2] * parts[2])
    out = jnp.where(place == norm_at, norm, jnp.where(place == one_at, 1.0, 0.0))
    for q in range(3):
        out = jnp.where(place == q, parts[q] * scale if scale != 1.0 else parts[q], out)
    return out


def prepare_kernel(pos_ref, out_ref):
    def visit(tile, carry):
        part = pos_ref.at[:, pl.ds(pl.multiple_of(tile * TILE, TILE), TILE)]
        for snapshot in range(16):
            high, mid, low = split3(rows_of(part, snapshot, LOG2E, 4, 3))
            stacked = jnp.concatenate([high, high, mid, mid, high, low], axis=0)
            out_ref[tile, snapshot] = stacked.T.astype(jnp.bfloat16)
        return carry

    lax.fori_loop(0, out_ref.shape[0], visit, 0)


def prepare_rows(pos):
    tiles = pos.shape[1] // TILE
    vmem = pl.BlockSpec(memory_space=pltpu.VMEM)
    return pl.pallas_call(
        prepare_kernel,
        in_specs=[vmem],
        out_specs=vmem,
        out_shape=jax.ShapeDtypeStruct((tiles, 16, TILE, DEPTH), jnp.bfloat16),
        compiler_params=pltpu.CompilerParams(vmem_limit_bytes=4 << 20),
        cost_estimate=pl.CostEstimate(flops=10**8, bytes_accessed=8 << 20, transcendentals=0),
        name="prepare_rows",
    )(pos)


def multiply(field, high, low, dims):
    terms = jnp.concatenate(split3(field), axis=0).astype(jnp.bfloat16)
    dot = functools.partial(
        lax.dot_general, dimension_numbers=dims, preferred_element_type=jnp.float32
    )
    by_high = dot(terms, high)
    by_low = dot(terms[:16], low)
    return (by_high[0:8] + by_low[0:8]) + (by_high[8:16] + by_low[8:16]) + by_high[16:24]


def stage_kernel(stage, sources, table, prepared_ref, row_vec, *refs):
    places = refs[:sources]
    last = stage == LAST_STAGE
    pair_ref, rows_out, col_acc, tile, cols, pair, sems = refs[-7:]
    if stage == 0:
        rows_out[...] = jnp.zeros_like(rows_out)
        col_acc[...] = jnp.zeros_like(col_acc)
    else:
        if not last:
            rows_out[...] = refs[sources + 1][...]
        col_acc[...] = refs[sources + 2][...]

    def copy(slot, buffer):
        return pltpu.make_async_copy(pair.at[buffer], pair_ref.at[slot], sems.at[buffer])

    def form(slot, formed):
        buffer = lax.rem(formed, 2)
        for source in range(sources):

            @pl.when(table[SOURCE, slot] == source)
            def _():
                tile[...] = places[source][table[PLACE, slot]]

        for snapshot in range(16):
            high, mid, low = split3(rows_of(tile, snapshot, 1.0, 3, 4))
            stacked = jnp.concatenate([high, mid, high, mid, low, high], axis=0)
            cols[snapshot] = stacked.astype(jnp.bfloat16)
        row_at = table[ROW_AT, slot]

        @pl.when(formed >= 2)
        def _():
            copy(slot, buffer).wait()

        def step(at, carry):
            part = pl.ds(pl.multiple_of(at * HALF, HALF), HALF)
            total = None
            for snapshot in range(16):
                exponent = jnp.dot(
                    prepared_ref[row_at, snapshot],
                    cols[snapshot, :, part],
                    preferred_element_type=jnp.float32,
                )
                term = jnp.exp2(exponent)
                total = term if total is None else total + term
            high = total.astype(jnp.bfloat16)
            pair[buffer, 0, :, part] = high
            pair[buffer, 1, :, part] = (total - high.astype(jnp.float32)).astype(jnp.bfloat16)
            return carry

        lax.fori_loop(0, TILE // HALF, step, 0)
        copy(slot, buffer).start()
        if last:
            rows_out[slot] = tile[48:56, :]
        else:
            rows_out[table[ROW_NEAR, slot]] += multiply(
                tile[48:56, :], pair[buffer, 0], pair[buffer, 1], BY_COLS
            )

        @pl.when(table[CROSSING, slot] != 0)
        def _():
            col_acc[table[COL_AT, slot]] += multiply(
                row_vec[row_at], pair[buffer, 0], pair[buffer, 1], BY_ROWS
            )

    def visit(slot, formed):
        mine = table[STAGE, slot] == stage

        @pl.when(mine)
        def _():
            form(slot, formed)

        return formed + jnp.where(mine, 1, 0)

    formed = lax.fori_loop(0, pair_ref.shape[0], visit, 0)
    for back in (1, 2):

        @pl.when(formed >= back)
        def _():
            copy(0, lax.rem(formed + back, 2)).wait()


def form_stage(stage, table, prepared, row_vec, places, state, blocks):
    slots = table.shape[1]
    vmem = pl.BlockSpec(memory_space=pltpu.VMEM)
    hbm = pl.BlockSpec(memory_space=pltpu.HBM)
    shapes = [
        pltpu.HBM((slots, 2, TILE, TILE), jnp.bfloat16),
        jax.ShapeDtypeStruct(
            (slots if stage == LAST_STAGE else row_vec.shape[0], 8, TILE), jnp.float32
        ),
        jax.ShapeDtypeStruct((blocks, 8, TILE), jnp.float32),
    ]
    first = 3 + len(places)
    return pl.pallas_call(
        functools.partial(stage_kernel, stage, len(places)),
        in_specs=[pl.BlockSpec(memory_space=pltpu.SMEM)]
        + [vmem] * (2 + len(places))
        + ([hbm, vmem, vmem] if state else []),
        out_specs=[hbm, vmem, vmem],
        out_shape=shapes,
        input_output_aliases={
            first + i: i for i in range(1 if stage == LAST_STAGE else len(state))
        },
        scratch_shapes=[
            pltpu.VMEM((56, TILE), jnp.float32),
            pltpu.VMEM((16, DEPTH, TILE), jnp.bfloat16),
            pltpu.VMEM((2, 2, TILE, TILE), jnp.bfloat16),
            pltpu.SemaphoreType.DMA((2,)),
        ],
        compiler_params=pltpu.CompilerParams(vmem_limit_bytes=8 << 20),
        cost_estimate=pl.CostEstimate(
            flops=8 * 10**9, bytes_accessed=8 << 20, transcendentals=10**7
        ),
        name=f"form_{stage}",
    )(table, prepared, row_vec, *places, *state)


def apply_kernel(wanted, col_at, table, pair_ref, field, *refs):
    acc, pair, sems = refs[-3:]
    slots = pair_ref.shape[0]

    def copy(slot):
        return pltpu.make_async_copy(pair_ref.at[slot], pair.at[slot], sems.at[slot])

    for slot in range(slots):

        @pl.when(table[wanted, slot] != 0)
        def _():
            copy(slot).start()

    acc[...] = jnp.zeros_like(acc) if len(refs) == 3 else refs[0][...]

    def visit(slot, carry):
        @pl.when(table[wanted, slot] != 0)
        def _():
            copy(slot).wait()
            row = table[ROW_NEAR, slot]
            col = slot if col_at is None else table[col_at, slot]
            if wanted != CROSSING:
                acc[row] += multiply(field[col], pair[slot, 0], pair[slot, 1], BY_COLS)
            else:
                acc[col] += multiply(field[row], pair[slot, 0], pair[slot, 1], BY_ROWS)

        return carry

    lax.fori_loop(0, slots, visit, 0)


def apply_tiles(wanted, col_at, name, table, pair, field, count, start=()):
    vmem = pl.BlockSpec(memory_space=pltpu.VMEM)
    hbm = pl.BlockSpec(memory_space=pltpu.HBM)
    return pl.pallas_call(
        functools.partial(apply_kernel, wanted, col_at),
        in_specs=[pl.BlockSpec(memory_space=pltpu.SMEM), hbm, vmem] + [vmem] * len(start),
        out_specs=vmem,
        out_shape=jax.ShapeDtypeStruct((count, 8, TILE), jnp.float32),
        scratch_shapes=[
            pltpu.VMEM(pair.shape, pair.dtype),
            pltpu.SemaphoreType.DMA((pair.shape[0],)),
        ],
        compiler_params=pltpu.CompilerParams(vmem_limit_bytes=16 << 20),
        cost_estimate=pl.CostEstimate(
            flops=3 * 10**9, bytes_accessed=12 << 20, transcendentals=0
        ),
        name=name,
    )(table, in_hbm(pair), field, *start)


def shift(value, axis, distance):
    size = lax.axis_size(axis)
    return lax.ppermute(value, axis, [(i, (i + distance) % size) for i in range(size)])


def spread(piece, axes):
    copies = jnp.broadcast_to(piece, (lax.axis_size(axes),) + piece.shape)
    return lax.all_to_all(copies, axes, 0, 0, tiled=True)


def spread_near(piece):
    both = jnp.stack([piece, shift(piece, "core", 1)])
    near = [both] + [shift(both, "x", d) for d in range(1, lax.axis_size("x"))]
    return jnp.stack(near, axis=1).reshape(2 * len(near), *piece.shape)


def reduce_near(row_acc):
    size = lax.axis_size("x")
    mine = row_acc[:size] + shift(row_acc[size:], "core", 1)
    total = mine[0]
    for d in range(1, size):
        total = total + shift(mine[d], "x", size - d)
    return total


def gather_y(piece):
    return jnp.stack([piece] + [shift(piece, "y", d) for d in range(1, lax.axis_size("y"))])


def gather_z(near):
    size, half = lax.axis_size("z"), near.shape[0] // 2
    arrived = [[near]]
    behind = ahead = near
    for distance in range(1, size // 2 + 1):
        if distance == size // 2:
            behind, ahead = behind[:half], ahead[half:]
        behind, ahead = shift(behind, "z", 1), shift(ahead, "z", size - 1)
        arrived.append([behind, ahead])
    return arrived


def table_kernel(pairs, valid, sizes, out):
    size_z, size_y, size_x, tiles = sizes
    z, y = lax.axis_index("z"), lax.axis_index("y")
    x, core = lax.axis_index("x"), lax.axis_index("core")
    slots = out.shape[1]
    arrival, keys = [], []
    for slot in range(slots):
        row, col, live = pairs[0, slot], pairs[1, slot], valid[0, slot] != 0
        behind = lax.rem(z - col // size_y + size_z, size_z)
        place = lax.rem(y - lax.rem(col, size_y) + size_y, size_y)
        upper = place >= size_y // 2
        far = jnp.where(upper, size_z, size_z - 1)
        source = jnp.where(behind < size_z // 2, 2 * behind - 1, 2 * (size_z - behind))
        source = jnp.where(behind == size_z // 2, far, source)
        source = jnp.where(behind == 0, 0, source)
        place = jnp.where((behind == size_z // 2) & upper, place - size_y // 2, place)
        crossing = ((z * size_y + y) * tiles + row) != (col * tiles + 2 * x + core)
        near = jnp.where(lax.rem(row, 2) == core, 0, size_x)
        near = near + lax.rem(x - row // 2 + size_x, size_x)
        out[ROW_AT, slot] = row
        out[ROW_NEAR, slot] = near
        out[COL_AT, slot] = col
        out[SOURCE, slot] = source
        out[PLACE, slot] = place
        out[LIVE, slot] = jnp.where(live, 1, 0)
        out[CROSSING, slot] = jnp.where(live & crossing, 1, 0)
        stage = jnp.where(live, (source + 1) // 2, LAST_STAGE)
        arrival.append(jnp.maximum(PER_STAGE * stage - 1, 0))
        keys.append(stage * slots + slot)
    ranks = [
        sum(jnp.where(other <= key, 1, 0) for other in keys) for key in keys
    ]
    for slot in range(slots):
        turn = arrival[slot]
        for other in range(slots):
            if other != slot:
                wait = arrival[other] + ranks[slot] - ranks[other]
                turn = jnp.maximum(turn, jnp.where(keys[other] <= keys[slot], wait, 0))
        stage = jnp.minimum((turn + 1) // PER_STAGE, LAST_STAGE)
        live = valid[0, slot] != 0
        out[STAGE, slot] = jnp.where(live, stage, -1)
        out[LATE, slot] = jnp.where(live & (stage == LAST_STAGE), 1, 0)


def slot_table(pairs, valid, sizes):
    smem = pl.BlockSpec(memory_space=pltpu.SMEM)

    def kernel(pairs_ref, valid_ref, out_ref):
        table_kernel(pairs_ref, valid_ref, sizes, out_ref)

    return pl.pallas_call(
        kernel,
        in_specs=[smem, smem],
        out_specs=smem,
        out_shape=jax.ShapeDtypeStruct((9, pairs.shape[1]), jnp.int32),
        name="slot_table",
    )(pairs, valid)


def combine(row_acc, col_acc):
    by_col = lax.all_to_all(col_acc, ROW, 0, 0, tiled=True)
    return reduce_near(row_acc) + jnp.sum(by_col, axis=0)


def per_device(positions, vectors, pairs, valid):
    grid_col = lax.axis_index(COL)
    block = positions.shape[2]
    tiles = block // TILE
    blocks = lax.axis_size(ROW)
    sizes = (lax.axis_size("z"), lax.axis_size("y"), lax.axis_size("x"), tiles)
    table = slot_table(pairs[0, 0].transpose(1, 0), valid[0], sizes)

    flat = positions.transpose(1, 0, 2).reshape(48, block)
    own = jnp.concatenate(
        [
            lax.dynamic_slice_in_dim(flat, grid_col * TILE, TILE, 1),
            lax.dynamic_slice_in_dim(vectors, grid_col * TILE, TILE, 1),
        ],
        axis=0,
    )
    row_vec = vectors.reshape(8, tiles, TILE).transpose(1, 0, 2)
    near = gather_y(own)
    flat, near = lax.optimization_barrier((flat, near))
    prepared = prepare_rows(flat)
    places, state = [], []
    for stage, arrived in enumerate(gather_z(near)):
        places = places + arrived
        early = state
        state = form_stage(stage, table, prepared, row_vec, places, state, blocks)
    pair, slot_vec, col_acc = state
    row_acc = apply_tiles(
        LATE, None, "apply_late", table, pair, slot_vec, tiles, (early[1],)
    )
    first = combine(row_acc, col_acc)

    col_vec = spread(first, ROW)
    col_acc = apply_tiles(CROSSING, COL_AT, "apply_cols", table, pair, spread_near(first), blocks)
    row_acc = apply_tiles(LIVE, COL_AT, "apply_rows", table, pair, col_vec, tiles)
    second = combine(row_acc, col_acc)

    rows = spread(second, COL)
    squares = jnp.sum(rows * rows, axis=(0, 2))
    squares = spread(jnp.pad(squares[None, :], ((0, 0), (0, 120))), ROW)
    total = jnp.sum(squares[:, 0, :8], axis=0) / (block * blocks)
    scaled = rows / jnp.sqrt(total + 1e-06)[None, :, None]
    return scaled.transpose(1, 0, 2).reshape(8, block)


def solution(mesh):
    physical = Mesh(mesh.devices.reshape(8, 4, 4, 2), ("z", "y", "x", "core"))
    placed = (
        P(None, None, ROW),
        P(None, ROW),
        P(ROW, COL, None, None),
        P(ROW, COL, None),
    )
    return jax.shard_map(
        per_device, mesh=physical, in_specs=placed, out_specs=P(None, ROW), check_vma=False
    )
```

```python
import functools
import math

import jax
import jax.numpy as jnp
from jax import lax
from jax.experimental import pallas as pl
from jax.experimental.pallas import tpu as pltpu
from jax.sharding import Mesh
from jax.sharding import PartitionSpec as P

TILE = 512
ROW = ("z", "y")
COL = ("x", "core")
ROW_AT, ROW_NEAR, COL_AT, SOURCE, PLACE, STAGE, LIVE, CROSSING, LATE, ROW_SEEN = range(10)
LAST_STAGE = 4
PER_STAGE = 2
BY_ROWS = (((1,), (0,)), ((), ()))
BY_COLS = (((1,), (1,)), ((), ()))
LOG2E = math.log2(math.e)
GROUPS = 6
DEPTH = 8 * GROUPS
HALF = 256


def in_hbm(value):
    return pltpu.with_memory_space_constraint(value, pltpu.HBM)


def split3(value):
    high = value.astype(jnp.bfloat16).astype(jnp.float32)
    rest = value - high
    mid = rest.astype(jnp.bfloat16).astype(jnp.float32)
    return high, mid, rest - mid


def rows_of(ref, snapshot, scale, norm_at, one_at):
    width = ref.shape[-1]
    place = lax.broadcasted_iota(jnp.int32, (8, width), 0)
    parts = [
        jnp.broadcast_to(ref[16 * q + snapshot : 16 * q + snapshot + 1, :], (8, width))
        for q in range(3)
    ]
    norm = (-0.5 * LOG2E) * (parts[0] * parts[0] + parts[1] * parts[1] + parts[2] * parts[2])
    out = jnp.where(place == norm_at, norm, jnp.where(place == one_at, 1.0, 0.0))
    for q in range(3):
        out = jnp.where(place == q, parts[q] * scale if scale != 1.0 else parts[q], out)
    return out


def prepare_kernel(pos_ref, out_ref):
    def visit(tile, carry):
        part = pos_ref.at[:, pl.ds(pl.multiple_of(tile * TILE, TILE), TILE)]
        for snapshot in range(16):
            high, mid, low = split3(rows_of(part, snapshot, LOG2E, 4, 3))
            stacked = jnp.concatenate([high, high, mid, mid, high, low], axis=0)
            out_ref[tile, snapshot] = stacked.T.astype(jnp.bfloat16)
        return carry

    lax.fori_loop(0, out_ref.shape[0], visit, 0)


def prepare_rows(pos):
    tiles = pos.shape[1] // TILE
    vmem = pl.BlockSpec(memory_space=pltpu.VMEM)
    return pl.pallas_call(
        prepare_kernel,
        in_specs=[vmem],
        out_specs=vmem,
        out_shape=jax.ShapeDtypeStruct((tiles, 16, TILE, DEPTH), jnp.bfloat16),
        compiler_params=pltpu.CompilerParams(vmem_limit_bytes=4 << 20),
        cost_estimate=pl.CostEstimate(flops=10**8, bytes_accessed=8 << 20, transcendentals=0),
        name="prepare_rows",
    )(pos)


def multiply(field, high, low, dims):
    terms = jnp.concatenate(split3(field), axis=0).astype(jnp.bfloat16)
    dot = functools.partial(
        lax.dot_general, dimension_numbers=dims, preferred_element_type=jnp.float32
    )
    by_high = dot(terms, high)
    by_low = dot(terms[:16], low)
    return (by_high[0:8] + by_low[0:8]) + (by_high[8:16] + by_low[8:16]) + by_high[16:24]


def stage_kernel(stage, sources, table, prepared_ref, row_vec, *refs):
    places = refs[:sources]
    last = stage == LAST_STAGE
    pair_ref, rows_out, col_acc, tile, cols, pair, sems = refs[-7:]
    if stage == 0:
        rows_out[...] = jnp.zeros_like(rows_out)
        col_acc[...] = jnp.zeros_like(col_acc)
    else:
        if not last:
            rows_out[...] = refs[sources + 1][...]
        col_acc[...] = refs[sources + 2][...]

    def copy(slot, buffer):
        return pltpu.make_async_copy(pair.at[buffer], pair_ref.at[slot], sems.at[buffer])

    def form(slot, formed):
        buffer = lax.rem(formed, 2)
        for source in range(sources):

            @pl.when(table[SOURCE, slot] == source)
            def _():
                tile[...] = places[source][table[PLACE, slot]]

        for snapshot in range(16):
            high, mid, low = split3(rows_of(tile, snapshot, 1.0, 3, 4))
            stacked = jnp.concatenate([high, mid, high, mid, low, high], axis=0)
            cols[snapshot] = stacked.astype(jnp.bfloat16)
        row_at = table[ROW_AT, slot]

        @pl.when(formed >= 2)
        def _():
            copy(slot, buffer).wait()

        def step(at, carry):
            part = pl.ds(pl.multiple_of(at * HALF, HALF), HALF)
            total = None
            for snapshot in range(16):
                exponent = jnp.dot(
                    prepared_ref[row_at, snapshot],
                    cols[snapshot, :, part],
                    preferred_element_type=jnp.float32,
                )
                term = jnp.exp2(exponent)
                total = term if total is None else total + term
            high = total.astype(jnp.bfloat16)
            pair[buffer, 0, :, part] = high
            pair[buffer, 1, :, part] = (total - high.astype(jnp.float32)).astype(jnp.bfloat16)
            return carry

        lax.fori_loop(0, TILE // HALF, step, 0)
        copy(slot, buffer).start()
        if last:
            rows_out[slot] = tile[48:56, :]
        else:
            rows_out[table[ROW_NEAR, slot]] += multiply(
                tile[48:56, :], pair[buffer, 0], pair[buffer, 1], BY_COLS
            )

        @pl.when(table[CROSSING, slot] != 0)
        def _():
            col_acc[table[COL_AT, slot]] += multiply(
                row_vec[row_at], pair[buffer, 0], pair[buffer, 1], BY_ROWS
            )

    def visit(slot, formed):
        mine = table[STAGE, slot] == stage

        @pl.when(mine)
        def _():
            form(slot, formed)

        return formed + jnp.where(mine, 1, 0)

    formed = lax.fori_loop(0, pair_ref.shape[0], visit, 0)
    for back in (1, 2):

        @pl.when(formed >= back)
        def _():
            copy(0, lax.rem(formed + back, 2)).wait()


def form_stage(stage, table, prepared, row_vec, places, state, blocks):
    slots = table.shape[1]
    vmem = pl.BlockSpec(memory_space=pltpu.VMEM)
    hbm = pl.BlockSpec(memory_space=pltpu.HBM)
    shapes = [
        pltpu.HBM((slots, 2, TILE, TILE), jnp.bfloat16),
        jax.ShapeDtypeStruct(
            (slots if stage == LAST_STAGE else row_vec.shape[0], 8, TILE), jnp.float32
        ),
        jax.ShapeDtypeStruct((blocks, 8, TILE), jnp.float32),
    ]
    first = 3 + len(places)
    return pl.pallas_call(
        functools.partial(stage_kernel, stage, len(places)),
        in_specs=[pl.BlockSpec(memory_space=pltpu.SMEM)]
        + [vmem] * (2 + len(places))
        + ([hbm, vmem, vmem] if state else []),
        out_specs=[hbm, vmem, vmem],
        out_shape=shapes,
        input_output_aliases={
            first + i: i for i in range(1 if stage == LAST_STAGE else len(state))
        },
        scratch_shapes=[
            pltpu.VMEM((56, TILE), jnp.float32),
            pltpu.VMEM((16, DEPTH, TILE), jnp.bfloat16),
            pltpu.VMEM((2, 2, TILE, TILE), jnp.bfloat16),
            pltpu.SemaphoreType.DMA((2,)),
        ],
        compiler_params=pltpu.CompilerParams(vmem_limit_bytes=8 << 20),
        cost_estimate=pl.CostEstimate(
            flops=8 * 10**9, bytes_accessed=8 << 20, transcendentals=10**7
        ),
        name=f"form_{stage}",
    )(table, prepared, row_vec, *places, *state)


def apply_kernel(wanted, col_at, table, pair_ref, field, *refs):
    acc, pair, sems = refs[-3:]
    slots = pair_ref.shape[0]

    def copy(slot):
        return pltpu.make_async_copy(pair_ref.at[slot], pair.at[slot], sems.at[slot])

    for slot in range(slots):

        @pl.when(table[wanted, slot] != 0)
        def _():
            copy(slot).start()

    acc[...] = jnp.zeros_like(acc) if len(refs) == 3 else refs[0][...]

    def visit(slot, carry):
        @pl.when(table[wanted, slot] != 0)
        def _():
            copy(slot).wait()
            row = table[ROW_NEAR, slot]
            col = slot if col_at is None else table[col_at, slot]
            if wanted != CROSSING:
                acc[row] += multiply(field[col], pair[slot, 0], pair[slot, 1], BY_COLS)
            else:
                acc[col] += multiply(field[row], pair[slot, 0], pair[slot, 1], BY_ROWS)

        return carry

    lax.fori_loop(0, slots, visit, 0)


def apply_tiles(wanted, col_at, name, table, pair, field, count, start=()):
    vmem = pl.BlockSpec(memory_space=pltpu.VMEM)
    hbm = pl.BlockSpec(memory_space=pltpu.HBM)
    return pl.pallas_call(
        functools.partial(apply_kernel, wanted, col_at),
        in_specs=[pl.BlockSpec(memory_space=pltpu.SMEM), hbm, vmem] + [vmem] * len(start),
        out_specs=vmem,
        out_shape=jax.ShapeDtypeStruct((count, 8, TILE), jnp.float32),
        scratch_shapes=[
            pltpu.VMEM(pair.shape, pair.dtype),
            pltpu.SemaphoreType.DMA((pair.shape[0],)),
        ],
        compiler_params=pltpu.CompilerParams(vmem_limit_bytes=16 << 20),
        cost_estimate=pl.CostEstimate(
            flops=3 * 10**9, bytes_accessed=12 << 20, transcendentals=0
        ),
        name=name,
    )(table, in_hbm(pair), field, *start)


def fetch_kernel(table, pair_ref, after, out, sems):
    slots = pair_ref.shape[0]

    def copy(slot):
        return pltpu.make_async_copy(pair_ref.at[slot], out.at[slot], sems.at[slot])

    for slot in range(slots):

        @pl.when(table[CROSSING, slot] != 0)
        def _():
            copy(slot).start()

    for slot in range(slots):

        @pl.when(table[CROSSING, slot] != 0)
        def _():
            copy(slot).wait()


def fetch(table, pair, after):
    vmem = pl.BlockSpec(memory_space=pltpu.VMEM)
    return pl.pallas_call(
        fetch_kernel,
        in_specs=[
            pl.BlockSpec(memory_space=pltpu.SMEM),
            pl.BlockSpec(memory_space=pltpu.HBM),
            vmem,
        ],
        out_specs=vmem,
        out_shape=jax.ShapeDtypeStruct(pair.shape, pair.dtype),
        scratch_shapes=[pltpu.SemaphoreType.DMA((pair.shape[0],))],
        compiler_params=pltpu.CompilerParams(vmem_limit_bytes=2 << 20),
        cost_estimate=pl.CostEstimate(flops=0, bytes_accessed=12 << 20, transcendentals=0),
        name="fetch",
    )(table, in_hbm(pair), after)


def cols_kernel(table, pair, field, acc):
    acc[...] = jnp.zeros_like(acc)

    def visit(slot, carry):
        @pl.when(table[CROSSING, slot] != 0)
        def _():
            acc[table[COL_AT, slot]] += multiply(
                field[table[ROW_SEEN, slot]], pair[slot, 0], pair[slot, 1], BY_ROWS
            )

        return carry

    lax.fori_loop(0, pair.shape[0], visit, 0)


def apply_cols(table, pair, field, count):
    vmem = pl.BlockSpec(memory_space=pltpu.VMEM)
    return pl.pallas_call(
        cols_kernel,
        in_specs=[pl.BlockSpec(memory_space=pltpu.SMEM), vmem, vmem],
        out_specs=vmem,
        out_shape=jax.ShapeDtypeStruct((count, 8, TILE), jnp.float32),
        compiler_params=pltpu.CompilerParams(vmem_limit_bytes=4 << 20),
        cost_estimate=pl.CostEstimate(
            flops=3 * 10**9, bytes_accessed=1 << 20, transcendentals=0
        ),
        name="apply_cols",
    )(table, pair, field)


def shift(value, axis, distance):
    size = lax.axis_size(axis)
    return lax.ppermute(value, axis, [(i, (i + distance) % size) for i in range(size)])


def spread(piece, axes):
    copies = jnp.broadcast_to(piece, (lax.axis_size(axes),) + piece.shape)
    return lax.all_to_all(copies, axes, 0, 0, tiled=True)


def spread_near(both):
    near = [both] + [shift(both, "x", d) for d in range(1, lax.axis_size("x"))]
    return jnp.concatenate(near, axis=0)


def reduce_near(row_acc):
    size = lax.axis_size("x")
    mine = row_acc[:size] + shift(row_acc[size:], "core", 1)
    total = mine[0]
    for d in range(1, size):
        total = total + shift(mine[d], "x", size - d)
    return total


def gather_y(piece):
    return jnp.stack([piece] + [shift(piece, "y", d) for d in range(1, lax.axis_size("y"))])


def gather_z(near):
    size, half = lax.axis_size("z"), near.shape[0] // 2
    arrived = [[near]]
    behind = ahead = near
    for distance in range(1, size // 2 + 1):
        if distance == size // 2:
            behind, ahead = behind[:half], ahead[half:]
        behind, ahead = shift(behind, "z", 1), shift(ahead, "z", size - 1)
        arrived.append([behind, ahead])
    return arrived


def table_kernel(pairs, valid, sizes, out):
    size_z, size_y, size_x, tiles = sizes
    z, y = lax.axis_index("z"), lax.axis_index("y")
    x, core = lax.axis_index("x"), lax.axis_index("core")
    slots = out.shape[1]
    arrival, keys = [], []
    for slot in range(slots):
        row, col, live = pairs[0, slot], pairs[1, slot], valid[0, slot] != 0
        behind = lax.rem(z - col // size_y + size_z, size_z)
        place = lax.rem(y - lax.rem(col, size_y) + size_y, size_y)
        upper = place >= size_y // 2
        far = jnp.where(upper, size_z, size_z - 1)
        source = jnp.where(behind < size_z // 2, 2 * behind - 1, 2 * (size_z - behind))
        source = jnp.where(behind == size_z // 2, far, source)
        source = jnp.where(behind == 0, 0, source)
        place = jnp.where((behind == size_z // 2) & upper, place - size_y // 2, place)
        crossing = ((z * size_y + y) * tiles + row) != (col * tiles + 2 * x + core)
        other = jnp.where(lax.rem(row, 2) == core, 0, 1)
        along = lax.rem(x - row // 2 + size_x, size_x)
        out[ROW_AT, slot] = row
        out[ROW_NEAR, slot] = other * size_x + along
        out[ROW_SEEN, slot] = 2 * along + other
        out[COL_AT, slot] = col
        out[SOURCE, slot] = source
        out[PLACE, slot] = place
        out[LIVE, slot] = jnp.where(live, 1, 0)
        out[CROSSING, slot] = jnp.where(live & crossing, 1, 0)
        stage = jnp.where(live, (source + 1) // 2, LAST_STAGE)
        arrival.append(jnp.maximum(PER_STAGE * stage - 1, 0))
        keys.append(stage * slots + slot)
    ranks = [
        sum(jnp.where(other <= key, 1, 0) for other in keys) for key in keys
    ]
    for slot in range(slots):
        turn = arrival[slot]
        for other in range(slots):
            if other != slot:
                wait = arrival[other] + ranks[slot] - ranks[other]
                turn = jnp.maximum(turn, jnp.where(keys[other] <= keys[slot], wait, 0))
        stage = jnp.minimum((turn + 1) // PER_STAGE, LAST_STAGE)
        live = valid[0, slot] != 0
        out[STAGE, slot] = jnp.where(live, stage, -1)
        out[LATE, slot] = jnp.where(live & (stage == LAST_STAGE), 1, 0)


def slot_table(pairs, valid, sizes):
    smem = pl.BlockSpec(memory_space=pltpu.SMEM)

    def kernel(pairs_ref, valid_ref, out_ref):
        table_kernel(pairs_ref, valid_ref, sizes, out_ref)

    return pl.pallas_call(
        kernel,
        in_specs=[smem, smem],
        out_specs=smem,
        out_shape=jax.ShapeDtypeStruct((10, pairs.shape[1]), jnp.int32),
        name="slot_table",
    )(pairs, valid)


def combine(row_acc, col_acc):
    by_col = lax.all_to_all(col_acc, ROW, 0, 0, tiled=True)
    return reduce_near(row_acc) + jnp.sum(by_col, axis=0)


def per_device(positions, vectors, pairs, valid):
    grid_col = lax.axis_index(COL)
    block = positions.shape[2]
    tiles = block // TILE
    blocks = lax.axis_size(ROW)
    sizes = (lax.axis_size("z"), lax.axis_size("y"), lax.axis_size("x"), tiles)
    table = slot_table(pairs[0, 0].transpose(1, 0), valid[0], sizes)

    flat = positions.transpose(1, 0, 2).reshape(48, block)
    own = lax.dynamic_slice_in_dim(
        jnp.concatenate([flat, vectors], axis=0), grid_col * TILE, TILE, 1
    )
    row_vec = vectors.reshape(8, tiles, TILE).transpose(1, 0, 2)
    near = gather_y(own)
    flat, near = lax.optimization_barrier((flat, near))
    prepared = prepare_rows(flat)
    places, state = [], []
    for stage, arrived in enumerate(gather_z(near)):
        places = places + arrived
        early = state
        state = form_stage(stage, table, prepared, row_vec, places, state, blocks)
    pair, slot_vec, col_acc = state
    row_acc = apply_tiles(
        LATE, None, "apply_late", table, pair, slot_vec, tiles, (early[1],)
    )
    first = combine(row_acc, col_acc)

    col_vec = spread(first, ROW)
    both = jnp.stack([first, shift(first, "core", 1)])
    tiles_here = fetch(table, pair, both)
    col_acc = apply_cols(table, tiles_here, spread_near(both), blocks)
    row_acc = apply_tiles(LIVE, COL_AT, "apply_rows", table, pair, col_vec, tiles)
    second = combine(row_acc, col_acc)

    rows = spread(second, COL)
    squares = jnp.sum(rows * rows, axis=(0, 2))
    squares = spread(jnp.pad(squares[None, :], ((0, 0), (0, 120))), ROW)
    total = jnp.sum(squares[:, 0, :8], axis=0) / (block * blocks)
    scaled = rows / jnp.sqrt(total + 1e-06)[None, :, None]
    return scaled.transpose(1, 0, 2).reshape(8, block)


def solution(mesh):
    physical = Mesh(mesh.devices.reshape(8, 4, 4, 2), ("z", "y", "x", "core"))
    placed = (
        P(None, None, ROW),
        P(None, ROW),
        P(ROW, COL, None, None),
        P(ROW, COL, None),
    )
    return jax.shard_map(
        per_device, mesh=physical, in_specs=placed, out_specs=P(None, ROW), check_vma=False
    )
```

```python
import functools
import math

import jax
import jax.numpy as jnp
from jax import lax
from jax.experimental import pallas as pl
from jax.experimental.pallas import tpu as pltpu
from jax.sharding import Mesh
from jax.sharding import PartitionSpec as P

TILE = 512
ROW = ("z", "y")
COL = ("x", "core")
ROW_AT, ROW_NEAR, COL_AT, SOURCE, PLACE, STAGE, LIVE, CROSSING, LATE, ROW_SEEN = range(10)
LAST_STAGE = 4
PER_STAGE = 2
BY_ROWS = (((1,), (0,)), ((), ()))
BY_COLS = (((1,), (1,)), ((), ()))
LOG2E = math.log2(math.e)
GROUPS = 6
DEPTH = 8 * GROUPS
HALF = 256


def in_hbm(value):
    return pltpu.with_memory_space_constraint(value, pltpu.HBM)


def split3(value):
    high = value.astype(jnp.bfloat16).astype(jnp.float32)
    rest = value - high
    mid = rest.astype(jnp.bfloat16).astype(jnp.float32)
    return high, mid, rest - mid


def rows_of(ref, snapshot, scale, norm_at, one_at):
    width = ref.shape[-1]
    place = lax.broadcasted_iota(jnp.int32, (8, width), 0)
    parts = [
        jnp.broadcast_to(ref[16 * q + snapshot : 16 * q + snapshot + 1, :], (8, width))
        for q in range(3)
    ]
    norm = (-0.5 * LOG2E) * (parts[0] * parts[0] + parts[1] * parts[1] + parts[2] * parts[2])
    out = jnp.where(place == norm_at, norm, jnp.where(place == one_at, 1.0, 0.0))
    for q in range(3):
        out = jnp.where(place == q, parts[q] * scale if scale != 1.0 else parts[q], out)
    return out


def prepare_kernel(pos_ref, out_ref):
    def visit(tile, carry):
        part = pos_ref.at[:, pl.ds(pl.multiple_of(tile * TILE, TILE), TILE)]
        for snapshot in range(16):
            high, mid, low = split3(rows_of(part, snapshot, LOG2E, 4, 3))
            stacked = jnp.concatenate([high, high, mid, mid, high, low], axis=0)
            out_ref[tile, snapshot] = stacked.T.astype(jnp.bfloat16)
        return carry

    lax.fori_loop(0, out_ref.shape[0], visit, 0)


def prepare_rows(pos):
    tiles = pos.shape[1] // TILE
    vmem = pl.BlockSpec(memory_space=pltpu.VMEM)
    return pl.pallas_call(
        prepare_kernel,
        in_specs=[vmem],
        out_specs=vmem,
        out_shape=jax.ShapeDtypeStruct((tiles, 16, TILE, DEPTH), jnp.bfloat16),
        compiler_params=pltpu.CompilerParams(vmem_limit_bytes=4 << 20),
        cost_estimate=pl.CostEstimate(flops=10**8, bytes_accessed=8 << 20, transcendentals=0),
        name="prepare_rows",
    )(pos)


def multiply(field, high, low, dims):
    upper = field.astype(jnp.bfloat16).astype(jnp.float32)
    terms = jnp.concatenate([upper, field - upper], axis=0).astype(jnp.bfloat16)
    dot = functools.partial(
        lax.dot_general, dimension_numbers=dims, preferred_element_type=jnp.float32
    )
    product = dot(terms, high) + dot(terms, low)
    return product[0:8] + product[8:16]


def stage_kernel(stage, sources, table, prepared_ref, row_vec, *refs):
    places = refs[:sources]
    last = stage == LAST_STAGE
    pair_ref, rows_out, col_acc, tile, cols, pair, sems = refs[-7:]
    if stage == 0:
        rows_out[...] = jnp.zeros_like(rows_out)
        col_acc[...] = jnp.zeros_like(col_acc)
    else:
        if not last:
            rows_out[...] = refs[sources + 1][...]
        col_acc[...] = refs[sources + 2][...]

    def copy(slot, buffer):
        return pltpu.make_async_copy(pair.at[buffer], pair_ref.at[slot], sems.at[buffer])

    def form(slot, formed):
        buffer = lax.rem(formed, 2)
        for source in range(sources):

            @pl.when(table[SOURCE, slot] == source)
            def _():
                tile[...] = places[source][table[PLACE, slot]]

        for snapshot in range(16):
            high, mid, low = split3(rows_of(tile, snapshot, 1.0, 3, 4))
            stacked = jnp.concatenate([high, mid, high, mid, low, high], axis=0)
            cols[snapshot] = stacked.astype(jnp.bfloat16)
        row_at = table[ROW_AT, slot]

        @pl.when(formed >= 2)
        def _():
            copy(slot, buffer).wait()

        def step(at, carry):
            part = pl.ds(pl.multiple_of(at * HALF, HALF), HALF)
            total = None
            for snapshot in range(16):
                exponent = jnp.dot(
                    prepared_ref[row_at, snapshot],
                    cols[snapshot, :, part],
                    preferred_element_type=jnp.float32,
                )
                term = jnp.exp2(exponent)
                total = term if total is None else total + term
            high = total.astype(jnp.bfloat16)
            pair[buffer, 0, :, part] = high
            pair[buffer, 1, :, part] = (total - high.astype(jnp.float32)).astype(jnp.bfloat16)
            return carry

        lax.fori_loop(0, TILE // HALF, step, 0)
        copy(slot, buffer).start()
        if last:
            rows_out[slot] = tile[48:56, :]
        else:
            rows_out[table[ROW_NEAR, slot]] += multiply(
                tile[48:56, :], pair[buffer, 0], pair[buffer, 1], BY_COLS
            )

        @pl.when(table[CROSSING, slot] != 0)
        def _():
            col_acc[table[COL_AT, slot]] += multiply(
                row_vec[row_at], pair[buffer, 0], pair[buffer, 1], BY_ROWS
            )

    def visit(slot, formed):
        mine = table[STAGE, slot] == stage

        @pl.when(mine)
        def _():
            form(slot, formed)

        return formed + jnp.where(mine, 1, 0)

    formed = lax.fori_loop(0, pair_ref.shape[0], visit, 0)
    for back in (1, 2):

        @pl.when(formed >= back)
        def _():
            copy(0, lax.rem(formed + back, 2)).wait()


def form_stage(stage, table, prepared, row_vec, places, state, blocks):
    slots = table.shape[1]
    vmem = pl.BlockSpec(memory_space=pltpu.VMEM)
    hbm = pl.BlockSpec(memory_space=pltpu.HBM)
    shapes = [
        pltpu.HBM((slots, 2, TILE, TILE), jnp.bfloat16),
        jax.ShapeDtypeStruct(
            (slots if stage == LAST_STAGE else row_vec.shape[0], 8, TILE), jnp.float32
        ),
        jax.ShapeDtypeStruct((blocks, 8, TILE), jnp.float32),
    ]
    first = 3 + len(places)
    return pl.pallas_call(
        functools.partial(stage_kernel, stage, len(places)),
        in_specs=[pl.BlockSpec(memory_space=pltpu.SMEM)]
        + [vmem] * (2 + len(places))
        + ([hbm, vmem, vmem] if state else []),
        out_specs=[hbm, vmem, vmem],
        out_shape=shapes,
        input_output_aliases={
            first + i: i for i in range(1 if stage == LAST_STAGE else len(state))
        },
        scratch_shapes=[
            pltpu.VMEM((56, TILE), jnp.float32),
            pltpu.VMEM((16, DEPTH, TILE), jnp.bfloat16),
            pltpu.VMEM((2, 2, TILE, TILE), jnp.bfloat16),
            pltpu.SemaphoreType.DMA((2,)),
        ],
        compiler_params=pltpu.CompilerParams(vmem_limit_bytes=8 << 20),
        cost_estimate=pl.CostEstimate(
            flops=8 * 10**9, bytes_accessed=8 << 20, transcendentals=10**7
        ),
        name=f"form_{stage}",
    )(table, prepared, row_vec, *places, *state)


def apply_kernel(wanted, col_at, table, pair_ref, field, *refs):
    acc, pair, sems = refs[-3:]
    slots = pair_ref.shape[0]

    def copy(slot):
        return pltpu.make_async_copy(pair_ref.at[slot], pair.at[slot], sems.at[slot])

    for slot in range(slots):

        @pl.when(table[wanted, slot] != 0)
        def _():
            copy(slot).start()

    acc[...] = jnp.zeros_like(acc) if len(refs) == 3 else refs[0][...]

    def visit(slot, carry):
        @pl.when(table[wanted, slot] != 0)
        def _():
            copy(slot).wait()
            row = table[ROW_NEAR, slot]
            col = slot if col_at is None else table[col_at, slot]
            if wanted != CROSSING:
                acc[row] += multiply(field[col], pair[slot, 0], pair[slot, 1], BY_COLS)
            else:
                acc[col] += multiply(field[row], pair[slot, 0], pair[slot, 1], BY_ROWS)

        return carry

    lax.fori_loop(0, slots, visit, 0)


def apply_tiles(wanted, col_at, name, table, pair, field, count, start=()):
    vmem = pl.BlockSpec(memory_space=pltpu.VMEM)
    hbm = pl.BlockSpec(memory_space=pltpu.HBM)
    return pl.pallas_call(
        functools.partial(apply_kernel, wanted, col_at),
        in_specs=[pl.BlockSpec(memory_space=pltpu.SMEM), hbm, vmem] + [vmem] * len(start),
        out_specs=vmem,
        out_shape=jax.ShapeDtypeStruct((count, 8, TILE), jnp.float32),
        scratch_shapes=[
            pltpu.VMEM(pair.shape, pair.dtype),
            pltpu.SemaphoreType.DMA((pair.shape[0],)),
        ],
        compiler_params=pltpu.CompilerParams(vmem_limit_bytes=16 << 20),
        cost_estimate=pl.CostEstimate(
            flops=3 * 10**9, bytes_accessed=12 << 20, transcendentals=0
        ),
        name=name,
    )(table, in_hbm(pair), field, *start)


def fetch_kernel(table, pair_ref, after, out, sems):
    slots = pair_ref.shape[0]

    def copy(slot):
        return pltpu.make_async_copy(pair_ref.at[slot], out.at[slot], sems.at[slot])

    for slot in range(slots):

        @pl.when(table[CROSSING, slot] != 0)
        def _():
            copy(slot).start()

    for slot in range(slots):

        @pl.when(table[CROSSING, slot] != 0)
        def _():
            copy(slot).wait()


def fetch(table, pair, after):
    vmem = pl.BlockSpec(memory_space=pltpu.VMEM)
    return pl.pallas_call(
        fetch_kernel,
        in_specs=[
            pl.BlockSpec(memory_space=pltpu.SMEM),
            pl.BlockSpec(memory_space=pltpu.HBM),
            vmem,
        ],
        out_specs=vmem,
        out_shape=jax.ShapeDtypeStruct(pair.shape, pair.dtype),
        scratch_shapes=[pltpu.SemaphoreType.DMA((pair.shape[0],))],
        compiler_params=pltpu.CompilerParams(vmem_limit_bytes=2 << 20),
        cost_estimate=pl.CostEstimate(flops=0, bytes_accessed=12 << 20, transcendentals=0),
        name="fetch",
    )(table, in_hbm(pair), after)


def cols_kernel(table, pair, field, acc):
    acc[...] = jnp.zeros_like(acc)

    def visit(slot, carry):
        @pl.when(table[CROSSING, slot] != 0)
        def _():
            acc[table[COL_AT, slot]] += multiply(
                field[table[ROW_SEEN, slot]], pair[slot, 0], pair[slot, 1], BY_ROWS
            )

        return carry

    lax.fori_loop(0, pair.shape[0], visit, 0)


def apply_cols(table, pair, field, count):
    vmem = pl.BlockSpec(memory_space=pltpu.VMEM)
    return pl.pallas_call(
        cols_kernel,
        in_specs=[pl.BlockSpec(memory_space=pltpu.SMEM), vmem, vmem],
        out_specs=vmem,
        out_shape=jax.ShapeDtypeStruct((count, 8, TILE), jnp.float32),
        compiler_params=pltpu.CompilerParams(vmem_limit_bytes=4 << 20),
        cost_estimate=pl.CostEstimate(
            flops=3 * 10**9, bytes_accessed=1 << 20, transcendentals=0
        ),
        name="apply_cols",
    )(table, pair, field)


def shift(value, axis, distance):
    size = lax.axis_size(axis)
    return lax.ppermute(value, axis, [(i, (i + distance) % size) for i in range(size)])


def spread(piece, axes):
    copies = jnp.broadcast_to(piece, (lax.axis_size(axes),) + piece.shape)
    return lax.all_to_all(copies, axes, 0, 0, tiled=True)


def spread_near(both):
    near = [both] + [shift(both, "x", d) for d in range(1, lax.axis_size("x"))]
    return jnp.concatenate(near, axis=0)


def reduce_near(row_acc):
    size = lax.axis_size("x")
    mine = row_acc[:size] + shift(row_acc[size:], "core", 1)
    total = mine[0]
    for d in range(1, size):
        total = total + shift(mine[d], "x", size - d)
    return total


def gather_y(piece):
    return jnp.stack([piece] + [shift(piece, "y", d) for d in range(1, lax.axis_size("y"))])


def gather_z(near):
    size, half = lax.axis_size("z"), near.shape[0] // 2
    arrived = [[near]]
    behind = ahead = near
    for distance in range(1, size // 2 + 1):
        if distance == size // 2:
            behind, ahead = behind[:half], ahead[half:]
        behind, ahead = shift(behind, "z", 1), shift(ahead, "z", size - 1)
        arrived.append([behind, ahead])
    return arrived


def table_kernel(pairs, valid, sizes, out):
    size_z, size_y, size_x, tiles = sizes
    z, y = lax.axis_index("z"), lax.axis_index("y")
    x, core = lax.axis_index("x"), lax.axis_index("core")
    slots = out.shape[1]
    arrival, keys = [], []
    for slot in range(slots):
        row, col, live = pairs[0, slot], pairs[1, slot], valid[0, slot] != 0
        behind = lax.rem(z - col // size_y + size_z, size_z)
        place = lax.rem(y - lax.rem(col, size_y) + size_y, size_y)
        upper = place >= size_y // 2
        far = jnp.where(upper, size_z, size_z - 1)
        source = jnp.where(behind < size_z // 2, 2 * behind - 1, 2 * (size_z - behind))
        source = jnp.where(behind == size_z // 2, far, source)
        source = jnp.where(behind == 0, 0, source)
        place = jnp.where((behind == size_z // 2) & upper, place - size_y // 2, place)
        crossing = ((z * size_y + y) * tiles + row) != (col * tiles + 2 * x + core)
        other = jnp.where(lax.rem(row, 2) == core, 0, 1)
        along = lax.rem(x - row // 2 + size_x, size_x)
        out[ROW_AT, slot] = row
        out[ROW_NEAR, slot] = other * size_x + along
        out[ROW_SEEN, slot] = 2 * along + other
        out[COL_AT, slot] = col
        out[SOURCE, slot] = source
        out[PLACE, slot] = place
        out[LIVE, slot] = jnp.where(live, 1, 0)
        out[CROSSING, slot] = jnp.where(live & crossing, 1, 0)
        stage = jnp.where(live, (source + 1) // 2, LAST_STAGE)
        arrival.append(jnp.maximum(PER_STAGE * stage - 1, 0))
        keys.append(stage * slots + slot)
    ranks = [
        sum(jnp.where(other <= key, 1, 0) for other in keys) for key in keys
    ]
    for slot in range(slots):
        turn = arrival[slot]
        for other in range(slots):
            if other != slot:
                wait = arrival[other] + ranks[slot] - ranks[other]
                turn = jnp.maximum(turn, jnp.where(keys[other] <= keys[slot], wait, 0))
        stage = jnp.minimum((turn + 1) // PER_STAGE, LAST_STAGE)
        live = valid[0, slot] != 0
        out[STAGE, slot] = jnp.where(live, stage, -1)
        out[LATE, slot] = jnp.where(live & (stage == LAST_STAGE), 1, 0)


def slot_table(pairs, valid, sizes):
    smem = pl.BlockSpec(memory_space=pltpu.SMEM)

    def kernel(pairs_ref, valid_ref, out_ref):
        table_kernel(pairs_ref, valid_ref, sizes, out_ref)

    return pl.pallas_call(
        kernel,
        in_specs=[smem, smem],
        out_specs=smem,
        out_shape=jax.ShapeDtypeStruct((10, pairs.shape[1]), jnp.int32),
        name="slot_table",
    )(pairs, valid)


def combine(row_acc, col_acc):
    by_col = lax.all_to_all(col_acc, ROW, 0, 0, tiled=True)
    return reduce_near(row_acc) + jnp.sum(by_col, axis=0)


def per_device(positions, vectors, pairs, valid):
    grid_col = lax.axis_index(COL)
    block = positions.shape[2]
    tiles = block // TILE
    blocks = lax.axis_size(ROW)
    sizes = (lax.axis_size("z"), lax.axis_size("y"), lax.axis_size("x"), tiles)
    table = slot_table(pairs[0, 0].transpose(1, 0), valid[0], sizes)

    flat = positions.transpose(1, 0, 2).reshape(48, block)
    own = lax.dynamic_slice_in_dim(
        jnp.concatenate([flat, vectors], axis=0), grid_col * TILE, TILE, 1
    )
    row_vec = vectors.reshape(8, tiles, TILE).transpose(1, 0, 2)
    near = gather_y(own)
    flat, near = lax.optimization_barrier((flat, near))
    prepared = prepare_rows(flat)
    places, state = [], []
    for stage, arrived in enumerate(gather_z(near)):
        places = places + arrived
        early = state
        state = form_stage(stage, table, prepared, row_vec, places, state, blocks)
    pair, slot_vec, col_acc = state
    row_acc = apply_tiles(
        LATE, None, "apply_late", table, pair, slot_vec, tiles, (early[1],)
    )
    first = combine(row_acc, col_acc)

    col_vec = spread(first, ROW)
    both = jnp.stack([first, shift(first, "core", 1)])
    tiles_here = fetch(table, pair, both)
    col_acc = apply_cols(table, tiles_here, spread_near(both), blocks)
    row_acc = apply_tiles(LIVE, COL_AT, "apply_rows", table, pair, col_vec, tiles)
    second = combine(row_acc, col_acc)

    rows = spread(second, COL)
    squares = jnp.sum(rows * rows, axis=(0, 2))
    squares = spread(jnp.pad(squares[None, :], ((0, 0), (0, 120))), ROW)
    total = jnp.sum(squares[:, 0, :8], axis=0) / (block * blocks)
    scaled = rows / jnp.sqrt(total + 1e-06)[None, :, None]
    return scaled.transpose(1, 0, 2).reshape(8, block)


def solution(mesh):
    physical = Mesh(mesh.devices.reshape(8, 4, 4, 2), ("z", "y", "x", "core"))
    placed = (
        P(None, None, ROW),
        P(None, ROW),
        P(ROW, COL, None, None),
        P(ROW, COL, None),
    )
    return jax.shard_map(
        per_device, mesh=physical, in_specs=placed, out_specs=P(None, ROW), check_vma=False
    )
```

```python
import functools
import math

import jax
import jax.numpy as jnp
from jax import lax
from jax.experimental import pallas as pl
from jax.experimental.pallas import tpu as pltpu
from jax.sharding import Mesh
from jax.sharding import PartitionSpec as P

TILE = 512
ROW = ("z", "y")
COL = ("x", "core")
ROW_AT, ROW_NEAR, COL_AT, SOURCE, PLACE, STAGE, LIVE, CROSSING, LATE = range(9)
LAST_STAGE = 4
PER_STAGE = 2
BY_ROWS = (((1,), (0,)), ((), ()))
BY_COLS = (((1,), (1,)), ((), ()))
LOG2E = math.log2(math.e)
GROUPS = 6
DEPTH = 8 * GROUPS
HALF = 256


def in_hbm(value):
    return pltpu.with_memory_space_constraint(value, pltpu.HBM)


def split3(value):
    high = value.astype(jnp.bfloat16).astype(jnp.float32)
    rest = value - high
    mid = rest.astype(jnp.bfloat16).astype(jnp.float32)
    return high, mid, rest - mid


def rows_of(ref, snapshot, scale, norm_at, one_at):
    width = ref.shape[-1]
    place = lax.broadcasted_iota(jnp.int32, (8, width), 0)
    parts = [
        jnp.broadcast_to(ref[16 * q + snapshot : 16 * q + snapshot + 1, :], (8, width))
        for q in range(3)
    ]
    norm = (-0.5 * LOG2E) * (parts[0] * parts[0] + parts[1] * parts[1] + parts[2] * parts[2])
    out = jnp.where(place == norm_at, norm, jnp.where(place == one_at, 1.0, 0.0))
    for q in range(3):
        out = jnp.where(place == q, parts[q] * scale if scale != 1.0 else parts[q], out)
    return out


def prepare_kernel(pos_ref, out_ref):
    def visit(tile, carry):
        part = pos_ref.at[:, pl.ds(pl.multiple_of(tile * TILE, TILE), TILE)]
        for snapshot in range(16):
            high, mid, low = split3(rows_of(part, snapshot, LOG2E, 4, 3))
            stacked = jnp.concatenate([high, high, mid, mid, high, low], axis=0)
            out_ref[tile, snapshot] = stacked.T.astype(jnp.bfloat16)
        return carry

    lax.fori_loop(0, out_ref.shape[0], visit, 0)


def prepare_rows(pos):
    tiles = pos.shape[1] // TILE
    vmem = pl.BlockSpec(memory_space=pltpu.VMEM)
    return pl.pallas_call(
        prepare_kernel,
        in_specs=[vmem],
        out_specs=vmem,
        out_shape=jax.ShapeDtypeStruct((tiles, 16, TILE, DEPTH), jnp.bfloat16),
        compiler_params=pltpu.CompilerParams(vmem_limit_bytes=4 << 20),
        cost_estimate=pl.CostEstimate(flops=10**8, bytes_accessed=8 << 20, transcendentals=0),
        name="prepare_rows",
    )(pos)


def multiply(field, high, low, dims):
    terms = jnp.concatenate(split3(field), axis=0).astype(jnp.bfloat16)
    dot = functools.partial(
        lax.dot_general, dimension_numbers=dims, preferred_element_type=jnp.float32
    )
    by_high = dot(terms, high)
    by_low = dot(terms[:16], low)
    return (by_high[0:8] + by_low[0:8]) + (by_high[8:16] + by_low[8:16]) + by_high[16:24]


def stage_kernel(stage, sources, table, prepared_ref, row_vec, *refs):
    places = refs[:sources]
    last = stage == LAST_STAGE
    pair_ref, rows_out, col_acc, tile, cols, pair, sems = refs[-7:]
    if stage == 0:
        rows_out[...] = jnp.zeros_like(rows_out)
        col_acc[...] = jnp.zeros_like(col_acc)
    else:
        if not last:
            rows_out[...] = refs[sources + 1][...]
        col_acc[...] = refs[sources + 2][...]

    def copy(slot, buffer):
        return pltpu.make_async_copy(pair.at[buffer], pair_ref.at[slot], sems.at[buffer])

    def form(slot, formed):
        buffer = lax.rem(formed, 2)
        for source in range(sources):

            @pl.when(table[SOURCE, slot] == source)
            def _():
                tile[...] = places[source][table[PLACE, slot]]

        for snapshot in range(16):
            high, mid, low = split3(rows_of(tile, snapshot, 1.0, 3, 4))
            stacked = jnp.concatenate([high, mid, high, mid, low, high], axis=0)
            cols[snapshot] = stacked.astype(jnp.bfloat16)
        row_at = table[ROW_AT, slot]

        @pl.when(formed >= 2)
        def _():
            copy(slot, buffer).wait()

        def step(at, carry):
            part = pl.ds(pl.multiple_of(at * HALF, HALF), HALF)
            total = None
            for snapshot in range(16):
                exponent = jnp.dot(
                    prepared_ref[row_at, snapshot],
                    cols[snapshot, :, part],
                    preferred_element_type=jnp.float32,
                )
                term = jnp.exp2(exponent)
                total = term if total is None else total + term
            high = total.astype(jnp.bfloat16)
            pair[buffer, 0, :, part] = high
            pair[buffer, 1, :, part] = (total - high.astype(jnp.float32)).astype(jnp.bfloat16)
            return carry

        lax.fori_loop(0, TILE // HALF, step, 0)
        copy(slot, buffer).start()
        if last:
            rows_out[slot] = tile[48:56, :]
        else:
            rows_out[table[ROW_NEAR, slot]] += multiply(
                tile[48:56, :], pair[buffer, 0], pair[buffer, 1], BY_COLS
            )

        @pl.when(table[CROSSING, slot] != 0)
        def _():
            col_acc[table[COL_AT, slot]] += multiply(
                row_vec[row_at], pair[buffer, 0], pair[buffer, 1], BY_ROWS
            )

    def visit(slot, formed):
        mine = table[STAGE, slot] == stage

        @pl.when(mine)
        def _():
            form(slot, formed)

        return formed + jnp.where(mine, 1, 0)

    formed = lax.fori_loop(0, pair_ref.shape[0], visit, 0)
    for back in (1, 2):

        @pl.when(formed >= back)
        def _():
            copy(0, lax.rem(formed + back, 2)).wait()


def form_stage(stage, table, prepared, row_vec, places, state, blocks):
    slots = table.shape[1]
    vmem = pl.BlockSpec(memory_space=pltpu.VMEM)
    hbm = pl.BlockSpec(memory_space=pltpu.HBM)
    shapes = [
        pltpu.HBM((slots, 2, TILE, TILE), jnp.bfloat16),
        jax.ShapeDtypeStruct(
            (slots if stage == LAST_STAGE else row_vec.shape[0], 8, TILE), jnp.float32
        ),
        jax.ShapeDtypeStruct((blocks, 8, TILE), jnp.float32),
    ]
    first = 3 + len(places)
    return pl.pallas_call(
        functools.partial(stage_kernel, stage, len(places)),
        in_specs=[pl.BlockSpec(memory_space=pltpu.SMEM)]
        + [vmem] * (2 + len(places))
        + ([hbm, vmem, vmem] if state else []),
        out_specs=[hbm, vmem, vmem],
        out_shape=shapes,
        input_output_aliases={
            first + i: i for i in range(1 if stage == LAST_STAGE else len(state))
        },
        scratch_shapes=[
            pltpu.VMEM((56, TILE), jnp.float32),
            pltpu.VMEM((16, DEPTH, TILE), jnp.bfloat16),
            pltpu.VMEM((2, 2, TILE, TILE), jnp.bfloat16),
            pltpu.SemaphoreType.DMA((2,)),
        ],
        compiler_params=pltpu.CompilerParams(vmem_limit_bytes=8 << 20),
        cost_estimate=pl.CostEstimate(
            flops=8 * 10**9, bytes_accessed=8 << 20, transcendentals=10**7
        ),
        name=f"form_{stage}",
    )(table, prepared, row_vec, *places, *state)


def apply_kernel(wanted, col_at, table, pair_ref, field, *refs):
    acc, pair, sems = refs[-3:]
    slots = pair_ref.shape[0]

    def copy(slot):
        return pltpu.make_async_copy(pair_ref.at[slot], pair.at[slot], sems.at[slot])

    for slot in range(slots):

        @pl.when(table[wanted, slot] != 0)
        def _():
            copy(slot).start()

    acc[...] = jnp.zeros_like(acc) if len(refs) == 3 else refs[0][...]

    def visit(slot, carry):
        @pl.when(table[wanted, slot] != 0)
        def _():
            copy(slot).wait()
            row = table[ROW_NEAR, slot]
            col = slot if col_at is None else table[col_at, slot]
            if wanted != CROSSING:
                acc[row] += multiply(field[col], pair[slot, 0], pair[slot, 1], BY_COLS)
            else:
                acc[col] += multiply(field[row], pair[slot, 0], pair[slot, 1], BY_ROWS)

        return carry

    lax.fori_loop(0, slots, visit, 0)


def apply_tiles(wanted, col_at, name, table, pair, field, count, start=()):
    vmem = pl.BlockSpec(memory_space=pltpu.VMEM)
    hbm = pl.BlockSpec(memory_space=pltpu.HBM)
    return pl.pallas_call(
        functools.partial(apply_kernel, wanted, col_at),
        in_specs=[pl.BlockSpec(memory_space=pltpu.SMEM), hbm, vmem] + [vmem] * len(start),
        out_specs=vmem,
        out_shape=jax.ShapeDtypeStruct((count, 8, TILE), jnp.float32),
        scratch_shapes=[
            pltpu.VMEM(pair.shape, pair.dtype),
            pltpu.SemaphoreType.DMA((pair.shape[0],)),
        ],
        compiler_params=pltpu.CompilerParams(vmem_limit_bytes=16 << 20),
        cost_estimate=pl.CostEstimate(
            flops=3 * 10**9, bytes_accessed=12 << 20, transcendentals=0
        ),
        name=name,
    )(table, in_hbm(pair), field, *start)


def shift(value, axis, distance):
    size = lax.axis_size(axis)
    return lax.ppermute(value, axis, [(i, (i + distance) % size) for i in range(size)])


def spread(piece, axes):
    copies = jnp.broadcast_to(piece, (lax.axis_size(axes),) + piece.shape)
    return lax.all_to_all(copies, axes, 0, 0, tiled=True)


def spread_near(piece):
    both = jnp.stack([piece, shift(piece, "core", 1)])
    near = [both] + [shift(both, "x", d) for d in range(1, lax.axis_size("x"))]
    return jnp.stack(near, axis=1).reshape(2 * len(near), *piece.shape)


def reduce_near(row_acc):
    size = lax.axis_size("x")
    mine = row_acc[:size] + shift(row_acc[size:], "core", 1)
    total = mine[0]
    for d in range(1, size):
        total = total + shift(mine[d], "x", size - d)
    return total


def gather_y(piece):
    return jnp.stack([piece] + [shift(piece, "y", d) for d in range(1, lax.axis_size("y"))])


def gather_z(near):
    size, half = lax.axis_size("z"), near.shape[0] // 2
    arrived = [[near]]
    behind = ahead = near
    for distance in range(1, size // 2 + 1):
        if distance == size // 2:
            behind, ahead = behind[:half], ahead[half:]
        behind, ahead = shift(behind, "z", 1), shift(ahead, "z", size - 1)
        arrived.append([behind, ahead])
    return arrived


def table_kernel(pairs, valid, sizes, out):
    size_z, size_y, size_x, tiles = sizes
    z, y = lax.axis_index("z"), lax.axis_index("y")
    x, core = lax.axis_index("x"), lax.axis_index("core")
    slots = out.shape[1]
    arrival, keys = [], []
    for slot in range(slots):
        row, col, live = pairs[0, slot], pairs[1, slot], valid[0, slot] != 0
        behind = lax.rem(z - col // size_y + size_z, size_z)
        place = lax.rem(y - lax.rem(col, size_y) + size_y, size_y)
        upper = place >= size_y // 2
        far = jnp.where(upper, size_z, size_z - 1)
        source = jnp.where(behind < size_z // 2, 2 * behind - 1, 2 * (size_z - behind))
        source = jnp.where(behind == size_z // 2, far, source)
        source = jnp.where(behind == 0, 0, source)
        place = jnp.where((behind == size_z // 2) & upper, place - size_y // 2, place)
        crossing = ((z * size_y + y) * tiles + row) != (col * tiles + 2 * x + core)
        near = jnp.where(lax.rem(row, 2) == core, 0, size_x)
        near = near + lax.rem(x - row // 2 + size_x, size_x)
        out[ROW_AT, slot] = row
        out[ROW_NEAR, slot] = near
        out[COL_AT, slot] = col
        out[SOURCE, slot] = source
        out[PLACE, slot] = place
        out[LIVE, slot] = jnp.where(live, 1, 0)
        out[CROSSING, slot] = jnp.where(live & crossing, 1, 0)
        stage = jnp.where(live, (source + 1) // 2, LAST_STAGE)
        arrival.append(jnp.maximum(PER_STAGE * stage - 1, 0))
        keys.append(stage * slots + slot)
    ranks = [
        sum(jnp.where(other <= key, 1, 0) for other in keys) for key in keys
    ]
    for slot in range(slots):
        turn = arrival[slot]
        for other in range(slots):
            if other != slot:
                wait = arrival[other] + ranks[slot] - ranks[other]
                turn = jnp.maximum(turn, jnp.where(keys[other] <= keys[slot], wait, 0))
        stage = jnp.minimum((turn + 1) // PER_STAGE, LAST_STAGE)
        live = valid[0, slot] != 0
        out[STAGE, slot] = jnp.where(live, stage, -1)
        out[LATE, slot] = jnp.where(live & (stage == LAST_STAGE), 1, 0)


def slot_table(pairs, valid, sizes):
    smem = pl.BlockSpec(memory_space=pltpu.SMEM)

    def kernel(pairs_ref, valid_ref, out_ref):
        table_kernel(pairs_ref, valid_ref, sizes, out_ref)

    return pl.pallas_call(
        kernel,
        in_specs=[smem, smem],
        out_specs=smem,
        out_shape=jax.ShapeDtypeStruct((9, pairs.shape[1]), jnp.int32),
        name="slot_table",
    )(pairs, valid)


def combine(row_acc, col_acc):
    by_col = lax.all_to_all(col_acc, ROW, 0, 0, tiled=True)
    return reduce_near(row_acc) + jnp.sum(by_col, axis=0)


def per_device(positions, vectors, pairs, valid):
    grid_col = lax.axis_index(COL)
    block = positions.shape[2]
    tiles = block // TILE
    blocks = lax.axis_size(ROW)
    sizes = (lax.axis_size("z"), lax.axis_size("y"), lax.axis_size("x"), tiles)
    table = slot_table(pairs[0, 0].transpose(1, 0), valid[0], sizes)

    flat = positions.transpose(1, 0, 2).reshape(48, block)
    own = lax.dynamic_slice_in_dim(
        jnp.concatenate([flat, vectors], axis=0), grid_col * TILE, TILE, 1
    )
    row_vec = vectors.reshape(8, tiles, TILE).transpose(1, 0, 2)
    near = gather_y(own)
    flat, near = lax.optimization_barrier((flat, near))
    prepared = prepare_rows(flat)
    places, state = [], []
    for stage, arrived in enumerate(gather_z(near)):
        places = places + arrived
        early = state
        state = form_stage(stage, table, prepared, row_vec, places, state, blocks)
    pair, slot_vec, col_acc = state
    row_acc = apply_tiles(
        LATE, None, "apply_late", table, pair, slot_vec, tiles, (early[1],)
    )
    first = combine(row_acc, col_acc)

    col_vec = spread(first, ROW)
    col_acc = apply_tiles(CROSSING, COL_AT, "apply_cols", table, pair, spread_near(first), blocks)
    row_acc = apply_tiles(LIVE, COL_AT, "apply_rows", table, pair, col_vec, tiles)
    second = combine(row_acc, col_acc)

    rows = spread(second, COL)
    squares = jnp.sum(rows * rows, axis=(0, 2))
    squares = spread(jnp.pad(squares[None, :], ((0, 0), (0, 120))), ROW)
    total = jnp.sum(squares[:, 0, :8], axis=0) / (block * blocks)
    scaled = rows / jnp.sqrt(total + 1e-06)[None, :, None]
    return scaled.transpose(1, 0, 2).reshape(8, block)


def solution(mesh):
    physical = Mesh(mesh.devices.reshape(8, 4, 4, 2), ("z", "y", "x", "core"))
    placed = (
        P(None, None, ROW),
        P(None, ROW),
        P(ROW, COL, None, None),
        P(ROW, COL, None),
    )
    return jax.shard_map(
        per_device, mesh=physical, in_specs=placed, out_specs=P(None, ROW), check_vma=False
    )
```

```python
import functools
import math

import jax
import jax.numpy as jnp
from jax import lax
from jax.experimental import pallas as pl
from jax.experimental.pallas import tpu as pltpu
from jax.sharding import Mesh
from jax.sharding import PartitionSpec as P

TILE = 512
ROW = ("z", "y")
COL = ("x", "core")
ROW_AT, ROW_NEAR, COL_AT, SOURCE, PLACE, STAGE, LIVE, CROSSING, LATE, ROW_SEEN = range(10)
LAST_STAGE = 4
PER_STAGE = 2
BY_ROWS = (((1,), (0,)), ((), ()))
BY_COLS = (((1,), (1,)), ((), ()))
LOG2E = math.log2(math.e)
GROUPS = 6
DEPTH = 8 * GROUPS
HALF = 256


def in_hbm(value):
    return pltpu.with_memory_space_constraint(value, pltpu.HBM)


def split3(value):
    high = value.astype(jnp.bfloat16).astype(jnp.float32)
    rest = value - high
    mid = rest.astype(jnp.bfloat16).astype(jnp.float32)
    return high, mid, rest - mid


def rows_of(ref, snapshot, scale, norm_at, one_at):
    width = ref.shape[-1]
    place = lax.broadcasted_iota(jnp.int32, (8, width), 0)
    parts = [
        jnp.broadcast_to(ref[16 * q + snapshot : 16 * q + snapshot + 1, :], (8, width))
        for q in range(3)
    ]
    norm = (-0.5 * LOG2E) * (parts[0] * parts[0] + parts[1] * parts[1] + parts[2] * parts[2])
    out = jnp.where(place == norm_at, norm, jnp.where(place == one_at, 1.0, 0.0))
    for q in range(3):
        out = jnp.where(place == q, parts[q] * scale if scale != 1.0 else parts[q], out)
    return out


def prepare_kernel(pos_ref, out_ref):
    def visit(tile, carry):
        part = pos_ref.at[:, pl.ds(pl.multiple_of(tile * TILE, TILE), TILE)]
        for snapshot in range(16):
            high, mid, low = split3(rows_of(part, snapshot, LOG2E, 4, 3))
            stacked = jnp.concatenate([high, high, mid, mid, high, low], axis=0)
            out_ref[tile, snapshot] = stacked.T.astype(jnp.bfloat16)
        return carry

    lax.fori_loop(0, out_ref.shape[0], visit, 0)


def prepare_rows(pos):
    tiles = pos.shape[1] // TILE
    vmem = pl.BlockSpec(memory_space=pltpu.VMEM)
    return pl.pallas_call(
        prepare_kernel,
        in_specs=[vmem],
        out_specs=vmem,
        out_shape=jax.ShapeDtypeStruct((tiles, 16, TILE, DEPTH), jnp.bfloat16),
        compiler_params=pltpu.CompilerParams(vmem_limit_bytes=4 << 20),
        cost_estimate=pl.CostEstimate(flops=10**8, bytes_accessed=8 << 20, transcendentals=0),
        name="prepare_rows",
    )(pos)


def multiply(field, high, low, dims):
    terms = jnp.concatenate(split3(field), axis=0).astype(jnp.bfloat16)
    dot = functools.partial(
        lax.dot_general, dimension_numbers=dims, preferred_element_type=jnp.float32
    )
    by_high = dot(terms, high)
    by_low = dot(terms[:16], low)
    return (by_high[0:8] + by_low[0:8]) + (by_high[8:16] + by_low[8:16]) + by_high[16:24]


def stage_kernel(stage, sources, table, prepared_ref, row_vec, *refs):
    places = refs[:sources]
    last = stage == LAST_STAGE
    pair_ref, rows_out, col_acc, tile, cols, pair, sems = refs[-7:]
    if stage == 0:
        rows_out[...] = jnp.zeros_like(rows_out)
        col_acc[...] = jnp.zeros_like(col_acc)
    else:
        if not last:
            rows_out[...] = refs[sources + 1][...]
        col_acc[...] = refs[sources + 2][...]

    def copy(slot, buffer):
        return pltpu.make_async_copy(pair.at[buffer], pair_ref.at[slot], sems.at[buffer])

    def form(slot, formed):
        buffer = lax.rem(formed, 2)
        for source in range(sources):

            @pl.when(table[SOURCE, slot] == source)
            def _():
                tile[...] = places[source][table[PLACE, slot]]

        for snapshot in range(16):
            high, mid, low = split3(rows_of(tile, snapshot, 1.0, 3, 4))
            stacked = jnp.concatenate([high, mid, high, mid, low, high], axis=0)
            cols[snapshot] = stacked.astype(jnp.bfloat16)
        row_at = table[ROW_AT, slot]

        @pl.when(formed >= 2)
        def _():
            copy(slot, buffer).wait()

        def step(at, carry):
            part = pl.ds(pl.multiple_of(at * HALF, HALF), HALF)
            total = None
            for snapshot in range(16):
                exponent = jnp.dot(
                    prepared_ref[row_at, snapshot],
                    cols[snapshot, :, part],
                    preferred_element_type=jnp.float32,
                )
                term = jnp.exp2(exponent)
                total = term if total is None else total + term
            high = total.astype(jnp.bfloat16)
            pair[buffer, 0, :, part] = high
            pair[buffer, 1, :, part] = (total - high.astype(jnp.float32)).astype(jnp.bfloat16)
            return carry

        lax.fori_loop(0, TILE // HALF, step, 0)
        copy(slot, buffer).start()
        if last:
            rows_out[slot] = tile[48:56, :]
        else:
            rows_out[table[ROW_NEAR, slot]] += multiply(
                tile[48:56, :], pair[buffer, 0], pair[buffer, 1], BY_COLS
            )

        @pl.when(table[CROSSING, slot] != 0)
        def _():
            col_acc[table[COL_AT, slot]] += multiply(
                row_vec[row_at], pair[buffer, 0], pair[buffer, 1], BY_ROWS
            )

    def visit(slot, formed):
        mine = table[STAGE, slot] == stage

        @pl.when(mine)
        def _():
            form(slot, formed)

        return formed + jnp.where(mine, 1, 0)

    formed = lax.fori_loop(0, pair_ref.shape[0], visit, 0)
    for back in (1, 2):

        @pl.when(formed >= back)
        def _():
            copy(0, lax.rem(formed + back, 2)).wait()


def form_stage(stage, table, prepared, row_vec, places, state, blocks):
    slots = table.shape[1]
    vmem = pl.BlockSpec(memory_space=pltpu.VMEM)
    hbm = pl.BlockSpec(memory_space=pltpu.HBM)
    shapes = [
        pltpu.HBM((slots, 2, TILE, TILE), jnp.bfloat16),
        jax.ShapeDtypeStruct(
            (slots if stage == LAST_STAGE else row_vec.shape[0], 8, TILE), jnp.float32
        ),
        jax.ShapeDtypeStruct((blocks, 8, TILE), jnp.float32),
    ]
    first = 3 + len(places)
    return pl.pallas_call(
        functools.partial(stage_kernel, stage, len(places)),
        in_specs=[pl.BlockSpec(memory_space=pltpu.SMEM)]
        + [vmem] * (2 + len(places))
        + ([hbm, vmem, vmem] if state else []),
        out_specs=[hbm, vmem, vmem],
        out_shape=shapes,
        input_output_aliases={
            first + i: i for i in range(1 if stage == LAST_STAGE else len(state))
        },
        scratch_shapes=[
            pltpu.VMEM((56, TILE), jnp.float32),
            pltpu.VMEM((16, DEPTH, TILE), jnp.bfloat16),
            pltpu.VMEM((2, 2, TILE, TILE), jnp.bfloat16),
            pltpu.SemaphoreType.DMA((2,)),
        ],
        compiler_params=pltpu.CompilerParams(vmem_limit_bytes=8 << 20),
        cost_estimate=pl.CostEstimate(
            flops=8 * 10**9, bytes_accessed=8 << 20, transcendentals=10**7
        ),
        name=f"form_{stage}",
    )(table, prepared, row_vec, *places, *state)


def apply_kernel(wanted, col_at, table, pair_ref, field, *refs):
    acc, pair, sems = refs[-3:]
    slots = pair_ref.shape[0]

    def copy(slot):
        return pltpu.make_async_copy(pair_ref.at[slot], pair.at[slot], sems.at[slot])

    for slot in range(slots):

        @pl.when(table[wanted, slot] != 0)
        def _():
            copy(slot).start()

    acc[...] = jnp.zeros_like(acc) if len(refs) == 3 else refs[0][...]

    def visit(slot, carry):
        @pl.when(table[wanted, slot] != 0)
        def _():
            copy(slot).wait()
            row = table[ROW_SEEN if wanted == CROSSING else ROW_NEAR, slot]
            col = slot if col_at is None else table[col_at, slot]
            if wanted != CROSSING:
                acc[row] += multiply(field[col], pair[slot, 0], pair[slot, 1], BY_COLS)
            else:
                acc[col] += multiply(field[row], pair[slot, 0], pair[slot, 1], BY_ROWS)

        return carry

    lax.fori_loop(0, slots, visit, 0)


def apply_tiles(wanted, col_at, name, table, pair, field, count, start=()):
    vmem = pl.BlockSpec(memory_space=pltpu.VMEM)
    hbm = pl.BlockSpec(memory_space=pltpu.HBM)
    return pl.pallas_call(
        functools.partial(apply_kernel, wanted, col_at),
        in_specs=[pl.BlockSpec(memory_space=pltpu.SMEM), hbm, vmem] + [vmem] * len(start),
        out_specs=vmem,
        out_shape=jax.ShapeDtypeStruct((count, 8, TILE), jnp.float32),
        scratch_shapes=[
            pltpu.VMEM(pair.shape, pair.dtype),
            pltpu.SemaphoreType.DMA((pair.shape[0],)),
        ],
        compiler_params=pltpu.CompilerParams(vmem_limit_bytes=16 << 20),
        cost_estimate=pl.CostEstimate(
            flops=3 * 10**9, bytes_accessed=12 << 20, transcendentals=0
        ),
        name=name,
    )(table, in_hbm(pair), field, *start)


def shift(value, axis, distance):
    size = lax.axis_size(axis)
    return lax.ppermute(value, axis, [(i, (i + distance) % size) for i in range(size)])


def spread(piece, axes):
    copies = jnp.broadcast_to(piece, (lax.axis_size(axes),) + piece.shape)
    return lax.all_to_all(copies, axes, 0, 0, tiled=True)


def spread_near(piece):
    both = jnp.stack([piece, shift(piece, "core", 1)])
    near = [both] + [shift(both, "x", d) for d in range(1, lax.axis_size("x"))]
    return jnp.concatenate(near, axis=0)


def reduce_near(row_acc):
    size = lax.axis_size("x")
    mine = row_acc[:size] + shift(row_acc[size:], "core", 1)
    total = mine[0]
    for d in range(1, size):
        total = total + shift(mine[d], "x", size - d)
    return total


def gather_y(piece):
    return jnp.stack([piece] + [shift(piece, "y", d) for d in range(1, lax.axis_size("y"))])


def gather_z(near):
    size, half = lax.axis_size("z"), near.shape[0] // 2
    arrived = [[near]]
    behind = ahead = near
    for distance in range(1, size // 2 + 1):
        if distance == size // 2:
            behind, ahead = behind[:half], ahead[half:]
        behind, ahead = shift(behind, "z", 1), shift(ahead, "z", size - 1)
        arrived.append([behind, ahead])
    return arrived


def table_kernel(pairs, valid, sizes, out):
    size_z, size_y, size_x, tiles = sizes
    z, y = lax.axis_index("z"), lax.axis_index("y")
    x, core = lax.axis_index("x"), lax.axis_index("core")
    slots = out.shape[1]
    arrival, keys = [], []
    for slot in range(slots):
        row, col, live = pairs[0, slot], pairs[1, slot], valid[0, slot] != 0
        behind = lax.rem(z - col // size_y + size_z, size_z)
        place = lax.rem(y - lax.rem(col, size_y) + size_y, size_y)
        upper = place >= size_y // 2
        far = jnp.where(upper, size_z, size_z - 1)
        source = jnp.where(behind < size_z // 2, 2 * behind - 1, 2 * (size_z - behind))
        source = jnp.where(behind == size_z // 2, far, source)
        source = jnp.where(behind == 0, 0, source)
        place = jnp.where((behind == size_z // 2) & upper, place - size_y // 2, place)
        crossing = ((z * size_y + y) * tiles + row) != (col * tiles + 2 * x + core)
        other = jnp.where(lax.rem(row, 2) == core, 0, 1)
        along = lax.rem(x - row // 2 + size_x, size_x)
        out[ROW_AT, slot] = row
        out[ROW_NEAR, slot] = other * size_x + along
        out[ROW_SEEN, slot] = 2 * along + other
        out[COL_AT, slot] = col
        out[SOURCE, slot] = source
        out[PLACE, slot] = place
        out[LIVE, slot] = jnp.where(live, 1, 0)
        out[CROSSING, slot] = jnp.where(live & crossing, 1, 0)
        stage = jnp.where(live, (source + 1) // 2, LAST_STAGE)
        arrival.append(jnp.maximum(PER_STAGE * stage - 1, 0))
        keys.append(stage * slots + slot)
    ranks = [
        sum(jnp.where(other <= key, 1, 0) for other in keys) for key in keys
    ]
    for slot in range(slots):
        turn = arrival[slot]
        for other in range(slots):
            if other != slot:
                wait = arrival[other] + ranks[slot] - ranks[other]
                turn = jnp.maximum(turn, jnp.where(keys[other] <= keys[slot], wait, 0))
        stage = jnp.minimum((turn + 1) // PER_STAGE, LAST_STAGE)
        live = valid[0, slot] != 0
        out[STAGE, slot] = jnp.where(live, stage, -1)
        out[LATE, slot] = jnp.where(live & (stage == LAST_STAGE), 1, 0)


def slot_table(pairs, valid, sizes):
    smem = pl.BlockSpec(memory_space=pltpu.SMEM)

    def kernel(pairs_ref, valid_ref, out_ref):
        table_kernel(pairs_ref, valid_ref, sizes, out_ref)

    return pl.pallas_call(
        kernel,
        in_specs=[smem, smem],
        out_specs=smem,
        out_shape=jax.ShapeDtypeStruct((10, pairs.shape[1]), jnp.int32),
        name="slot_table",
    )(pairs, valid)


def combine(row_acc, col_acc):
    by_col = lax.all_to_all(col_acc, ROW, 0, 0, tiled=True)
    return reduce_near(row_acc) + jnp.sum(by_col, axis=0)


def per_device(positions, vectors, pairs, valid):
    grid_col = lax.axis_index(COL)
    block = positions.shape[2]
    tiles = block // TILE
    blocks = lax.axis_size(ROW)
    sizes = (lax.axis_size("z"), lax.axis_size("y"), lax.axis_size("x"), tiles)
    table = slot_table(pairs[0, 0].transpose(1, 0), valid[0], sizes)

    flat = positions.transpose(1, 0, 2).reshape(48, block)
    own = lax.dynamic_slice_in_dim(
        jnp.concatenate([flat, vectors], axis=0), grid_col * TILE, TILE, 1
    )
    row_vec = vectors.reshape(8, tiles, TILE).transpose(1, 0, 2)
    near = gather_y(own)
    flat, near = lax.optimization_barrier((flat, near))
    prepared = prepare_rows(flat)
    places, state = [], []
    for stage, arrived in enumerate(gather_z(near)):
        places = places + arrived
        early = state
        state = form_stage(stage, table, prepared, row_vec, places, state, blocks)
    pair, slot_vec, col_acc = state
    row_acc = apply_tiles(
        LATE, None, "apply_late", table, pair, slot_vec, tiles, (early[1],)
    )
    first = combine(row_acc, col_acc)

    col_vec = spread(first, ROW)
    col_acc = apply_tiles(CROSSING, COL_AT, "apply_cols", table, pair, spread_near(first), blocks)
    row_acc = apply_tiles(LIVE, COL_AT, "apply_rows", table, pair, col_vec, tiles)
    second = combine(row_acc, col_acc)

    rows = spread(second, COL)
    squares = jnp.sum(rows * rows, axis=(0, 2))
    squares = spread(jnp.pad(squares[None, :], ((0, 0), (0, 120))), ROW)
    total = jnp.sum(squares[:, 0, :8], axis=0) / (block * blocks)
    scaled = rows / jnp.sqrt(total + 1e-06)[None, :, None]
    return scaled.transpose(1, 0, 2).reshape(8, block)


def solution(mesh):
    physical = Mesh(mesh.devices.reshape(8, 4, 4, 2), ("z", "y", "x", "core"))
    placed = (
        P(None, None, ROW),
        P(None, ROW),
        P(ROW, COL, None, None),
        P(ROW, COL, None),
    )
    return jax.shard_map(
        per_device, mesh=physical, in_specs=placed, out_specs=P(None, ROW), check_vma=False
    )
```
